32 devices in a mesh: pb: 8 (over y, x, core), pa: 4 (over z).
Axes of the slice: x: 2, y: 2, z: 4, core: 2. Of those that a mesh axis runs over, the one named last changes fastest.
Arguments:
- query_tokens: bfloat16 [128, 32, 768], P(('pb', 'pa')), may hold values from -6 to 6
- passage_tokens: bfloat16 [32, 1024, 768], P(('pb', 'pa')), may hold values from -6 to 6
- passage_lengths: int32 [32, 8], replicated, may hold values from 1 to 512, 1024 in all within a row
- positives: int32 [128], replicated, may hold values from 0 to 255
- qkv_weight: float32 [768, 2304], P(('pb', 'pa')), may hold values from -0.21875 to 0.21875
- qkv_first: float32 [768, 2304], P(('pb', 'pa')), may hold values from -4.7683716e-06 to 4.7683716e-06
- qkv_second: float32 [768, 2304], P(('pb', 'pa')), may hold values from 5.5668377e-14 to 2.2267351e-13
- out_weight: float32 [768, 768], P(('pb', 'pa')), may hold values from -0.875 to 0.875
- out_first: float32 [768, 768], P(('pb', 'pa')), may hold values from -4.7683716e-06 to 4.7683716e-06
- out_second: float32 [768, 768], P(('pb', 'pa')), may hold values from 5.5668377e-14 to 2.2267351e-13
- up_weight: float32 [768, 3072], P(('pb', 'pa')), may hold values from -0.21875 to 0.21875
- up_first: float32 [768, 3072], P(('pb', 'pa')), may hold values from -4.7683716e-06 to 4.7683716e-06
- up_second: float32 [768, 3072], P(('pb', 'pa')), may hold values from 5.5668377e-14 to 2.2267351e-13
- down_weight: float32 [3072, 768], P(('pb', 'pa')), may hold values from -0.109375 to 0.109375
- down_first: float32 [3072, 768], P(('pb', 'pa')), may hold values from -4.7683716e-06 to 4.7683716e-06
- down_second: float32 [3072, 768], P(('pb', 'pa')), may hold values from 5.5668377e-14 to 2.2267351e-13
- proj_weight: float32 [768, 128], P(('pb', 'pa')), may hold values from -0.21875 to 0.21875
- proj_first: float32 [768, 128], P(('pb', 'pa')), may hold values from -4.7683716e-06 to 4.7683716e-06
- proj_second: float32 [768, 128], P(('pb', 'pa')), may hold values from 5.5668377e-14 to 2.2267351e-13
- vector_params: float32 [12, 768], P(None, ('pb', 'pa')), may hold values from -1.2 to 1.4, as said below
- vector_first: float32 [12, 768], P(None, ('pb', 'pa')), may hold values from -1.9073486e-05 to 1.9073486e-05
- vector_second: float32 [12, 768], P(None, ('pb', 'pa')), may hold values from 8.9069404e-13 to 3.5627762e-12
Outputs:
- grad_norm: float32 [], replicated
- qkv_next: float32 [768, 2304], P(('pb', 'pa'))
- qkv_first_next: float32 [768, 2304], P(('pb', 'pa'))
- qkv_second_next: float32 [768, 2304], P(('pb', 'pa'))
- out_next: float32 [768, 768], P(('pb', 'pa'))
- out_first_next: float32 [768, 768], P(('pb', 'pa'))
- out_second_next: float32 [768, 768], P(('pb', 'pa'))
- up_next: float32 [768, 3072], P(('pb', 'pa'))
- up_first_next: float32 [768, 3072], P(('pb', 'pa'))
- up_second_next: float32 [768, 3072], P(('pb', 'pa'))
- down_next: float32 [3072, 768], P(('pb', 'pa'))
- down_first_next: float32 [3072, 768], P(('pb', 'pa'))
- down_second_next: float32 [3072, 768], P(('pb', 'pa'))
- proj_next: float32 [768, 128], P(('pb', 'pa'))
- proj_first_next: float32 [768, 128], P(('pb', 'pa'))
- proj_second_next: float32 [768, 128], P(('pb', 'pa'))
- vector_next: float32 [12, 768], P(None, ('pb', 'pa'))
- vector_first_next: float32 [12, 768], P(None, ('pb', 'pa'))
- vector_second_next: float32 [12, 768], P(None, ('pb', 'pa'))
The draws below stay inside these ranges and needn't reach their ends.
Inputs may be any that keep to these rules, and one draw needn't show every extreme that they name: `passage_lengths`: each row sums to 1024; one passage of each row is the longest. `positives`: any passage id. `vector_params`: rows 3 and 10 are gains between 0.6 and 1.4, the other rows biases of both signs.
All inputs are finite; a program needn't handle non-finite values.
Results may differ from the reference program's by a relative error of at most 0.0093.
Values may be sent and summed in bfloat16 or wider, within the bound.
No kernel may reach another device: no remote copies, remote signals or barrier semaphores. Data moves between devices by JAX's collectives and lax.ppermute only.
A program may use at most 320 MiB of HBM per device.

```python
import math
import jax
import jax.numpy as jnp
import numpy as np
from jax import lax

D = 768
HEADS = 12
HEAD_DIM = 64
FF = 3072
EMB = 128
QLEN = 32
BIN = 1024
PPB = 8
STEP = 10
BINS = 32
NQ = 128
NP = 256
PARAMS = 7185408


def draw_vector_params(key, part):
    biases = jnp.clip(0.3 * jax.random.normal(jax.random.fold_in(key, 11), (12, D), jnp.float32), -1.2, 1.2)
    gains = jax.random.uniform(jax.random.fold_in(key, 12), (12, D), jnp.float32, 0.6, 1.4)
    row_number = jnp.arange(12)[:, None]
    return jnp.where((row_number == 3) | (row_number == 10), gains, biases)


def plant(result, own_key, low, top_value):
    longest = result.shape.index(max(result.shape))
    spots = []
    for shift in (0, 1):
        where = [jax.random.randint(jax.random.fold_in(own_key, axis), (), 0, length) for axis, length in enumerate(result.shape)]
        where[longest] = (where[longest] + shift) % result.shape[longest]
        spots.append(tuple(where))
    return result.at[spots[0]].set(low).at[spots[1]].set(top_value)


def levels(stream_key, shape, split, least, high):
    level = 1.0
    for position, blocks in split:
        draws = jax.random.uniform(jax.random.fold_in(jax.random.fold_in(stream_key, 6), position), (blocks,), jnp.float32, least / len(split), high / len(split))
        level = level * jnp.repeat(jnp.exp(draws), shape[position] // blocks).reshape((-1,) + (1,) * (len(shape) - 1 - position))
    return level


def split_up(amount, total, bound, lean):
    weights = [(1 << 20) // math.isqrt(grade ** lean) + 1 for grade in range(2, amount + 1)]
    surplus, holding = total - bound - (amount - 1), [1] * (amount - 1)
    while surplus > 0:
        movable = [i for i in range(amount - 1) if holding[i] < bound]
        pool, remaining = sum([weights[i] for i in movable]), surplus
        for i in movable:
            more = min(bound - holding[i], max(1, remaining * weights[i] // pool), surplus)
            holding[i] = holding[i] + more
            surplus = surplus - more
    return np.array([bound] + holding)


def uneven(stream_key, amount, total, limit, slope):
    if amount == 2:
        one = jax.random.randint(stream_key, (), max(1, total - limit), min(limit, total - 1) + 1)
        return jnp.stack([one, total - one])
    tallies = jnp.asarray(split_up(amount, total, limit, slope), jnp.int32)
    couples = (amount - 1) // 2
    giver, taker = tallies[1:1 + 2 * couples:2], tallies[2:2 + 2 * couples:2]
    room = jnp.minimum(giver - 1, limit - taker)
    passed = jax.random.randint(jax.random.fold_in(stream_key, 1), (couples,), 0, 1 << 20) % (room + 1)
    tallies = tallies.at[1:1 + 2 * couples:2].set(giver - passed).at[2:2 + 2 * couples:2].set(taker + passed)
    return tallies[jax.random.permutation(jax.random.fold_in(stream_key, 2), amount)]


def normal_values(key, dims, scale, limit, pieces=(), held_as=jnp.bfloat16):
    drawn = scale * jax.random.normal(key, dims, jnp.float32)
    if pieces:
        drawn = drawn * levels(key, dims, pieces, -0.22, 0.18)
    return jnp.clip(drawn, -limit, limit).astype(held_as)


def setup_inputs(seed: int = 0) -> dict:
    splits = jax.random.split(jax.random.key(seed), 23)
    query_tokens = normal_values(splits[0], (NQ, QLEN, D), 1.0, 6.0, ((0, 32),))
    passage_tokens = normal_values(splits[1], (BINS, BIN, D), 1.0, 6.0, ((0, 32),))
    passage_lengths = jax.vmap(lambda own: uneven(own, PPB, BIN, BIN // 2, 2))(jax.random.split(splits[2], BINS)).reshape((BINS, PPB)).astype(jnp.int32)
    positives = plant(jax.random.randint(splits[3], (NQ,), 0, NP), jax.random.fold_in(splits[3], 1), 0, NP - 1).astype(jnp.int32)
    qkv_weight = normal_values(splits[4], (D, 3 * D), D ** -0.5, 0.21875, ((0, 32),), jnp.float32)
    qkv_first = normal_values(splits[5], (D, 3 * D), (0.00222 * PARAMS ** -0.5), 4.76837158203125e-06, ((0, 32),), jnp.float32)
    qkv_second = jnp.clip(jnp.exp(math.log(2.2267350994770868e-13) - 1.3862944 * jax.random.uniform(splits[6], (D, 3 * D), jnp.float32) ** levels(splits[6], (D, 3 * D), ((0, 32),), -0.2, 0.2)), 5.566837748692717e-14, 2.2267350994770868e-13)
    out_weight = normal_values(splits[7], (D, D), (D // 16) ** -0.5, 0.875, ((0, 32),), jnp.float32)
    out_first = normal_values(splits[8], (D, D), (0.00222 * PARAMS ** -0.5), 4.76837158203125e-06, ((0, 32),), jnp.float32)
    out_second = jnp.clip(jnp.exp(math.log(2.2267350994770868e-13) - 1.3862944 * jax.random.uniform(splits[9], (D, D), jnp.float32) ** levels(splits[9], (D, D), ((0, 32),), -0.2, 0.2)), 5.566837748692717e-14, 2.2267350994770868e-13)
    up_weight = normal_values(splits[10], (D, FF), D ** -0.5, 0.21875, ((0, 32),), jnp.float32)
    up_first = normal_values(splits[11], (D, FF), (0.00222 * PARAMS ** -0.5), 4.76837158203125e-06, ((0, 32),), jnp.float32)
    up_second = jnp.clip(jnp.exp(math.log(2.2267350994770868e-13) - 1.3862944 * jax.random.uniform(splits[12], (D, FF), jnp.float32) ** levels(splits[12], (D, FF), ((0, 32),), -0.2, 0.2)), 5.566837748692717e-14, 2.2267350994770868e-13)
    down_weight = normal_values(splits[13], (FF, D), FF ** -0.5, 0.109375, ((0, 32),), jnp.float32)
    down_first = normal_values(splits[14], (FF, D), (0.00222 * PARAMS ** -0.5), 4.76837158203125e-06, ((0, 32),), jnp.float32)
    down_second = jnp.clip(jnp.exp(math.log(2.2267350994770868e-13) - 1.3862944 * jax.random.uniform(splits[15], (FF, D), jnp.float32) ** levels(splits[15], (FF, D), ((0, 32),), -0.2, 0.2)), 5.566837748692717e-14, 2.2267350994770868e-13)
    proj_weight = normal_values(splits[16], (D, EMB), D ** -0.5, 0.21875, ((0, 32),), jnp.float32)
    proj_first = normal_values(splits[17], (D, EMB), (0.00222 * PARAMS ** -0.5), 4.76837158203125e-06, ((0, 32),), jnp.float32)
    proj_second = jnp.clip(jnp.exp(math.log(2.2267350994770868e-13) - 1.3862944 * jax.random.uniform(splits[18], (D, EMB), jnp.float32) ** levels(splits[18], (D, EMB), ((0, 32),), -0.2, 0.2)), 5.566837748692717e-14, 2.2267350994770868e-13)
    vector_params = draw_vector_params(jax.random.fold_in(splits[22], 71), 0)
    vector_first = normal_values(splits[20], (12, D), (0.0089 * PARAMS ** -0.5), 1.9073486328125e-05, ((1, 32),), jnp.float32)
    vector_second = jnp.clip(jnp.exp(math.log(3.562776159163339e-12) - 1.3862944 * jax.random.uniform(splits[21], (12, D), jnp.float32) ** levels(splits[21], (12, D), ((1, 32),), -0.2, 0.2)), 8.906940397908347e-13, 3.562776159163339e-12)
    return dict(query_tokens=query_tokens, passage_tokens=passage_tokens, passage_lengths=passage_lengths, positives=positives, qkv_weight=qkv_weight, qkv_first=qkv_first, qkv_second=qkv_second, out_weight=out_weight, out_first=out_first, out_second=out_second, up_weight=up_weight, up_first=up_first, up_second=up_second, down_weight=down_weight, down_first=down_first, down_second=down_second, proj_weight=proj_weight, proj_first=proj_first, proj_second=proj_second, vector_params=vector_params, vector_first=vector_first, vector_second=vector_second)


@jax.custom_vjp
def low(v):
    return lax.optimization_barrier(v.astype(jnp.bfloat16)).astype(jnp.float32)

@jax.custom_vjp
def reduced_precision_backward(v):
    return v

def low_keep(v):
    return (low(v), None)

def low_pass(kept, grad):
    return (grad,)

def back_keep(v):
    return (v, None)

def back_low(kept, grad):
    return (low(grad),)
low.defvjp(low_keep, low_pass)
reduced_precision_backward.defvjp(back_keep, back_low)
full_accuracy_flag = lax.Precision.HIGHEST
sharpness_divisor = 0.1
clip_max = 0.02
learn_rate = 0.04
vector_rate = 0.4
beta_one = 0.9
beta_two = 0.999
adam_eps = 1e-08
decay_rate = 0.01
norm_eps = 1e-12

def layer_norm(hidden, gain, shift):
    centred = hidden - lax.optimization_barrier(jnp.mean(hidden, -1, keepdims=True))
    spread = lax.optimization_barrier(jnp.mean(centred * centred, -1, keepdims=True))
    return centred * lax.rsqrt(spread + norm_eps) * gain + shift

def normalize(projected):
    return projected * lax.rsqrt(lax.optimization_barrier(jnp.sum(projected * projected, -1, keepdims=True)) + 1e-06)

def segments_of(lengths_row):
    ends = jnp.cumsum(lengths_row)
    places = jnp.arange(BIN, dtype=jnp.int32)
    return lax.optimization_barrier(jnp.sum((places[:, None] >= ends[None, :]).astype(jnp.int32), 1)).astype(jnp.int32)

def encode(tokens, segment, params):
    qkv_matrix, out_matrix, up_matrix, down_matrix, proj_matrix, vectors = params
    batch, length, width = tokens.shape
    flat = tokens.reshape(batch * length, width)
    bias_qkv = jnp.concatenate([vectors[0], jnp.zeros_like(vectors[0]), vectors[1]])
    mixed = low(reduced_precision_backward(jnp.dot(flat, qkv_matrix, precision=full_accuracy_flag)) + bias_qkv)
    mixed = mixed.reshape(batch, length, 3, HEADS, HEAD_DIM)
    raw_scores = jnp.einsum('bqhd,bkhd->bhqk', mixed[:, :, 0], mixed[:, :, 1], precision=full_accuracy_flag)
    same_seq = (segment[:, :, None] == segment[:, None, :])[:, None]
    logits = jnp.where(same_seq, reduced_precision_backward(raw_scores) * HEAD_DIM ** (-0.5), -1e+30)
    attention = jax.nn.softmax(logits, axis=-1)
    attended = jnp.einsum('bhqk,bkhd->bqhd', low(attention), mixed[:, :, 2], precision=full_accuracy_flag)
    attended = low(reduced_precision_backward(attended.reshape(batch * length, width)))
    branch = reduced_precision_backward(jnp.dot(attended, out_matrix, precision=full_accuracy_flag)) + vectors[2]
    normed_one = layer_norm(flat + branch, vectors[3], vectors[4])
    hidden = reduced_precision_backward(jnp.dot(low(normed_one), up_matrix, precision=full_accuracy_flag)) + vectors[5:9].reshape(-1)
    activated = low(jax.nn.gelu(hidden, approximate=False))
    second_branch = reduced_precision_backward(jnp.dot(activated, down_matrix, precision=full_accuracy_flag)) + vectors[9]
    normed_two = layer_norm(normed_one + second_branch, vectors[10], vectors[11])
    projected = reduced_precision_backward(jnp.dot(low(normed_two), proj_matrix, precision=full_accuracy_flag))
    return low(normalize(projected)).reshape(batch, length, -1)

def score_bin(query_collection, passage_normalized, lengths_row):
    belonging_mask = (segments_of(lengths_row)[:, None] == jnp.arange(PPB, dtype=jnp.int32)[None, :]).astype(jnp.float32)
    angle_agreement = reduced_precision_backward(jnp.einsum('fsh,vh->fsv', query_collection, passage_normalized, precision=full_accuracy_flag))
    accumulated_sums = jnp.einsum('esd,du->esu', jnp.exp((angle_agreement - 1.0) / sharpness_divisor), belonging_mask, precision=full_accuracy_flag)
    return lax.optimization_barrier(jnp.sum(sharpness_divisor * jnp.log(accumulated_sums) + 1.0, 1))

def total_loss(params, query_tokens, passage_tokens, passage_lengths, positives):
    lowered = tuple((low(value) for value in params))
    group = math.gcd(NQ, max(1, 4096 // QLEN))
    zero_seg = jnp.zeros((group, QLEN), jnp.int32)

    def encode_group(block):
        return encode(block, zero_seg, lowered)
    query_unit = lax.map(jax.checkpoint(encode_group), query_tokens.reshape(NQ // group, group, QLEN, D))

    def encode_bin(inputs):
        return encode(inputs[0][None], segments_of(inputs[1])[None], lowered)[0]
    passage_normalized = lax.map(jax.checkpoint(encode_bin), (passage_tokens, passage_lengths))

    def score_group(query_collection):

        def one_bin(inputs):
            return score_bin(query_collection, inputs[0], inputs[1])
        per_bin = lax.map(jax.checkpoint(one_bin), (passage_normalized, passage_lengths))
        return jnp.transpose(per_bin, (1, 0, 2)).reshape(query_collection.shape[0], NP)
    scores = lax.map(jax.checkpoint(score_group), query_unit).reshape(NQ, NP)
    highest = lax.optimization_barrier(jnp.max(scores, -1, keepdims=True))
    log_total = highest[:, 0] + jnp.log(lax.optimization_barrier(jnp.sum(jnp.exp(scores - highest), -1)))
    chosen = jnp.arange(NP, dtype=jnp.int32)[None, :] == positives[:, None]
    picked = lax.optimization_barrier(jnp.sum(jnp.where(chosen, scores, 0.0), -1))
    return jnp.mean(log_total - picked)

def adam_update(weight, moment_one, moment_two, gradient, factor, rate):
    clipped = gradient * factor
    new_one = beta_one * moment_one + (1.0 - beta_one) * clipped
    new_two = beta_two * moment_two + (1.0 - beta_two) * clipped * clipped
    direction = new_one / (1.0 - beta_one ** STEP) / (jnp.sqrt(new_two / (1.0 - beta_two ** STEP)) + adam_eps)
    return (weight - rate * (direction + decay_rate * weight), new_one, new_two)

def reference(query_tokens, passage_tokens, passage_lengths, positives, qkv_weight, qkv_first, qkv_second, out_weight, out_first, out_second, up_weight, up_first, up_second, down_weight, down_first, down_second, proj_weight, proj_first, proj_second, vector_params, vector_first, vector_second):
    params = (qkv_weight, out_weight, up_weight, down_weight, proj_weight, vector_params)
    firsts = (qkv_first, out_first, up_first, down_first, proj_first, vector_first)
    seconds = (qkv_second, out_second, up_second, down_second, proj_second, vector_second)
    query_float = query_tokens.astype(jnp.float32)
    passage_float = passage_tokens.astype(jnp.float32)

    def loss_of(values):
        return total_loss(values, query_float, passage_float, passage_lengths, positives)
    loss, pull = jax.vjp(loss_of, params)
    gradients = pull(jnp.ones_like(loss))[0]
    norm_value = jnp.sqrt(sum((jnp.sum(gradient * gradient) for gradient in gradients)))
    factor = jnp.minimum(1.0, clip_max / (norm_value + 1e-06))
    qkv_res = adam_update(params[0], firsts[0], seconds[0], gradients[0], factor, learn_rate)
    out_res = adam_update(params[1], firsts[1], seconds[1], gradients[1], factor, learn_rate)
    up_res = adam_update(params[2], firsts[2], seconds[2], gradients[2], factor, learn_rate)
    down_res = adam_update(params[3], firsts[3], seconds[3], gradients[3], factor, learn_rate)
    proj_res = adam_update(params[4], firsts[4], seconds[4], gradients[4], factor, learn_rate)
    vector_res = adam_update(params[5], firsts[5], seconds[5], gradients[5], factor, vector_rate)
    return (norm_value, qkv_res[0], qkv_res[1], qkv_res[2], out_res[0], out_res[1], out_res[2], up_res[0], up_res[1], up_res[2], down_res[0], down_res[1], down_res[2], proj_res[0], proj_res[1], proj_res[2], vector_res[0], vector_res[1], vector_res[2])
```

```python
import functools

import jax
import jax.numpy as jnp
from jax import lax
from jax.experimental import pallas as pl
from jax.experimental.pallas import tpu as pltpu
from jax.sharding import PartitionSpec as P

D = 768
HEAD_DIM = 64
QLEN = 32
BIN = 1024
PPB = 8
STEP = 10
QPD = 4
ATTEND_TILE = 512
FEED_ROWS = 512
BACK_ROWS = 256


sharpness_divisor = 0.1
clip_max = 0.02
learn_rate = 0.04
vector_rate = 0.4
beta_one = 0.9
beta_two = 0.999
adam_eps = 1e-08
decay_rate = 0.01
norm_eps = 1e-12


def shift_pairs(amount):
    return [(i, (i + amount) % 4) for i in range(4)]


FIRST_STEP = [(i, i ^ 2 if i % 2 == 0 else i ^ 4) for i in range(8)]
SECOND_STEP = [(i, i ^ 4 if i % 2 == 0 else i ^ 2) for i in range(8)]
CORE_PAIR = [(i, i ^ 1) for i in range(8)]


def staged_mesh():
    return lax.axis_size("pb") == 8 and lax.axis_size("pa") == 4


def position():
    row = lax.axis_index("pb")
    core, x_bit, y_bit = row % 2, (row // 2) % 2, row // 4
    return (
        lax.axis_index("pa"),
        core,
        jnp.where(core == 0, x_bit, y_bit),
        jnp.where(core == 0, y_bit, x_bit),
    )


def in_order(bit, own, other):
    first = bit == 0
    return jnp.stack([jnp.where(first, own, other), jnp.where(first, other, own)])


def gather_rows(part, columns):
    if not staged_mesh():
        whole = lax.all_gather(part, ("pb", "pa"), axis=0, tiled=True)
        return [whole[:, low:high] for low, high in columns]
    depth, core, first_bit, second_bit = position()
    moved = [lax.ppermute(part, "pa", shift_pairs(k)) for k in (1, 2, 3)]
    around = [part, moved[2], moved[1], moved[0]]
    line = jnp.stack([lax.select_n((place - depth) % 4, *around) for place in range(4)])
    pair = in_order(first_bit, line, lax.ppermute(line, "pb", FIRST_STEP))
    quad = in_order(second_bit, pair, lax.ppermute(pair, "pb", SECOND_STEP))
    partner = lax.ppermute(quad, "pb", CORE_PAIR)
    results = []
    for low, high in columns:
        own, other = quad[..., low:high], partner[..., low:high]
        even = jnp.where(core == 0, own, other)
        odd = jnp.where(core == 0, other, own).swapaxes(0, 1)
        results.append(jnp.stack([even, odd], 2).reshape(32 * part.shape[0], high - low))
    return results


def scatter_rows(terms):
    if not staged_mesh():
        return lax.psum_scatter(
            terms.astype(jnp.float32), ("pb", "pa"), scatter_dimension=0, tiled=True
        )
    depth, core, first_bit, second_bit = position()
    blocks = terms.reshape((2, 2, 2, 4, terms.shape[0] // 32) + terms.shape[1:])
    even, odd = blocks[:, :, 0], blocks[:, :, 1].swapaxes(0, 1)
    keep = jnp.where(core == 0, even, odd)
    send = jnp.where(core == 0, odd, even).astype(jnp.bfloat16)

    def block(array, place):
        return lax.dynamic_index_in_dim(array, place, 0, False)

    def sent(array, place):
        return block(array, place).astype(jnp.bfloat16)

    def joined(own, moved):
        return own.astype(jnp.float32) + moved.astype(jnp.float32)

    quad = joined(keep, lax.ppermute(send, "pb", CORE_PAIR))
    pair = joined(
        block(quad, second_bit), lax.ppermute(sent(quad, 1 - second_bit), "pb", SECOND_STEP)
    )
    line = joined(
        block(pair, first_bit), lax.ppermute(sent(pair, 1 - first_bit), "pb", FIRST_STEP)
    )
    total = block(line, depth)
    for k in (1, 2, 3):
        moved = lax.ppermute(sent(line, (depth + k) % 4), "pa", shift_pairs(k))
        total = joined(total, moved)
    return total


def sum_everywhere(value):
    count = lax.axis_size(("pb", "pa"))
    copies = jnp.broadcast_to(value[None], (count,) + value.shape)
    return jnp.sum(lax.all_to_all(copies, ("pb", "pa"), 0, 0), 0)


F32 = jnp.float32
LOW = jnp.bfloat16
ACROSS = (((1,), (1,)), ((), ()))
PLAIN = (((1,), (0,)), ((), ()))


def dot(left, right, dims=PLAIN):
    return lax.dot_general(left, right, dims, preferred_element_type=F32)


def standard(hidden):
    centred = hidden - jnp.mean(hidden, -1, keepdims=True)
    spread = jnp.mean(centred * centred, -1, keepdims=True)
    scale = lax.rsqrt(spread + norm_eps)
    return centred * scale, scale


def standard_backward(grad, unit, scale):
    return scale * (
        grad
        - jnp.mean(grad, -1, keepdims=True)
        - unit * jnp.mean(grad * unit, -1, keepdims=True)
    )


def gelu_with_slope(value):
    below = 0.5 + 0.5 * lax.erf(value * 0.7071067811865476)
    density = 0.3989422804014327 * jnp.exp(-0.5 * value * value)
    return value * below, below + value * density


def whole_block(array):
    return pl.BlockSpec(array.shape, lambda *_: (0,) * array.ndim, pipeline_mode=pl.Buffered(1))


def row_block(rows, width):
    return pl.BlockSpec((rows, width), lambda i: (i, 0))


def row_call(kernel, count, rows, inputs, weights, outputs, sums=(), flops=0, limit=56):
    moved = count * sum(a.shape[1] * a.dtype.itemsize for a in inputs)
    moved += sum(w.size * w.dtype.itemsize for w in weights)
    moved += count * sum(w * jnp.dtype(t).itemsize for w, t in outputs)
    return pl.pallas_call(
        kernel,
        grid=(count // rows,),
        in_specs=[row_block(rows, a.shape[1]) for a in inputs] + [whole_block(w) for w in weights],
        out_specs=[row_block(rows, w) for w, _ in outputs]
        + [pl.BlockSpec((8, w), lambda i: (0, 0)) for w in sums],
        out_shape=[jax.ShapeDtypeStruct((count, w), t) for w, t in outputs]
        + [jax.ShapeDtypeStruct((8, w), F32) for w in sums],
        compiler_params=pltpu.CompilerParams(vmem_limit_bytes=limit << 20),
        cost_estimate=pl.CostEstimate(flops=flops, transcendentals=0, bytes_accessed=moved),
    )(*inputs, *weights)


def widen_kernel(x_ref, att_ref, out_w, up_w, vec, wide, resid_ref, low_ref, act_ref, slope_ref):
    resid = x_ref[...].astype(F32) + dot(att_ref[...], out_w[...]) + vec[2:3]
    resid_ref[...] = resid
    low = (standard(resid)[0] * vec[3:4] + vec[4:5]).astype(LOW)
    low_ref[...] = low
    for at in range(0, up_w.shape[1], 512):
        part = slice(at, at + 512)
        value, slope = gelu_with_slope(dot(low, up_w[:, part]) + wide[0:1, part])
        act_ref[:, part] = value.astype(LOW)
        slope_ref[:, part] = slope.astype(LOW)


def narrow_kernel(act_ref, resid_ref, down_w, proj_w, vec, two_ref, low_ref, proj_ref, unit_ref):
    normed = standard(resid_ref[...])[0] * vec[3:4] + vec[4:5]
    two = normed + dot(act_ref[...], down_w[...]) + vec[9:10]
    two_ref[...] = two
    low = (standard(two)[0] * vec[10:11] + vec[11:12]).astype(LOW)
    low_ref[...] = low
    projected = dot(low, proj_w[...])
    proj_ref[...] = projected
    square = jnp.sum(projected * projected, -1, keepdims=True) + 1e-06
    unit_ref[...] = (projected * lax.rsqrt(square)).astype(LOW)


def back_kernel(
    grad_ref, proj_ref, two_ref, slope_ref, resid_ref,
    proj_w, down_w, up_w, out_w, vec,
    gproj_ref, gtwo_ref, ghid_ref, gone_ref, gatt_ref, sum_ref, wide_ref,
):
    @pl.when(pl.program_id(0) == 0)
    def _():
        sum_ref[...] = jnp.zeros_like(sum_ref)
        wide_ref[...] = jnp.zeros_like(wide_ref)

    def add(row, value):
        sum_ref[row : row + 1, :] += jnp.sum(value, 0, keepdims=True)

    grad, projected = grad_ref[...], proj_ref[...]
    scale = lax.rsqrt(jnp.sum(projected * projected, -1, keepdims=True) + 1e-06)
    along = jnp.sum(projected * grad, -1, keepdims=True)
    gproj = (scale * grad - projected * (scale * scale * scale * along)).astype(LOW)
    gproj_ref[...] = gproj
    gnormed = dot(gproj, proj_w[...], ACROSS)
    unit, scale = standard(two_ref[...])
    add(4, gnormed * unit)
    add(5, gnormed)
    gtwo = standard_backward(gnormed * vec[10:11], unit, scale)
    add(3, gtwo)
    gtwo_low = gtwo.astype(LOW)
    gtwo_ref[...] = gtwo_low
    gnormed = gtwo
    for at in range(0, up_w.shape[1], 512):
        part = slice(at, at + 512)
        ghid = dot(gtwo_low, down_w[part, :], ACROSS) * slope_ref[:, part].astype(F32)
        wide_ref[0:1, part] += jnp.sum(ghid, 0, keepdims=True)
        ghid_low = ghid.astype(LOW)
        ghid_ref[:, part] = ghid_low
        gnormed = gnormed + dot(ghid_low, up_w[:, part], ACROSS)
    unit, scale = standard(resid_ref[...])
    add(1, gnormed * unit)
    add(2, gnormed)
    gone = standard_backward(gnormed * vec[3:4], unit, scale)
    add(0, gone)
    gone_low = gone.astype(LOW)
    gone_ref[...] = gone_low
    gatt_ref[...] = dot(gone_low, out_w[...], ACROSS).astype(LOW)


def attend_kernel(tile, spans, q_ref, k_ref, v_ref, col, row, out_ref, total_ref, logits, flipped):
    flipped[...] = v_ref[...].T
    lane = lax.broadcasted_iota(jnp.int32, (tile, 128), 1)

    def block(index, carry):
        here = pl.ds(pl.multiple_of(index * tile, tile), tile)
        query = q_ref[here, :] * jnp.asarray(0.125, LOW)
        zero = jnp.zeros_like(query)
        pair = (jnp.where(lane < 64, query, zero), jnp.where(lane < 64, zero, query))
        segment = row[0:1, here]
        low, high = spans[index, 0], spans[index, 1]

        def score(step, tops):
            there = pl.ds(pl.multiple_of(step * tile, tile), tile)
            keys = k_ref[there, :]
            same = col[there, :] == segment
            result = []
            for head in range(2):
                value = jnp.where(same, dot(keys, pair[head], ACROSS), -1e30)
                logits[head, there, :] = value
                result.append(jnp.maximum(tops[head], jnp.max(value, 0, keepdims=True)))
            return tuple(result)

        lowest = jnp.full((1, tile), -1e30, F32)
        tops = lax.fori_loop(low, high, score, (lowest, lowest))

        def mix(step, state):
            there = pl.ds(pl.multiple_of(step * tile, tile), tile)
            result = []
            for head in range(2):
                term = jnp.exp(logits[head, there, :] - tops[head])
                result.append(state[2 * head] + jnp.sum(term, 0, keepdims=True))
                values = flipped[64 * head : 64 * head + 64, there]
                result.append(state[2 * head + 1] + dot(values, term.astype(LOW)))
            return tuple(result)

        none, empty = jnp.zeros((1, tile), F32), jnp.zeros((64, tile), F32)
        sum0, mix0, sum1, mix1 = lax.fori_loop(low, high, mix, (none, empty, none, empty))
        both = jnp.concatenate([mix0 / sum0, mix1 / sum1], 0)
        out_ref[here, :] = both.T.astype(LOW)
        total_ref[0, 0:1, here] = tops[0] + jnp.log(sum0)
        total_ref[0, 1:2, here] = tops[1] + jnp.log(sum1)
        return carry

    lax.fori_loop(0, q_ref.shape[0] // tile, block, 0)


def head_pair(count, third):
    return pl.BlockSpec((count, 128), lambda h, s: (0, third * 6 + h))


def attend_forward(mixed, spans, col, row, tile):
    count = mixed.shape[0]
    return pl.pallas_call(
        functools.partial(attend_kernel, tile),
        out_shape=(
            jax.ShapeDtypeStruct((count, D), LOW),
            jax.ShapeDtypeStruct((6, 8, count), F32),
        ),
        grid_spec=pltpu.PrefetchScalarGridSpec(
            num_scalar_prefetch=1,
            grid=(6,),
            in_specs=[head_pair(count, third) for third in range(3)]
            + [
                pl.BlockSpec((count, tile), lambda h, s: (0, 0)),
                pl.BlockSpec((8, count), lambda h, s: (0, 0)),
            ],
            out_specs=[head_pair(count, 0), pl.BlockSpec((1, 8, count), lambda h, s: (h, 0, 0))],
            scratch_shapes=[pltpu.VMEM((2, count, tile), F32), pltpu.VMEM((128, count), LOW)],
        ),
        compiler_params=pltpu.CompilerParams(vmem_limit_bytes=40 << 20),
        cost_estimate=pl.CostEstimate(
            flops=8 * count * count * D,
            transcendentals=12 * count * count,
            bytes_accessed=8 * count * D,
        ),
    )(spans, mixed, mixed, mixed, col, row)


def attend_back_kernel(
    tile, spans, q_ref, k_ref, v_ref, g_ref, total_ref, col, row,
    grad_ref, sum_ref, flipped, gkey, gvalue, probs, gprobs,
):
    flipped[...] = k_ref[...].T
    gkey[...] = jnp.zeros_like(gkey)
    gvalue[...] = jnp.zeros_like(gvalue)
    lane = lax.broadcasted_iota(jnp.int32, (tile, 128), 1)

    def block(index, query_sum):
        here = pl.ds(pl.multiple_of(index * tile, tile), tile)
        query = q_ref[here, :] * jnp.asarray(0.125, LOW)
        zero = jnp.zeros_like(query)
        queries = (jnp.where(lane < 64, query, zero), jnp.where(lane < 64, zero, query))
        grad = g_ref[here, :]
        grads = (jnp.where(lane < 64, grad, zero), jnp.where(lane < 64, zero, grad))
        totals = (total_ref[0, 0:1, here], total_ref[0, 1:2, here])
        segment = row[0:1, here]
        low, high = spans[index, 0], spans[index, 1]

        def first(step, dots):
            there = pl.ds(pl.multiple_of(step * tile, tile), tile)
            keys, values = k_ref[there, :], v_ref[there, :]
            same = col[there, :] == segment
            result = []
            part = None
            for head in range(2):
                logit = dot(keys, queries[head], ACROSS)
                prob = jnp.where(same, jnp.exp(logit - totals[head]), 0.0)
                gprob = dot(values, grads[head], ACROSS)
                probs[head, there, :] = prob
                gprobs[head, there, :] = gprob
                result.append(dots[head] + jnp.sum(prob * gprob, 0, keepdims=True))
                more = dot(prob.astype(LOW), grads[head])
                part = more if part is None else part + more
            gvalue[there, :] += part
            return tuple(result)

        none = jnp.zeros((1, tile), F32)
        dots = lax.fori_loop(low, high, first, (none, none))

        def second(step, state):
            there = pl.ds(pl.multiple_of(step * tile, tile), tile)
            result = []
            part = None
            for head in range(2):
                delta = probs[head, there, :] * (gprobs[head, there, :] - dots[head])
                delta = delta.astype(LOW)
                more = dot(delta, queries[head])
                part = more if part is None else part + more
                keys = flipped[64 * head : 64 * head + 64, there]
                result.append(state[head] + dot(keys, delta))
            gkey[there, :] += part
            return tuple(result)

        empty = jnp.zeros((64, tile), F32)
        both = lax.fori_loop(low, high, second, (empty, empty))
        whole = jnp.concatenate(both, 0).T * 0.125
        grad_ref[0, here, :] = whole.astype(LOW)
        return query_sum + jnp.sum(whole, 0, keepdims=True)

    count = q_ref.shape[0]
    query_sum = lax.fori_loop(0, count // tile, block, jnp.zeros((1, 128), F32))
    grad_ref[1] = gkey[...].astype(LOW)
    grad_ref[2] = gvalue[...].astype(LOW)
    sum_ref[...] = jnp.zeros_like(sum_ref)
    sum_ref[0:1, :] = query_sum
    sum_ref[1:2, :] = jnp.sum(gvalue[...], 0, keepdims=True)


def attend_backward(mixed, grad, total, spans, col, row, tile):
    count = mixed.shape[0]
    return pl.pallas_call(
        functools.partial(attend_back_kernel, tile),
        out_shape=(
            jax.ShapeDtypeStruct((3, count, D), LOW),
            jax.ShapeDtypeStruct((8, D), F32),
        ),
        grid_spec=pltpu.PrefetchScalarGridSpec(
            num_scalar_prefetch=1,
            grid=(6,),
            in_specs=[head_pair(count, third) for third in range(3)]
            + [
                head_pair(count, 0),
                pl.BlockSpec((1, 8, count), lambda h, s: (h, 0, 0)),
                pl.BlockSpec((count, tile), lambda h, s: (0, 0)),
                pl.BlockSpec((8, count), lambda h, s: (0, 0)),
            ],
            out_specs=[
                pl.BlockSpec((3, count, 128), lambda h, s: (0, 0, h)),
                pl.BlockSpec((8, 128), lambda h, s: (0, h)),
            ],
            scratch_shapes=[
                pltpu.VMEM((128, count), LOW),
                pltpu.VMEM((count, 128), F32),
                pltpu.VMEM((count, 128), F32),
                pltpu.VMEM((2, count, tile), F32),
                pltpu.VMEM((2, count, tile), F32),
            ],
        ),
        compiler_params=pltpu.CompilerParams(vmem_limit_bytes=48 << 20),
        cost_estimate=pl.CostEstimate(
            flops=20 * count * count * D,
            transcendentals=12 * count * count,
            bytes_accessed=16 * count * D,
        ),
    )(spans, mixed, mixed, mixed, grad, total, col, row)


def segment_tables(segment, tile):
    count = segment.shape[0]
    ends = segment.reshape(count // tile, tile)
    first = jnp.sum((segment[None, :] < ends[:, :1]).astype(jnp.int32), 1)
    last = jnp.sum((segment[None, :] <= ends[:, -1:]).astype(jnp.int32), 1)
    return (
        jnp.stack([first // tile, (last + tile - 1) // tile], 1),
        jnp.broadcast_to(segment[:, None], (count, tile)),
        jnp.broadcast_to(segment[None, :], (8, count)),
    )


def split_low(value):
    high = value.astype(LOW)
    return high, (value - high.astype(F32)).astype(LOW)


def sharp(cosine):
    return jnp.exp(cosine * 10.0 - 10.0)


def score_kernel(query_ref, passage_ref, member_ref, score_ref, sums_ref):
    high, rest = split_low(sharp(dot(query_ref[...], passage_ref[...], ACROSS)))
    sums = dot(high, member_ref[...]) + dot(rest, member_ref[...])
    sums_ref[...] = sums
    lane = lax.broadcasted_iota(jnp.int32, sums.shape, 1)
    soft = jnp.where(lane < PPB, 0.1 * jnp.log(jnp.where(lane < PPB, sums, 1.0)) + 1.0, 0.0)
    score_ref[...] = jnp.sum(soft.reshape(-1, QLEN, 128), 1)


def score_ratio(grad_ref, sums_ref):
    rows = sums_ref.shape[0]
    lane = lax.broadcasted_iota(jnp.int32, (rows, 128), 1)
    grads = jnp.broadcast_to(grad_ref[...][:, None, :], (rows // QLEN, QLEN, 128))
    ratio = grads.reshape(rows, 128) / jnp.where(lane % 64 < PPB, sums_ref[...], 1.0)
    high, rest = split_low(ratio)
    return jnp.where(lane < 64, high, rest)


def score_query_kernel(query_ref, passage_ref, member_ref, grad_ref, sums_ref, out_ref):
    ratio = score_ratio(grad_ref, sums_ref)
    terms = sharp(dot(query_ref[...], passage_ref[...], ACROSS))
    terms = (terms * dot(ratio, member_ref[...], ACROSS)).astype(LOW)
    out_ref[...] = dot(terms, passage_ref[...])


def score_passage_kernel(query_ref, passage_ref, member_ref, grad_ref, sums_ref, out_ref):
    @pl.when(pl.program_id(0) == 0)
    def _():
        out_ref[...] = jnp.zeros_like(out_ref)

    ratio = score_ratio(grad_ref, sums_ref)
    terms = sharp(dot(passage_ref[...], query_ref[...], ACROSS))
    terms = (terms * dot(member_ref[...], ratio, ACROSS)).astype(LOW)
    out_ref[...] += dot(terms, query_ref[...])


SCORE_ROWS = 512


def score_call(kernel, inputs, in_specs, out_specs, out_shape, flops):
    return pl.pallas_call(
        kernel,
        grid=(inputs[0].shape[0] // SCORE_ROWS,),
        in_specs=in_specs,
        out_specs=out_specs,
        out_shape=out_shape,
        compiler_params=pltpu.CompilerParams(vmem_limit_bytes=40 << 20),
        cost_estimate=pl.CostEstimate(
            flops=flops,
            transcendentals=inputs[0].shape[0] * BIN,
            bytes_accessed=inputs[0].shape[0] * 1024,
        ),
    )(*inputs)


def score_specs():
    rows = SCORE_ROWS
    fixed = pl.BlockSpec((BIN, 128), lambda i: (0, 0))
    return (
        pl.BlockSpec((rows, 128), lambda i: (i, 0)),
        fixed,
        pl.BlockSpec((rows // QLEN, 128), lambda i: (i, 0)),
    )


def score_forward(queries, passages, member):
    rows, fixed, grads = score_specs()
    count = queries.shape[0]
    return score_call(
        score_kernel,
        (queries, passages, member),
        [rows, fixed, fixed],
        [grads, rows],
        [
            jax.ShapeDtypeStruct((count // QLEN, 128), F32),
            jax.ShapeDtypeStruct((count, 128), F32),
        ],
        6 * count * BIN * 128,
    )


def score_backward(queries, passages, member, grad_scores, sums):
    rows, fixed, grads = score_specs()
    count = queries.shape[0]
    inputs = (queries, passages, member, grad_scores, sums)
    in_specs = [rows, fixed, fixed, grads, rows]
    flops = 6 * count * BIN * 128
    out = jax.ShapeDtypeStruct((count, 128), F32)
    grad_queries = score_call(score_query_kernel, inputs, in_specs, rows, out, flops)
    out = jax.ShapeDtypeStruct((BIN, 128), F32)
    grad_passages = score_call(score_passage_kernel, inputs, in_specs, fixed, out, flops)
    return grad_queries, grad_passages


def encode_forward(tokens, tables, tile, rows, weights):
    qkv_matrix, out_matrix, up_matrix, down_matrix, proj_matrix, vectors, wide = weights
    count = tokens.shape[0]
    bias_qkv = jnp.concatenate([vectors[0], jnp.zeros_like(vectors[0]), vectors[1]])
    mixed = (dot(tokens, qkv_matrix) + bias_qkv).astype(LOW)
    attended, total = attend_forward(mixed, *tables, tile)
    resid, normed, active, slope = row_call(
        widen_kernel,
        count,
        rows,
        (tokens, attended),
        (out_matrix, up_matrix, vectors, wide),
        [(D, F32), (D, LOW), (4 * D, LOW), (4 * D, LOW)],
        flops=10 * count * D * D,
    )
    two, normed_out, projected, unit = row_call(
        narrow_kernel,
        count,
        rows,
        (active, resid),
        (down_matrix, proj_matrix, vectors),
        [(D, F32), (D, LOW), (128, F32), (128, LOW)],
        flops=8 * count * D * D,
    )
    kept = (tokens, mixed, total, attended, resid, normed, active, slope, two, normed_out, projected)
    return unit, kept


def encode_backward(tables, tile, rows, weights, kept, grad_unit):
    qkv_matrix, out_matrix, up_matrix, down_matrix, proj_matrix, vectors, wide = weights
    tokens, mixed, total, attended, resid, normed, active, slope, two, normed_out, projected = kept
    count = tokens.shape[0]
    gproj, gtwo, ghid, gone, gatt, sums, wide_sums = row_call(
        back_kernel,
        count,
        rows,
        (grad_unit, projected, two, slope, resid),
        (proj_matrix, down_matrix, up_matrix, out_matrix, vectors),
        [(128, LOW), (D, LOW), (4 * D, LOW), (D, LOW), (D, LOW)],
        (D, 4 * D),
        flops=18 * count * D * D,
    )
    gmixed, attend_sums = attend_backward(mixed, gatt, total, *tables, tile)
    vector_grad = jnp.concatenate(
        [attend_sums[:2], sums[:3], wide_sums[:1].reshape(4, D), sums[3:6]], 0
    )
    pairs = (
        (tokens, gmixed),
        (attended, gone),
        (normed, ghid),
        (active, gtwo),
        (normed_out, gproj),
    )
    return pairs, vector_grad


def cross_grad(scores, partition, passage_ids, chosen_ids, query_total):
    onehot = (passage_ids[None, :] == chosen_ids[:, None]).astype(jnp.float32)
    return (jnp.exp(scores) / partition[:, None] - onehot) / query_total


def adam_update(weight, moment_one, moment_two, gradient, factor, rate):
    clipped = gradient * factor
    new_one = beta_one * moment_one + (1.0 - beta_one) * clipped
    new_two = beta_two * moment_two + (1.0 - beta_two) * clipped * clipped
    direction = (
        new_one / (1.0 - beta_one**STEP) / (jnp.sqrt(new_two / (1.0 - beta_two**STEP)) + adam_eps)
    )
    return (weight - rate * (direction + decay_rate * weight), new_one, new_two)


def body(
    query_tokens,
    passage_tokens,
    passage_lengths,
    positives,
    qkv_weight,
    qkv_first,
    qkv_second,
    out_weight,
    out_first,
    out_second,
    up_weight,
    up_first,
    up_second,
    down_weight,
    down_first,
    down_second,
    proj_weight,
    proj_first,
    proj_second,
    vector_params,
    vector_first,
    vector_second,
):
    low = jnp.bfloat16
    vector_part = jnp.pad(vector_params.T, ((0, 0), (0, 116))).astype(low)
    qkv_matrix, vectors = gather_rows(
        jnp.concatenate([qkv_weight.astype(low), vector_part], 1), [(0, 2304), (2304, 2432)]
    )
    up_matrix, out_matrix, proj_matrix = gather_rows(
        jnp.concatenate([up_weight, out_weight, proj_weight], 1).astype(low),
        [(0, 3072), (3072, 3840), (3840, 3968)],
    )
    (down_matrix,) = gather_rows(down_weight.astype(low), [(0, 768)])
    weights = (
        qkv_matrix,
        out_matrix,
        up_matrix,
        down_matrix,
        proj_matrix,
        vectors[:, :12].T.astype(F32),
        vectors[:, 5:9].T.astype(F32).reshape(1, 4 * D),
    )
    own_index = lax.axis_index(("pb", "pa"))
    query_total = QPD * lax.axis_size(("pb", "pa"))
    query_flat = query_tokens.reshape(QPD * QLEN, D)
    query_tables = segment_tables(jnp.arange(QPD * QLEN, dtype=jnp.int32) // QLEN, QPD * QLEN)
    own_lengths = lax.dynamic_index_in_dim(passage_lengths, own_index, 0, keepdims=False)
    ends = jnp.cumsum(own_lengths)
    places = jnp.arange(BIN, dtype=jnp.int32)
    own_seg = jnp.sum((places[:, None] >= ends[None, :]).astype(jnp.int32), 1)
    passage_tables = segment_tables(own_seg, ATTEND_TILE)
    member = (own_seg[:, None] == jnp.arange(128, dtype=jnp.int32)[None, :] % 64).astype(low)
    query_unit, query_kept = encode_forward(
        query_flat, query_tables, QPD * QLEN, QPD * QLEN, weights
    )
    passage_unit, passage_kept = encode_forward(
        passage_tokens[0], passage_tables, ATTEND_TILE, FEED_ROWS, weights
    )
    (every_query,) = gather_rows(query_unit, [(0, 128)])
    passage_ids = own_index * PPB + jnp.arange(PPB, dtype=jnp.int32)
    scores, totals = score_forward(every_query, passage_unit, member)
    scores = scores[:, :PPB]
    partition = sum_everywhere(jnp.sum(jnp.exp(scores), 1))
    grad_scores = cross_grad(scores, partition, passage_ids, positives, query_total)
    grad_scores = jnp.tile(jnp.pad(grad_scores, ((0, 0), (0, 64 - PPB))), (1, 2))
    grad_every, grad_passage = score_backward(
        every_query, passage_unit, member, grad_scores, totals
    )
    grad_query = scatter_rows(grad_every)
    query_pairs, query_vector = encode_backward(
        query_tables, QPD * QLEN, QPD * QLEN, weights, query_kept, grad_query
    )
    passage_pairs, passage_vector = encode_backward(
        passage_tables, ATTEND_TILE, BACK_ROWS, weights, passage_kept, grad_passage
    )

    def weight_terms(index):
        (left, right), (left_more, right_more) = passage_pairs[index], query_pairs[index]
        left = jnp.concatenate([left, left_more], 0)
        right = jnp.concatenate([right, right_more], -2)
        if index == 0:
            return jnp.einsum("td,itk->dik", left, right, preferred_element_type=F32).reshape(
                D, 3 * D
            )
        return dot(left, right, (((0,), (0,)), ((), ())))

    down_sum = scatter_rows(weight_terms(3))
    proj_terms = weight_terms(4)
    proj_high = proj_terms.astype(low)
    proj_rest = (proj_terms - proj_high.astype(F32)).astype(low)
    middle = scatter_rows(
        jnp.concatenate(
            [weight_terms(2).astype(low), weight_terms(1).astype(low), proj_high, proj_rest], 1
        )
    )
    vector_terms = jnp.pad((query_vector + passage_vector).T, ((0, 0), (0, 116)))
    first = scatter_rows(
        jnp.concatenate([weight_terms(0).astype(low), vector_terms.astype(low)], 1)
    )
    reduced = (
        first[:, :2304],
        middle[:, 3072:3840],
        middle[:, :3072],
        down_sum,
        middle[:, 3840:3968] + middle[:, 3968:],
        first[:, 2304:2316].T,
    )
    square = sum((jnp.sum(gradient * gradient) for gradient in reduced))
    norm_value = jnp.sqrt(sum_everywhere(jnp.full((1, 128), square))[0, 0])
    factor = jnp.minimum(1.0, clip_max / (norm_value + 1e-06))
    qkv_res = adam_update(qkv_weight, qkv_first, qkv_second, reduced[0], factor, learn_rate)
    out_res = adam_update(out_weight, out_first, out_second, reduced[1], factor, learn_rate)
    up_res = adam_update(up_weight, up_first, up_second, reduced[2], factor, learn_rate)
    down_res = adam_update(down_weight, down_first, down_second, reduced[3], factor, learn_rate)
    proj_res = adam_update(proj_weight, proj_first, proj_second, reduced[4], factor, learn_rate)
    vector_res = adam_update(
        vector_params, vector_first, vector_second, reduced[5], factor, vector_rate
    )
    return (
        norm_value,
        qkv_res[0],
        qkv_res[1],
        qkv_res[2],
        out_res[0],
        out_res[1],
        out_res[2],
        up_res[0],
        up_res[1],
        up_res[2],
        down_res[0],
        down_res[1],
        down_res[2],
        proj_res[0],
        proj_res[1],
        proj_res[2],
        vector_res[0],
        vector_res[1],
        vector_res[2],
    )


def solution(mesh):
    placed = (
        P(("pb", "pa"), None, None),
        P(("pb", "pa"), None, None),
        P(),
        P(),
        P(("pb", "pa"), None),
        P(("pb", "pa"), None),
        P(("pb", "pa"), None),
        P(("pb", "pa"), None),
        P(("pb", "pa"), None),
        P(("pb", "pa"), None),
        P(("pb", "pa"), None),
        P(("pb", "pa"), None),
        P(("pb", "pa"), None),
        P(("pb", "pa"), None),
        P(("pb", "pa"), None),
        P(("pb", "pa"), None),
        P(("pb", "pa"), None),
        P(("pb", "pa"), None),
        P(("pb", "pa"), None),
        P(None, ("pb", "pa")),
        P(None, ("pb", "pa")),
        P(None, ("pb", "pa")),
    )
    return jax.shard_map(
        body,
        mesh=mesh,
        in_specs=placed,
        out_specs=(
            P(),
            P(("pb", "pa"), None),
            P(("pb", "pa"), None),
            P(("pb", "pa"), None),
            P(("pb", "pa"), None),
            P(("pb", "pa"), None),
            P(("pb", "pa"), None),
            P(("pb", "pa"), None),
            P(("pb", "pa"), None),
            P(("pb", "pa"), None),
            P(("pb", "pa"), None),
            P(("pb", "pa"), None),
            P(("pb", "pa"), None),
            P(("pb", "pa"), None),
            P(("pb", "pa"), None),
            P(("pb", "pa"), None),
            P(None, ("pb", "pa")),
            P(None, ("pb", "pa")),
            P(None, ("pb", "pa")),
        ),
        check_vma=False,
    )
```

```python
import functools

import jax
import jax.numpy as jnp
from jax import lax
from jax.experimental import pallas as pl
from jax.experimental.pallas import tpu as pltpu
from jax.sharding import PartitionSpec as P

D = 768
HEAD_DIM = 64
QLEN = 32
BIN = 1024
PPB = 8
STEP = 10
QPD = 4
QUERY_ROWS = QPD * QLEN
TOKENS = BIN + QUERY_ROWS
ATTEND_TILE = 512
FEED_ROWS = 512
BACK_ROWS = 256


F32 = jnp.float32
LOW = jnp.bfloat16
sharpness_divisor = 0.1
clip_max = 0.02
learn_rate = 0.04
vector_rate = 0.4
beta_one = 0.9
beta_two = 0.999
adam_eps = 1e-08
decay_rate = 0.01
norm_eps = 1e-12


def shift_pairs(amount):
    return [(i, (i + amount) % 4) for i in range(4)]


FIRST_STEP = [(i, i ^ 2 if i % 2 == 0 else i ^ 4) for i in range(8)]
SECOND_STEP = [(i, i ^ 4 if i % 2 == 0 else i ^ 2) for i in range(8)]
CORE_PAIR = [(i, i ^ 1) for i in range(8)]


def staged_mesh():
    return lax.axis_size("pb") == 8 and lax.axis_size("pa") == 4


def position():
    row = lax.axis_index("pb")
    core, x_bit, y_bit = row % 2, (row // 2) % 2, row // 4
    return (
        lax.axis_index("pa"),
        core,
        jnp.where(core == 0, x_bit, y_bit),
        jnp.where(core == 0, y_bit, x_bit),
    )


def gate(value, *others):
    return lax.optimization_barrier((value, others))[0]


def place_blocks(sources, copies, outputs, index):
    def run(scalars, *refs):
        given, (results, sems) = refs[: len(sources)], (refs[len(sources) : -1], refs[-1])
        moves = [
            pltpu.make_async_copy(
                given[source].at[where(scalars)], results[out].at[there(scalars)], sems.at[number]
            )
            for number, (source, where, out, there) in enumerate(copies)
        ]
        for move in moves:
            move.start()
        for move in moves:
            move.wait()

    anywhere = pl.BlockSpec(memory_space=pl.ANY)
    return pl.pallas_call(
        run,
        grid_spec=pltpu.PrefetchScalarGridSpec(
            num_scalar_prefetch=1,
            grid=(),
            in_specs=[anywhere] * len(sources),
            out_specs=[anywhere] * len(outputs),
            scratch_shapes=[pltpu.SemaphoreType.DMA((len(copies),))],
        ),
        out_shape=outputs,
        compiler_params=pltpu.CompilerParams(vmem_limit_bytes=4 << 20),
        cost_estimate=pl.CostEstimate(
            flops=0,
            transcendentals=0,
            bytes_accessed=2 * sum(o.size * o.dtype.itemsize for o in outputs),
        ),
    )(index, *sources)


def scalars_of_position():
    return jnp.stack([jnp.asarray(v, jnp.int32) for v in position()])


def send_line(part):
    if not staged_mesh():
        return [lax.all_gather(part, "pa", axis=0, tiled=True)]
    return [lax.ppermute(part, "pa", shift_pairs(k)) for k in (1, 2, 3)]


def line_of(part, moved):
    if not staged_mesh():
        return moved[0]
    depth = position()[0]
    around = [part, moved[2], moved[1], moved[0]]
    line = jnp.stack([lax.select_n((place - depth) % 4, *around) for place in range(4)])
    return line.reshape((4 * part.shape[0],) + part.shape[1:])


def gather_rest(line):
    return lax.all_gather(line, "pb", axis=0, tiled=True)


def in_order(own, other, which):
    both = jax.ShapeDtypeStruct((2,) + own.shape, own.dtype)
    copies = [
        (0, lambda s: Ellipsis, 0, lambda s: s[which]),
        (1, lambda s: Ellipsis, 0, lambda s: 1 - s[which]),
    ]
    return place_blocks([own, other], copies, [both], scalars_of_position())[0]


def gather_pair(line, *others):
    if not staged_mesh():
        return line
    return in_order(line, gate(lax.ppermute(line, "pb", FIRST_STEP), others), 2)


def gather_quad(pair, *others):
    if not staged_mesh():
        return pair
    return in_order(pair, gate(lax.ppermute(pair, "pb", SECOND_STEP), others), 3)


def gather_whole(quad, ranges, *others):
    if not staged_mesh():
        whole = gather_rest(quad)
        return [whole[:, low:high] for low, high in ranges]
    partner = gate(lax.ppermute(quad, "pb", CORE_PAIR), others)
    rows = quad.shape[2]
    copies, outputs = [], []
    for number, (low, high) in enumerate(ranges):
        outputs.append(jax.ShapeDtypeStruct((8, rows, high - low), quad.dtype))
        for source in range(2):
            for second in range(2):
                for first in range(2):

                    def where(s, second=second, first=first, low=low, high=high):
                        return second, first, slice(None), slice(low, high)

                    def there(s, source=source, second=second, first=first):
                        core = s[1] if source == 0 else 1 - s[1]
                        swapped = 4 * first + 2 * second
                        return core + jnp.where(core == 0, 4 * second + 2 * first, swapped)

                    copies.append((source, where, number, there))
    results = place_blocks([quad, partner], copies, outputs, scalars_of_position())
    return [a.reshape(8 * rows, a.shape[2]) for a in results]


def split_low(value):
    high = lax.reduce_precision(value, 8, 7)
    return high.astype(LOW), (value - high).astype(LOW)


def packed(arrays, exact):
    pieces = []
    for array, whole in zip(arrays, exact):
        pieces += split_low(array) if whole else [array.astype(LOW)]
    return pieces[0] if len(pieces) == 1 else jnp.concatenate(pieces, -1)


def joined(arrays, exact, moved):
    results, at = [], 0
    for array, whole in zip(arrays, exact):
        total = array.astype(F32)
        for _ in range(2 if whole else 1):
            total = total + moved[..., at : at + array.shape[-1]].astype(F32)
            at += array.shape[-1]
        results.append(total)
    return results


def blocks_at(arrays, place):
    return [lax.dynamic_index_in_dim(array, place, 0, False) for array in arrays]


def scatter_quad(arrays, exact, *others):
    if not staged_mesh():
        return [
            lax.psum_scatter(a.astype(F32), "pb", scatter_dimension=0, tiled=True)
            for a in arrays
        ]
    core = position()[1]
    results = []
    for array, whole in zip(arrays, exact):
        parts = array.reshape((4, 2, array.shape[0] // 8) + array.shape[1:])
        keep, send = (lax.dynamic_index_in_dim(parts, c, 1, False) for c in (core, 1 - core))
        moved = lax.ppermute(send if whole else send.astype(LOW), "pb", CORE_PAIR)
        results.append(keep.astype(F32) + gate(moved, others).astype(F32))
    return results


def scatter_pair(arrays, exact, *others):
    if not staged_mesh():
        return arrays
    _, core, _, bit = position()

    def two_at(bit):
        first = jnp.where(core == 0, 2 * bit, bit)
        second = first + jnp.where(core == 0, 1, 2)
        return [
            jnp.stack([lax.dynamic_index_in_dim(a, i, 0, False) for i in (first, second)])
            for a in arrays
        ]

    send = packed(two_at(1 - bit), exact)
    return joined(two_at(bit), exact, gate(lax.ppermute(send, "pb", SECOND_STEP), others))


def scatter_line(arrays, exact):
    if not staged_mesh():
        return arrays
    bit = position()[2]
    send = packed(blocks_at(arrays, 1 - bit), exact)
    return joined(blocks_at(arrays, bit), exact, lax.ppermute(send, "pb", FIRST_STEP))


def scatter_rest(arrays):
    return [lax.psum_scatter(a, "pa", scatter_dimension=0, tiled=True) for a in arrays]


def scatter_total(arrays, exact):
    if not staged_mesh():
        return scatter_rest(arrays)
    depth = position()[0]
    arrays = [a.reshape((4, a.shape[0] // 4) + a.shape[1:]) for a in arrays]
    total = blocks_at(arrays, depth)
    for k in (1, 2, 3):
        send = packed(blocks_at(arrays, (depth + k) % 4), exact)
        total = joined(total, exact, lax.ppermute(send, "pa", shift_pairs(k)))
    return total


def sum_everywhere(value):
    count = lax.axis_size(("pb", "pa"))
    copies = jnp.broadcast_to(value[None], (count,) + value.shape)
    return jnp.sum(lax.all_to_all(copies, ("pb", "pa"), 0, 0), 0)


ACROSS = (((1,), (1,)), ((), ()))
PLAIN = (((1,), (0,)), ((), ()))


def dot(left, right, dims=PLAIN):
    return lax.dot_general(left, right, dims, preferred_element_type=F32)


def standard(hidden):
    centred = hidden - jnp.mean(hidden, -1, keepdims=True)
    spread = jnp.mean(centred * centred, -1, keepdims=True)
    scale = lax.rsqrt(spread + norm_eps)
    return centred * scale, scale


def standard_backward(grad, unit, scale):
    return scale * (
        grad
        - jnp.mean(grad, -1, keepdims=True)
        - unit * jnp.mean(grad * unit, -1, keepdims=True)
    )


def gelu_with_slope(value):
    below = 0.5 + 0.5 * lax.erf(value * 0.7071067811865476)
    density = 0.3989422804014327 * jnp.exp(-0.5 * value * value)
    return value * below, below + value * density


def columns(array, low=0, high=None):
    width = array.shape[1] - low if high is None else high - low
    spec = pl.BlockSpec(
        (array.shape[0], width), lambda i: (0, low // width), pipeline_mode=pl.Buffered(1)
    )
    return array, spec


def row_call(kernel, rows, first, count, inputs, weights, outputs, sums=(), into=None, flops=0):
    done = 0 if into is None else len(inputs) + len(weights)

    def run(*refs):
        given, results = refs[: len(inputs) + len(weights)], refs[-len(outputs) - len(sums) :]
        if sums:

            @pl.when(pl.program_id(0) == 0)
            def _():
                for place in range(len(sums)):
                    place -= len(sums)
                    start = refs[place - len(outputs) - len(sums)] if done else None
                    here = results[place]
                    here[...] = start[...] if done else jnp.zeros_like(here)

        kernel(*given, *results)

    moved = rows * count * sum(a.shape[1] * a.dtype.itemsize for a, _ in inputs)
    moved += sum(w.size * w.dtype.itemsize for w, _ in weights)
    moved += rows * count * sum(w * jnp.dtype(t).itemsize for w, t in outputs)

    def rows_at(width, begin):
        return pl.BlockSpec((rows, width), lambda i: (begin + i, 0))

    sum_specs = [pl.BlockSpec((16, w), lambda i: (0, 0)) for w in sums]
    in_specs = [rows_at(a.shape[1], begin) for a, begin in inputs]
    in_specs += [spec for _, spec in weights]
    arguments = [a for a, _ in inputs] + [w for w, _ in weights]
    if into is not None:
        in_specs += [pl.BlockSpec(memory_space=pl.ANY)] * len(outputs) + sum_specs
        arguments += list(into)
    return pl.pallas_call(
        run,
        grid=(count,),
        in_specs=in_specs,
        out_specs=[rows_at(w, first) for w, _ in outputs] + sum_specs,
        out_shape=[jax.ShapeDtypeStruct((TOKENS, w), t) for w, t in outputs]
        + [jax.ShapeDtypeStruct((16, w), F32) for w in sums],
        input_output_aliases={done + i: i for i in range(len(outputs) + len(sums))} if done else {},
        compiler_params=pltpu.CompilerParams(vmem_limit_bytes=56 << 20),
        cost_estimate=pl.CostEstimate(
            flops=flops * rows * count, transcendentals=0, bytes_accessed=moved
        ),
    )(*arguments)


def widen_kernel(x_ref, att_ref, out_w, up_w, vec, resid_ref, low_ref, act_ref, slope_ref):
    resid = x_ref[...].astype(F32) + dot(att_ref[...], out_w[...]) + vec[2:3]
    resid_ref[...] = resid
    low = (standard(resid)[0] * vec[3:4] + vec[4:5]).astype(LOW)
    low_ref[...] = low
    for row in range(4):
        part = slice(row * D, row * D + D)
        value, slope = gelu_with_slope(dot(low, up_w[:, part]) + vec[5 + row : 6 + row])
        act_ref[:, part] = value.astype(LOW)
        slope_ref[:, part] = slope.astype(LOW)


def narrow_kernel(act_ref, resid_ref, down_w, proj_w, vec, two_ref, low_ref, proj_ref, unit_ref):
    normed = standard(resid_ref[...])[0] * vec[3:4] + vec[4:5]
    two = normed + dot(act_ref[...], down_w[...]) + vec[9:10]
    two_ref[...] = two
    low = (standard(two)[0] * vec[10:11] + vec[11:12]).astype(LOW)
    low_ref[...] = low
    projected = dot(low, proj_w[...])
    proj_ref[...] = projected
    square = jnp.sum(projected * projected, -1, keepdims=True) + 1e-06
    unit_ref[...] = (projected * lax.rsqrt(square)).astype(LOW)


def back_kernel(
    grad_ref, proj_ref, two_ref, slope_ref, resid_ref,
    proj_w, down_w, up_w, out_w, vec,
    gproj_ref, gtwo_ref, ghid_ref, gone_ref, gatt_ref, sum_ref,
):
    def add(row, value):
        sum_ref[row : row + 1, :] += jnp.sum(value, 0, keepdims=True)

    grad, projected = grad_ref[...], proj_ref[...]
    scale = lax.rsqrt(jnp.sum(projected * projected, -1, keepdims=True) + 1e-06)
    along = jnp.sum(projected * grad, -1, keepdims=True)
    gproj = (scale * grad - projected * (scale * scale * scale * along)).astype(LOW)
    gproj_ref[...] = gproj
    gnormed = dot(gproj, proj_w[...], ACROSS)
    unit, scale = standard(two_ref[...])
    add(10, gnormed * unit)
    add(11, gnormed)
    gtwo = standard_backward(gnormed * vec[10:11], unit, scale)
    add(9, gtwo)
    gtwo_low = gtwo.astype(LOW)
    gtwo_ref[...] = gtwo_low
    gnormed = gtwo
    for row in range(4):
        part = slice(row * D, row * D + D)
        ghid = dot(gtwo_low, down_w[part, :], ACROSS) * slope_ref[:, part].astype(F32)
        add(5 + row, ghid)
        ghid_low = ghid.astype(LOW)
        ghid_ref[:, part] = ghid_low
        gnormed = gnormed + dot(ghid_low, up_w[:, part], ACROSS)
    unit, scale = standard(resid_ref[...])
    add(3, gnormed * unit)
    add(4, gnormed)
    gone = standard_backward(gnormed * vec[3:4], unit, scale)
    add(2, gone)
    gone_low = gone.astype(LOW)
    gone_ref[...] = gone_low
    gatt_ref[...] = dot(gone_low, out_w[...], ACROSS).astype(LOW)


def attend_kernel(tile, spans, q_ref, k_ref, v_ref, col, row, out_ref, total_ref, logits, flipped):
    flipped[...] = v_ref[...].T
    lane = lax.broadcasted_iota(jnp.int32, (tile, 128), 1)

    def block(index, carry):
        here = pl.ds(pl.multiple_of(index * tile, tile), tile)
        query = q_ref[here, :] * jnp.asarray(0.125, LOW)
        zero = jnp.zeros_like(query)
        pair = (jnp.where(lane < 64, query, zero), jnp.where(lane < 64, zero, query))
        segment = row[0:1, here]
        low, high = spans[index, 0], spans[index, 1]

        def score(step, tops):
            there = pl.ds(pl.multiple_of(step * tile, tile), tile)
            keys = k_ref[there, :]
            same = col[there, :] == segment
            result = []
            for head in range(2):
                value = jnp.where(same, dot(keys, pair[head], ACROSS), -1e30)
                logits[head, there, :] = value
                result.append(jnp.maximum(tops[head], jnp.max(value, 0, keepdims=True)))
            return tuple(result)

        lowest = jnp.full((1, tile), -1e30, F32)
        tops = lax.fori_loop(low, high, score, (lowest, lowest))

        def mix(step, state):
            there = pl.ds(pl.multiple_of(step * tile, tile), tile)
            result = []
            for head in range(2):
                term = jnp.exp(logits[head, there, :] - tops[head])
                result.append(state[2 * head] + jnp.sum(term, 0, keepdims=True))
                values = flipped[64 * head : 64 * head + 64, there]
                result.append(state[2 * head + 1] + dot(values, term.astype(LOW)))
            return tuple(result)

        none, empty = jnp.zeros((1, tile), F32), jnp.zeros((64, tile), F32)
        sum0, mix0, sum1, mix1 = lax.fori_loop(low, high, mix, (none, empty, none, empty))
        both = jnp.concatenate([mix0 / sum0, mix1 / sum1], 0)
        out_ref[here, :] = both.T.astype(LOW)
        total_ref[0, 0:1, here] = tops[0] + jnp.log(sum0)
        total_ref[0, 1:2, here] = tops[1] + jnp.log(sum1)
        return carry

    lax.fori_loop(0, q_ref.shape[0] // tile, block, 0)


def head_pair(count, row, first):
    return pl.BlockSpec((count, 128), lambda h, s: (row, first + h))


def attend_call(kernel, tile, count, pairs, tables, arrays, specs, outputs, into, scratch, cost):
    spans, col, row = tables
    specs = specs + [
        pl.BlockSpec((count, tile), lambda h, s: (0, 0)),
        pl.BlockSpec((8, count), lambda h, s: (0, 0)),
    ]
    arguments = [spans, *arrays, col, row]
    aliases = {}
    used = len(arguments)
    if into is not None:
        aliases = {used + i: i for i in range(len(into))}
        specs = specs + [pl.BlockSpec(memory_space=pl.ANY)] * len(into)
        arguments += list(into)

    def run(*refs):
        kernel(tile, *refs[:used], *refs[len(arguments) :])

    return pl.pallas_call(
        run,
        out_shape=[shape for shape, _ in outputs],
        grid_spec=pltpu.PrefetchScalarGridSpec(
            num_scalar_prefetch=1,
            grid=(pairs,),
            in_specs=specs,
            out_specs=[spec for _, spec in outputs],
            scratch_shapes=scratch,
        ),
        input_output_aliases=aliases,
        compiler_params=pltpu.CompilerParams(vmem_limit_bytes=48 << 20),
        cost_estimate=pl.CostEstimate(
            flops=cost * pairs * count * count * 128,
            transcendentals=0,
            bytes_accessed=8 * pairs * count * 128,
        ),
    )(*arguments)


def attend_forward(mixed, tables, tile, first, pairs, row, into=None):
    count = mixed.shape[0]
    return attend_call(
        attend_kernel,
        tile,
        count,
        pairs,
        tables,
        [mixed] * 3,
        [head_pair(count, 0, third * 6 + first) for third in range(3)],
        [
            (jax.ShapeDtypeStruct((TOKENS, D), LOW), head_pair(count, row, first)),
            (
                jax.ShapeDtypeStruct((6, 8, count), F32),
                pl.BlockSpec((1, 8, count), lambda h, s: (first + h, 0, 0)),
            ),
        ],
        into,
        [pltpu.VMEM((2, count, tile), F32), pltpu.VMEM((128, count), LOW)],
        40,
    )


def attend_back_kernel(
    tile, spans, q_ref, k_ref, v_ref, g_ref, total_ref, col, row,
    grad_ref, sum_ref, flipped, gkey, gvalue, probs, gprobs,
):
    flipped[...] = k_ref[...].T
    gkey[...] = jnp.zeros_like(gkey)
    gvalue[...] = jnp.zeros_like(gvalue)
    lane = lax.broadcasted_iota(jnp.int32, (tile, 128), 1)

    def block(index, query_sum):
        here = pl.ds(pl.multiple_of(index * tile, tile), tile)
        query = q_ref[here, :] * jnp.asarray(0.125, LOW)
        zero = jnp.zeros_like(query)
        queries = (jnp.where(lane < 64, query, zero), jnp.where(lane < 64, zero, query))
        grad = g_ref[here, :]
        grads = (jnp.where(lane < 64, grad, zero), jnp.where(lane < 64, zero, grad))
        totals = (total_ref[0, 0:1, here], total_ref[0, 1:2, here])
        segment = row[0:1, here]
        low, high = spans[index, 0], spans[index, 1]

        def first(step, dots):
            there = pl.ds(pl.multiple_of(step * tile, tile), tile)
            keys, values = k_ref[there, :], v_ref[there, :]
            same = col[there, :] == segment
            result = []
            part = None
            for head in range(2):
                logit = dot(keys, queries[head], ACROSS)
                prob = jnp.where(same, jnp.exp(logit - totals[head]), 0.0)
                gprob = dot(values, grads[head], ACROSS)
                probs[head, there, :] = prob
                gprobs[head, there, :] = gprob
                result.append(dots[head] + jnp.sum(prob * gprob, 0, keepdims=True))
                more = dot(prob.astype(LOW), grads[head])
                part = more if part is None else part + more
            gvalue[there, :] += part
            return tuple(result)

        none = jnp.zeros((1, tile), F32)
        dots = lax.fori_loop(low, high, first, (none, none))

        def second(step, state):
            there = pl.ds(pl.multiple_of(step * tile, tile), tile)
            result = []
            part = None
            for head in range(2):
                delta = probs[head, there, :] * (gprobs[head, there, :] - dots[head])
                delta = delta.astype(LOW)
                more = dot(delta, queries[head])
                part = more if part is None else part + more
                keys = flipped[64 * head : 64 * head + 64, there]
                result.append(state[head] + dot(keys, delta))
            gkey[there, :] += part
            return tuple(result)

        empty = jnp.zeros((64, tile), F32)
        both = lax.fori_loop(low, high, second, (empty, empty))
        whole = jnp.concatenate(both, 0).T * 0.125
        grad_ref[0, here, :] = whole.astype(LOW)
        return query_sum + jnp.sum(whole, 0, keepdims=True)

    count = q_ref.shape[0]
    query_sum = lax.fori_loop(0, count // tile, block, jnp.zeros((1, 128), F32))
    grad_ref[1] = gkey[...].astype(LOW)
    grad_ref[2] = gvalue[...].astype(LOW)
    sum_ref[...] = jnp.zeros_like(sum_ref)
    sum_ref[0:1, :] = query_sum
    sum_ref[1:2, :] = jnp.sum(gvalue[...], 0, keepdims=True)


def attend_backward(mixed, grad, total, tables, tile, first, pairs, row, into=None):
    count = mixed.shape[0]
    return attend_call(
        attend_back_kernel,
        tile,
        count,
        pairs,
        tables,
        [mixed] * 3 + [grad, total],
        [head_pair(count, 0, third * 6 + first) for third in range(3)]
        + [
            head_pair(count, row, first),
            pl.BlockSpec((1, 8, count), lambda h, s: (first + h, 0, 0)),
        ],
        [
            (
                jax.ShapeDtypeStruct((3, TOKENS, D), LOW),
                pl.BlockSpec((3, count, 128), lambda h, s: (0, row, first + h)),
            ),
            (
                jax.ShapeDtypeStruct((16, D), F32),
                pl.BlockSpec((16, 128), lambda h, s: (0, first + h)),
            ),
        ],
        into,
        [
            pltpu.VMEM((128, count), LOW),
            pltpu.VMEM((count, 128), F32),
            pltpu.VMEM((count, 128), F32),
            pltpu.VMEM((2, count, tile), F32),
            pltpu.VMEM((2, count, tile), F32),
        ],
        80,
    )


def segment_tables(segment, tile):
    count = segment.shape[0]
    ends = segment.reshape(count // tile, tile)
    first = jnp.sum((segment[None, :] < ends[:, :1]).astype(jnp.int32), 1)
    last = jnp.sum((segment[None, :] <= ends[:, -1:]).astype(jnp.int32), 1)
    return (
        jnp.stack([first // tile, (last + tile - 1) // tile], 1),
        jnp.broadcast_to(segment[:, None], (count, tile)),
        jnp.broadcast_to(segment[None, :], (8, count)),
    )


def two_terms(value):
    high = value.astype(LOW)
    return high, (value - high.astype(F32)).astype(LOW)


def sharp(cosine):
    return jnp.exp(cosine * 10.0 - 10.0)


def score_kernel(query_ref, passage_ref, member_ref, score_ref, sums_ref):
    high, rest = two_terms(sharp(dot(query_ref[...], passage_ref[...], ACROSS)))
    sums = dot(high, member_ref[...]) + dot(rest, member_ref[...])
    sums_ref[...] = sums
    lane = lax.broadcasted_iota(jnp.int32, sums.shape, 1)
    soft = jnp.where(lane < PPB, 0.1 * jnp.log(jnp.where(lane < PPB, sums, 1.0)) + 1.0, 0.0)
    score_ref[...] = jnp.sum(soft.reshape(-1, QLEN, 128), 1)


def score_ratio(grad_ref, sums_ref):
    rows = sums_ref.shape[0]
    lane = lax.broadcasted_iota(jnp.int32, (rows, 128), 1)
    grads = jnp.broadcast_to(grad_ref[...][:, None, :], (rows // QLEN, QLEN, 128))
    ratio = grads.reshape(rows, 128) / jnp.where(lane % 64 < PPB, sums_ref[...], 1.0)
    high, rest = two_terms(ratio)
    return jnp.where(lane < 64, high, rest)


def score_query_kernel(query_ref, passage_ref, member_ref, grad_ref, sums_ref, out_ref):
    ratio = score_ratio(grad_ref, sums_ref)
    terms = sharp(dot(query_ref[...], passage_ref[...], ACROSS))
    terms = (terms * dot(ratio, member_ref[...], ACROSS)).astype(LOW)
    out_ref[...] = dot(terms, passage_ref[...])


def score_passage_kernel(query_ref, passage_ref, member_ref, grad_ref, sums_ref, out_ref):
    @pl.when(pl.program_id(0) == 0)
    def _():
        out_ref[...] = jnp.zeros_like(out_ref)

    ratio = score_ratio(grad_ref, sums_ref)
    terms = sharp(dot(passage_ref[...], query_ref[...], ACROSS))
    terms = (terms * dot(member_ref[...], ratio, ACROSS)).astype(LOW)
    out_ref[...] += dot(terms, query_ref[...])


SCORE_ROWS = 512


def score_call(kernel, inputs, in_specs, out_specs, out_shape, flops):
    return pl.pallas_call(
        kernel,
        grid=(inputs[0].shape[0] // SCORE_ROWS,),
        in_specs=in_specs,
        out_specs=out_specs,
        out_shape=out_shape,
        compiler_params=pltpu.CompilerParams(vmem_limit_bytes=40 << 20),
        cost_estimate=pl.CostEstimate(
            flops=flops,
            transcendentals=inputs[0].shape[0] * BIN,
            bytes_accessed=inputs[0].shape[0] * 1024,
        ),
    )(*inputs)


def score_specs():
    rows = SCORE_ROWS
    fixed = pl.BlockSpec((BIN, 128), lambda i: (0, 0))
    return (
        pl.BlockSpec((rows, 128), lambda i: (i, 0)),
        fixed,
        pl.BlockSpec((rows // QLEN, 128), lambda i: (i, 0)),
    )


def score_forward(queries, passages, member):
    rows, fixed, grads = score_specs()
    count = queries.shape[0]
    return score_call(
        score_kernel,
        (queries, passages, member),
        [rows, fixed, fixed],
        [grads, rows],
        [
            jax.ShapeDtypeStruct((count // QLEN, 128), F32),
            jax.ShapeDtypeStruct((count, 128), F32),
        ],
        6 * count * BIN * 128,
    )


def score_backward(kernel, queries, passages, member, grad_scores, sums):
    rows, fixed, grads = score_specs()
    count = queries.shape[0]
    inputs = (queries, passages, member, grad_scores, sums)
    in_specs = [rows, fixed, fixed, grads, rows]
    width, spec = (BIN, fixed) if kernel is score_passage_kernel else (count, rows)
    out = jax.ShapeDtypeStruct((width, 128), F32)
    return score_call(kernel, inputs, in_specs, spec, out, 6 * count * BIN * 128)


def cross_grad(scores, partition, passage_ids, chosen_ids, query_total):
    onehot = (passage_ids[None, :] == chosen_ids[:, None]).astype(jnp.float32)
    return (jnp.exp(scores) / partition[:, None] - onehot) / query_total


def adam_update(weight, moment_one, moment_two, gradient, factor, rate):
    clipped = gradient * factor
    new_one = beta_one * moment_one + (1.0 - beta_one) * clipped
    new_two = beta_two * moment_two + (1.0 - beta_two) * clipped * clipped
    direction = (
        new_one / (1.0 - beta_one**STEP) / (jnp.sqrt(new_two / (1.0 - beta_two**STEP)) + adam_eps)
    )
    return (weight - rate * (direction + decay_rate * weight), new_one, new_two)


def body(
    query_tokens,
    passage_tokens,
    passage_lengths,
    positives,
    qkv_weight,
    qkv_first,
    qkv_second,
    out_weight,
    out_first,
    out_second,
    up_weight,
    up_first,
    up_second,
    down_weight,
    down_first,
    down_second,
    proj_weight,
    proj_first,
    proj_second,
    vector_params,
    vector_first,
    vector_second,
):
    own_index = lax.axis_index(("pb", "pa"))
    query_total = QPD * lax.axis_size(("pb", "pa"))
    query_flat = query_tokens.reshape(QUERY_ROWS, D)
    tokens = jnp.concatenate([passage_tokens[0], query_flat], 0)
    query_tables = segment_tables(jnp.arange(QUERY_ROWS, dtype=jnp.int32) // QLEN, QUERY_ROWS)
    own_lengths = lax.dynamic_index_in_dim(passage_lengths, own_index, 0, keepdims=False)
    ends = jnp.cumsum(own_lengths)
    places = jnp.arange(BIN, dtype=jnp.int32)
    own_seg = jnp.sum((places[:, None] >= ends[None, :]).astype(jnp.int32), 1)
    passage_tables = segment_tables(own_seg, ATTEND_TILE)
    member = (own_seg[:, None] == jnp.arange(128, dtype=jnp.int32)[None, :] % 64).astype(LOW)

    vector_part = jnp.pad(vector_params.T, ((0, 0), (0, 116))).astype(LOW)
    first_part = jnp.concatenate([qkv_weight.astype(LOW), vector_part], 1)
    middle_part = jnp.concatenate([up_weight, out_weight, proj_weight], 1).astype(LOW)
    down_part = down_weight.astype(LOW)
    first_line = line_of(first_part, send_line(first_part))
    middle_moved = send_line(gate(middle_part, first_line))
    first_pair = gather_pair(first_line)
    ready = gate((tokens, query_tables, passage_tables, member), first_pair)
    first_quad = gather_quad(first_pair, ready)
    tokens, query_tables, passage_tables, member = ready
    middle = gather_rest(line_of(middle_part, gate(middle_moved, first_quad)))
    qkv_matrix, vectors = gather_whole(first_quad, [(0, 2304), (2304, 2432)])
    vectors = vectors[:, :12].T.astype(F32)
    bias_qkv = jnp.concatenate([vectors[0], jnp.zeros_like(vectors[0]), vectors[1]])

    def mix(rows):
        return (dot(rows, qkv_matrix) + bias_qkv).astype(LOW)

    query_mixed = mix(query_flat)
    down_moved = send_line(gate(down_part, query_mixed))
    passage_mixed = mix(gate(passage_tokens[0], query_mixed))
    attended, query_log = attend_forward(
        gate(query_mixed, passage_mixed), query_tables, QUERY_ROWS, 0, 6, BIN // QUERY_ROWS
    )
    down_line = line_of(down_part, gate(down_moved, attended))
    passage_state = attend_forward(
        gate(passage_mixed, down_line), passage_tables, ATTEND_TILE, 0, 3, 0, (attended,)
    )
    down_pair = gather_pair(down_line, passage_state)
    attended, passage_log = attend_forward(
        gate(passage_mixed, down_pair), passage_tables, ATTEND_TILE, 3, 3, 0, passage_state
    )
    down_quad = gather_quad(down_pair, attended)
    up = columns(middle, 0, 4 * D)
    out = columns(middle, 4 * D, 5 * D)
    proj = columns(middle, 5 * D, 5 * D + 128)
    vector_rows = columns(vectors)

    def widen(rows, first, count, att, into):
        return row_call(
            widen_kernel,
            rows,
            first,
            count,
            [(tokens, first), (att, first)],
            (out, up, vector_rows),
            [(D, F32), (D, LOW), (4 * D, LOW), (4 * D, LOW)],
            into=into,
            flops=10 * D * D,
        )

    def narrow(rows, first, count, wider, into):
        return row_call(
            narrow_kernel,
            rows,
            first,
            count,
            [(wider[2], first), (wider[0], first)],
            (down, proj, vector_rows),
            [(D, F32), (D, LOW), (128, F32), (128, LOW)],
            into=into,
            flops=8 * D * D,
        )

    wider = widen(QUERY_ROWS, BIN // QUERY_ROWS, 1, gate(attended, down_quad), None)
    (down_matrix,) = gather_whole(down_quad, [(0, D)], wider)
    down = columns(down_matrix)
    narrower = narrow(QUERY_ROWS, BIN // QUERY_ROWS, 1, wider, None)
    query_part = narrower[3][BIN:]
    query_line = line_of(query_part, send_line(query_part))
    every_query = gather_rest(query_line)
    wider = widen(
        FEED_ROWS, 0, BIN // FEED_ROWS, gate(attended, query_line), gate(wider, narrower)
    )
    narrower = narrow(FEED_ROWS, 0, BIN // FEED_ROWS, wider, narrower)
    resid, normed, active, slope = wider
    two, normed_out, projected, unit = narrower
    passage_unit = unit[:BIN]

    passage_ids = own_index * PPB + jnp.arange(PPB, dtype=jnp.int32)
    scores, totals = score_forward(every_query, passage_unit, member)
    scores = scores[:, :PPB]
    partition = sum_everywhere(jnp.sum(jnp.exp(scores), 1))
    grad_scores = cross_grad(scores, partition, passage_ids, positives, query_total)
    grad_scores = jnp.tile(jnp.pad(grad_scores, ((0, 0), (0, 64 - PPB))), (1, 2))
    grad_every = score_backward(
        score_query_kernel, every_query, passage_unit, member, grad_scores, totals
    )
    whole, rounded = (True,), (False,)
    query_back = scatter_quad([grad_every], whole)
    grad_passage = score_backward(
        score_passage_kernel,
        gate(every_query, query_back),
        passage_unit,
        member,
        grad_scores,
        totals,
    )

    def go_back(rows, first, count, grad, into):
        return row_call(
            back_kernel,
            rows,
            first,
            count,
            [grad, (projected, first), (two, first), (slope, first), (resid, first)],
            (proj, down, up, out, vector_rows),
            [(128, LOW), (D, LOW), (4 * D, LOW), (D, LOW), (D, LOW)],
            (D,),
            into=into,
            flops=18 * D * D,
        )

    query_back = scatter_pair(query_back, whole)
    back = go_back(
        BACK_ROWS, 0, BIN // BACK_ROWS, (gate(grad_passage, query_back), 0), None
    )
    query_back = scatter_line(query_back, whole)
    (grad_query,) = scatter_total(gate(query_back, back), whole)
    back = go_back(QUERY_ROWS, BIN // QUERY_ROWS, 1, (grad_query, 0), back)
    gproj, gtwo, ghid, gone, gatt, sums = back

    def terms(left, right):
        return dot(left, right, (((0,), (0,)), ((), ())))

    def attend_back(first, pairs, into, *others):
        mixed = gate(passage_mixed, *others)
        return attend_backward(
            mixed, gatt, passage_log, passage_tables, ATTEND_TILE, first, pairs, 0, into
        )

    down_terms = terms(active, gtwo)
    up_terms = terms(normed, gate(ghid, down_terms))
    down_back = scatter_quad([down_terms], rounded, up_terms)
    down_back = scatter_pair(down_back, rounded)
    rest = gate((gone, gproj), up_terms)
    out_terms, proj_terms = terms(attended, rest[0]), terms(normed_out, rest[1])
    query_grads = attend_backward(
        gate(query_mixed, out_terms, proj_terms),
        gatt,
        query_log,
        query_tables,
        QUERY_ROWS,
        0,
        6,
        BIN // QUERY_ROWS,
    )
    kinds = (False, False, True)
    middle_back = scatter_quad([up_terms, out_terms, proj_terms], kinds, query_grads)
    middle_back = scatter_pair(middle_back, kinds)
    down_back = scatter_line(down_back, rounded)
    grads = attend_back(0, 2, query_grads[:1], query_grads)
    (down_sum,) = scatter_total(gate(down_back, grads), rounded)
    middle_back = scatter_line(gate(middle_back, grads), kinds)
    grads = attend_back(2, 2, grads)
    up_sum, out_sum, proj_sum = scatter_total(gate(middle_back, grads), kinds)
    grads = attend_back(4, 2, grads, down_sum)
    first_terms = [terms(tokens, grads[0][third]) for third in range(3)]
    mixed_sums = grads[1] + query_grads[1]
    vector_grad = jnp.concatenate([mixed_sums[:2], sums[2:12]], 0)
    vector_terms = jnp.pad(vector_grad.T, ((0, 0), (0, 116)))
    kinds = (False,) * 4
    first_back = scatter_quad([*first_terms, vector_terms], kinds)
    first_back = scatter_pair(first_back, kinds, up_sum)
    *thirds, vector_sum = scatter_total(scatter_line(first_back, kinds), kinds)
    qkv_sum = jnp.concatenate(thirds, 1)
    reduced = (qkv_sum, out_sum, up_sum, down_sum, proj_sum, vector_sum[:, :12].T)
    square = sum((jnp.sum(gradient * gradient) for gradient in reduced))
    norm_value = jnp.sqrt(sum_everywhere(jnp.full((1, 128), square))[0, 0])
    factor = jnp.minimum(1.0, clip_max / (norm_value + 1e-06))
    qkv_res = adam_update(qkv_weight, qkv_first, qkv_second, reduced[0], factor, learn_rate)
    out_res = adam_update(out_weight, out_first, out_second, reduced[1], factor, learn_rate)
    up_res = adam_update(up_weight, up_first, up_second, reduced[2], factor, learn_rate)
    down_res = adam_update(down_weight, down_first, down_second, reduced[3], factor, learn_rate)
    proj_res = adam_update(proj_weight, proj_first, proj_second, reduced[4], factor, learn_rate)
    vector_res = adam_update(
        vector_params, vector_first, vector_second, reduced[5], factor, vector_rate
    )
    return (
        norm_value,
        qkv_res[0],
        qkv_res[1],
        qkv_res[2],
        out_res[0],
        out_res[1],
        out_res[2],
        up_res[0],
        up_res[1],
        up_res[2],
        down_res[0],
        down_res[1],
        down_res[2],
        proj_res[0],
        proj_res[1],
        proj_res[2],
        vector_res[0],
        vector_res[1],
        vector_res[2],
    )


def solution(mesh):
    placed = (
        P(("pb", "pa"), None, None),
        P(("pb", "pa"), None, None),
        P(),
        P(),
        P(("pb", "pa"), None),
        P(("pb", "pa"), None),
        P(("pb", "pa"), None),
        P(("pb", "pa"), None),
        P(("pb", "pa"), None),
        P(("pb", "pa"), None),
        P(("pb", "pa"), None),
        P(("pb", "pa"), None),
        P(("pb", "pa"), None),
        P(("pb", "pa"), None),
        P(("pb", "pa"), None),
        P(("pb", "pa"), None),
        P(("pb", "pa"), None),
        P(("pb", "pa"), None),
        P(("pb", "pa"), None),
        P(None, ("pb", "pa")),
        P(None, ("pb", "pa")),
        P(None, ("pb", "pa")),
    )
    return jax.shard_map(
        body,
        mesh=mesh,
        in_specs=placed,
        out_specs=(
            P(),
            P(("pb", "pa"), None),
            P(("pb", "pa"), None),
            P(("pb", "pa"), None),
            P(("pb", "pa"), None),
            P(("pb", "pa"), None),
            P(("pb", "pa"), None),
            P(("pb", "pa"), None),
            P(("pb", "pa"), None),
            P(("pb", "pa"), None),
            P(("pb", "pa"), None),
            P(("pb", "pa"), None),
            P(("pb", "pa"), None),
            P(("pb", "pa"), None),
            P(("pb", "pa"), None),
            P(("pb", "pa"), None),
            P(None, ("pb", "pa")),
            P(None, ("pb", "pa")),
            P(None, ("pb", "pa")),
        ),
        check_vma=False,
    )
```

```python
import functools

import jax
import jax.numpy as jnp
from jax import lax
from jax.experimental import pallas as pl
from jax.experimental.pallas import tpu as pltpu
from jax.sharding import PartitionSpec as P

D = 768
HEAD_DIM = 64
QLEN = 32
BIN = 1024
PPB = 8
STEP = 10
QPD = 4
QUERY_ROWS = QPD * QLEN
TOKENS = BIN + QUERY_ROWS
ATTEND_TILE = 256
FEED_ROWS = 256
BACK_ROWS = 256


F32 = jnp.float32
LOW = jnp.bfloat16
sharpness_divisor = 0.1
clip_max = 0.02
learn_rate = 0.04
vector_rate = 0.4
beta_one = 0.9
beta_two = 0.999
adam_eps = 1e-08
decay_rate = 0.01
norm_eps = 1e-12


def shift_pairs(amount):
    return [(i, (i + amount) % 4) for i in range(4)]


FIRST_STEP = [(i, i ^ 2 if i % 2 == 0 else i ^ 4) for i in range(8)]
SECOND_STEP = [(i, i ^ 4 if i % 2 == 0 else i ^ 2) for i in range(8)]
CORE_PAIR = [(i, i ^ 1) for i in range(8)]


def staged_mesh():
    return lax.axis_size("pb") == 8 and lax.axis_size("pa") == 4


def position():
    row = lax.axis_index("pb")
    core, x_bit, y_bit = row % 2, (row // 2) % 2, row // 4
    return (
        lax.axis_index("pa"),
        core,
        jnp.where(core == 0, x_bit, y_bit),
        jnp.where(core == 0, y_bit, x_bit),
    )


def gate(value, *others):
    return lax.optimization_barrier((value, others))[0]


def place_blocks(sources, copies, outputs, index):
    def run(scalars, *refs):
        given, (results, sems) = refs[: len(sources)], (refs[len(sources) : -1], refs[-1])
        moves = [
            pltpu.make_async_copy(
                given[source].at[where(scalars)], results[out].at[there(scalars)], sems.at[number]
            )
            for number, (source, where, out, there) in enumerate(copies)
        ]
        for move in moves:
            move.start()
        for move in moves:
            move.wait()

    anywhere = pl.BlockSpec(memory_space=pl.ANY)
    return pl.pallas_call(
        run,
        grid_spec=pltpu.PrefetchScalarGridSpec(
            num_scalar_prefetch=1,
            grid=(),
            in_specs=[anywhere] * len(sources),
            out_specs=[anywhere] * len(outputs),
            scratch_shapes=[pltpu.SemaphoreType.DMA((len(copies),))],
        ),
        out_shape=outputs,
        compiler_params=pltpu.CompilerParams(vmem_limit_bytes=4 << 20),
        cost_estimate=pl.CostEstimate(
            flops=0,
            transcendentals=0,
            bytes_accessed=2 * sum(o.size * o.dtype.itemsize for o in outputs),
        ),
    )(index, *sources)


def scalars_of_position():
    return jnp.stack([jnp.asarray(v, jnp.int32) for v in position()])


def send_line(part):
    if not staged_mesh():
        return [lax.all_gather(part, "pa", axis=0, tiled=True)]
    return [lax.ppermute(part, "pa", shift_pairs(k)) for k in (1, 2, 3)]


def line_of(part, moved):
    if not staged_mesh():
        return moved[0]
    depth = position()[0]
    around = [part, moved[2], moved[1], moved[0]]
    line = jnp.stack([lax.select_n((place - depth) % 4, *around) for place in range(4)])
    return line.reshape((4 * part.shape[0],) + part.shape[1:])


def gather_rest(line):
    return lax.all_gather(line, "pb", axis=0, tiled=True)


def in_order(own, other, which):
    both = jax.ShapeDtypeStruct((2,) + own.shape, own.dtype)
    copies = [
        (0, lambda s: Ellipsis, 0, lambda s: s[which]),
        (1, lambda s: Ellipsis, 0, lambda s: 1 - s[which]),
    ]
    return place_blocks([own, other], copies, [both], scalars_of_position())[0]


def gather_pair(line, *others):
    if not staged_mesh():
        return line
    return in_order(line, gate(lax.ppermute(line, "pb", FIRST_STEP), others), 2)


def gather_quad(pair, *others):
    if not staged_mesh():
        return pair
    return in_order(pair, gate(lax.ppermute(pair, "pb", SECOND_STEP), others), 3)


def gather_whole(quad, ranges, *others):
    if not staged_mesh():
        whole = gather_rest(quad)
        return [whole[:, low:high] for low, high in ranges]
    partner = gate(lax.ppermute(quad, "pb", CORE_PAIR), others)
    rows = quad.shape[2]
    copies, outputs = [], []
    for number, (low, high) in enumerate(ranges):
        outputs.append(jax.ShapeDtypeStruct((8, rows, high - low), quad.dtype))
        for source in range(2):
            for second in range(2):
                for first in range(2):

                    def where(s, second=second, first=first, low=low, high=high):
                        return second, first, slice(None), slice(low, high)

                    def there(s, source=source, second=second, first=first):
                        core = s[1] if source == 0 else 1 - s[1]
                        swapped = 4 * first + 2 * second
                        return core + jnp.where(core == 0, 4 * second + 2 * first, swapped)

                    copies.append((source, where, number, there))
    results = place_blocks([quad, partner], copies, outputs, scalars_of_position())
    return [a.reshape(8 * rows, a.shape[2]) for a in results]


def split_low(value):
    high = lax.reduce_precision(value, 8, 7)
    return high.astype(LOW), (value - high).astype(LOW)


def packed(arrays, exact):
    pieces = []
    for array, whole in zip(arrays, exact):
        pieces += split_low(array) if whole else [array.astype(LOW)]
    return pieces[0] if len(pieces) == 1 else jnp.concatenate(pieces, -1)


def joined(arrays, exact, moved):
    results, at = [], 0
    for array, whole in zip(arrays, exact):
        total = array.astype(F32)
        for _ in range(2 if whole else 1):
            total = total + moved[..., at : at + array.shape[-1]].astype(F32)
            at += array.shape[-1]
        results.append(total)
    return results


def blocks_at(arrays, place):
    return [lax.dynamic_index_in_dim(array, place, 0, False) for array in arrays]


def core_blocks(array, other):
    core = position()[1]
    parts = array.reshape((4, 2, array.shape[0] // 8) + array.shape[1:])
    return lax.dynamic_index_in_dim(parts, 1 - core if other else core, 1, False)


def scatter_sends(arrays, exact):
    if not staged_mesh():
        return arrays
    sends = [core_blocks(array, True) for array in arrays]
    return [a if whole else a.astype(LOW) for a, whole in zip(sends, exact)]


def scatter_quad(arrays, sends, *others):
    if not staged_mesh():
        return [
            lax.psum_scatter(a.astype(F32), "pb", scatter_dimension=0, tiled=True)
            for a in arrays
        ]
    moved = gate([lax.ppermute(a, "pb", CORE_PAIR) for a in sends], others)
    return [
        core_blocks(array, False).astype(F32) + m.astype(F32) for array, m in zip(arrays, moved)
    ]


def scatter_pair(arrays, exact, *others):
    if not staged_mesh():
        return arrays
    _, core, _, bit = position()

    def two_at(bit):
        first = jnp.where(core == 0, 2 * bit, bit)
        second = first + jnp.where(core == 0, 1, 2)
        return [
            jnp.stack([lax.dynamic_index_in_dim(a, i, 0, False) for i in (first, second)])
            for a in arrays
        ]

    send = packed(two_at(1 - bit), exact)
    return joined(two_at(bit), exact, gate(lax.ppermute(send, "pb", SECOND_STEP), others))


def scatter_line(arrays, exact):
    if not staged_mesh():
        return arrays
    bit = position()[2]
    send = packed(blocks_at(arrays, 1 - bit), exact)
    return joined(blocks_at(arrays, bit), exact, lax.ppermute(send, "pb", FIRST_STEP))


def scatter_rest(arrays):
    return [lax.psum_scatter(a, "pa", scatter_dimension=0, tiled=True) for a in arrays]


def scatter_total(arrays, exact):
    if not staged_mesh():
        return scatter_rest(arrays)
    depth = position()[0]
    arrays = [a.reshape((4, a.shape[0] // 4) + a.shape[1:]) for a in arrays]
    total = blocks_at(arrays, depth)
    for k in (1, 2, 3):
        send = packed(blocks_at(arrays, (depth + k) % 4), exact)
        total = joined(total, exact, lax.ppermute(send, "pa", shift_pairs(k)))
    return total


def sum_everywhere(value):
    count = lax.axis_size(("pb", "pa"))
    copies = jnp.broadcast_to(value[None], (count,) + value.shape)
    return jnp.sum(lax.all_to_all(copies, ("pb", "pa"), 0, 0), 0)


ACROSS = (((1,), (1,)), ((), ()))
PLAIN = (((1,), (0,)), ((), ()))


def dot(left, right, dims=PLAIN):
    return lax.dot_general(left, right, dims, preferred_element_type=F32)


def standard(hidden):
    centred = hidden - jnp.mean(hidden, -1, keepdims=True)
    spread = jnp.mean(centred * centred, -1, keepdims=True)
    scale = lax.rsqrt(spread + norm_eps)
    return centred * scale, scale


def standard_backward(grad, unit, scale):
    return scale * (
        grad
        - jnp.mean(grad, -1, keepdims=True)
        - unit * jnp.mean(grad * unit, -1, keepdims=True)
    )


def gelu_with_slope(value):
    below = 0.5 + 0.5 * lax.erf(value * 0.7071067811865476)
    density = 0.3989422804014327 * jnp.exp(-0.5 * value * value)
    return value * below, below + value * density


def columns(array, low=0, high=None):
    width = array.shape[1] - low if high is None else high - low
    spec = pl.BlockSpec(
        (array.shape[0], width), lambda i: (0, low // width), pipeline_mode=pl.Buffered(1)
    )
    return array, spec


def transposed(array):
    rows, width = array.shape
    return pl.pallas_call(
        lambda x_ref, out_ref: out_ref.__setitem__(Ellipsis, x_ref[...].T),
        grid=(width // 128,),
        in_specs=[pl.BlockSpec((rows, 128), lambda i: (0, i))],
        out_specs=pl.BlockSpec((128, rows), lambda i: (i, 0)),
        out_shape=jax.ShapeDtypeStruct((width, rows), array.dtype),
    )(array)


def row_call(kernel, rows, first, count, inputs, weights, outputs, sums=(), into=None, flops=0):
    done = 0 if into is None else len(inputs) + len(weights)

    def run(*refs):
        given, results = refs[: len(inputs) + len(weights)], refs[-len(outputs) - len(sums) :]
        if sums:

            @pl.when(pl.program_id(0) == 0)
            def _():
                for place in range(len(sums)):
                    place -= len(sums)
                    start = refs[place - len(outputs) - len(sums)] if done else None
                    here = results[place]
                    here[...] = start[...] if done else jnp.zeros_like(here)

        kernel(*given, *results)

    moved = rows * count * sum(a.shape[1] * a.dtype.itemsize for a, _ in inputs)
    moved += sum(w.size * w.dtype.itemsize for w, _ in weights)
    moved += rows * count * sum(w * jnp.dtype(t).itemsize for w, t in outputs)

    def rows_at(width, begin):
        return pl.BlockSpec((rows, width), lambda i: (begin + i, 0))

    sum_specs = [pl.BlockSpec((16, w), lambda i: (0, 0)) for w in sums]
    in_specs = [rows_at(a.shape[1], begin) for a, begin in inputs]
    in_specs += [spec for _, spec in weights]
    arguments = [a for a, _ in inputs] + [w for w, _ in weights]
    if into is not None:
        in_specs += [pl.BlockSpec(memory_space=pl.ANY)] * len(outputs) + sum_specs
        arguments += list(into)
    return pl.pallas_call(
        run,
        grid=(count,),
        in_specs=in_specs,
        out_specs=[rows_at(w, first) for w, _ in outputs] + sum_specs,
        out_shape=[jax.ShapeDtypeStruct((TOKENS, w), t) for w, t in outputs]
        + [jax.ShapeDtypeStruct((16, w), F32) for w in sums],
        input_output_aliases={done + i: i for i in range(len(outputs) + len(sums))} if done else {},
        compiler_params=pltpu.CompilerParams(vmem_limit_bytes=56 << 20),
        cost_estimate=pl.CostEstimate(
            flops=flops * rows * count, transcendentals=0, bytes_accessed=moved
        ),
    )(*arguments)


def widen_kernel(x_ref, att_ref, out_w, up_w, vec, resid_ref, low_ref, act_ref, slope_ref):
    resid = x_ref[...].astype(F32) + dot(att_ref[...], out_w[...]) + vec[2:3]
    resid_ref[...] = resid
    low = (standard(resid)[0] * vec[3:4] + vec[4:5]).astype(LOW)
    low_ref[...] = low
    for row in range(4):
        part = slice(row * D, row * D + D)
        value, slope = gelu_with_slope(dot(low, up_w[:, part]) + vec[5 + row : 6 + row])
        act_ref[:, part] = value.astype(LOW)
        slope_ref[:, part] = slope.astype(LOW)


def narrow_kernel(act_ref, resid_ref, down_w, proj_w, vec, two_ref, low_ref, proj_ref, unit_ref):
    normed = standard(resid_ref[...])[0] * vec[3:4] + vec[4:5]
    two = normed + dot(act_ref[...], down_w[...]) + vec[9:10]
    two_ref[...] = two
    low = (standard(two)[0] * vec[10:11] + vec[11:12]).astype(LOW)
    low_ref[...] = low
    projected = dot(low, proj_w[...])
    proj_ref[...] = projected
    square = jnp.sum(projected * projected, -1, keepdims=True) + 1e-06
    unit_ref[...] = (projected * lax.rsqrt(square)).astype(LOW)


def back_kernel(
    grad_ref, proj_ref, two_ref, slope_ref, resid_ref,
    proj_w, down_w, up_w, out_w, vec,
    gproj_ref, gtwo_ref, ghid_ref, gone_ref, gatt_ref, sum_ref,
):
    def add(row, value):
        sum_ref[row : row + 1, :] += jnp.sum(value, 0, keepdims=True)

    grad, projected = grad_ref[...], proj_ref[...]
    scale = lax.rsqrt(jnp.sum(projected * projected, -1, keepdims=True) + 1e-06)
    along = jnp.sum(projected * grad, -1, keepdims=True)
    gproj = (scale * grad - projected * (scale * scale * scale * along)).astype(LOW)
    gproj_ref[...] = gproj
    gnormed = dot(gproj, proj_w[...], ACROSS)
    unit, scale = standard(two_ref[...])
    add(10, gnormed * unit)
    add(11, gnormed)
    gtwo = standard_backward(gnormed * vec[10:11], unit, scale)
    add(9, gtwo)
    gtwo_low = gtwo.astype(LOW)
    gtwo_ref[...] = gtwo_low
    gnormed = gtwo
    for row in range(4):
        part = slice(row * D, row * D + D)
        ghid = dot(gtwo_low, down_w[part, :], ACROSS) * slope_ref[:, part].astype(F32)
        add(5 + row, ghid)
        ghid_low = ghid.astype(LOW)
        ghid_ref[:, part] = ghid_low
        gnormed = gnormed + dot(ghid_low, up_w[:, part], ACROSS)
    unit, scale = standard(resid_ref[...])
    add(3, gnormed * unit)
    add(4, gnormed)
    gone = standard_backward(gnormed * vec[3:4], unit, scale)
    add(2, gone)
    gone_low = gone.astype(LOW)
    gone_ref[...] = gone_low
    gatt_ref[...] = dot(gone_low, out_w[...], ACROSS).astype(LOW)


def attend_kernel(
    tile, lengths, spans, q_ref, k_ref, v_ref, col, row, out_ref, total_ref, logits, probs, flipped
):
    flipped[...] = v_ref[...].T
    lane = lax.broadcasted_iota(jnp.int32, (tile, 128), 1)

    def block(index, carry):
        here = pl.ds(pl.multiple_of(index * tile, tile), tile)
        low, kind = spans[index, 0], spans[index, 1]

        def attend(length):
            there = pl.ds(pl.multiple_of(low, 128), length)
            query = q_ref[here, :] * jnp.asarray(0.125, LOW)
            same = col[there, :] == row[0:1, here]
            tops = []
            for head in range(2):
                own = jnp.where((lane < 64) == (head == 0), query, jnp.zeros_like(query))
                value = jnp.where(same, dot(k_ref[there, :], own, ACROSS), -1e30)
                logits[head, 0:length, :] = value
                top = jnp.max(value.reshape(-1, 8, tile), 0)
                tops.append(jnp.max(top, 0, keepdims=True))
            sums = []
            for head in range(2):
                term = jnp.exp(logits[head, 0:length, :] - tops[head])
                sums.append(jnp.sum(term.reshape(-1, 8, tile), 0))
                probs[head, 0:length, :] = term.astype(LOW)
            parts = []
            for head in range(2):
                total = jnp.sum(sums[head], 0, keepdims=True)
                values = flipped[64 * head : 64 * head + 64, there]
                parts.append(dot(values, probs[head, 0:length, :]) / total)
                total_ref[0, head : head + 1, here] = tops[head] + jnp.log(total)
            out_ref[here, :] = jnp.concatenate(parts, 0).T.astype(LOW)

        for number, length in enumerate(lengths):
            pl.when(kind == number)(functools.partial(attend, length))
        return carry

    lax.fori_loop(0, q_ref.shape[0] // tile, block, 0)


def head_pair(count, row, first):
    return pl.BlockSpec((count, 128), lambda h, s: (row, first + h))


def attend_lengths(count):
    return [length for length in (128, 256, 384, 512, 640, 768, 1024) if count < 256 or length > 128][
        : 1 if count < 256 else None
    ]


def attend_call(kernel, tile, count, pairs, tables, arrays, specs, outputs, into, scratch, cost):
    spans, col, row = tables
    specs = specs + [
        pl.BlockSpec((count, tile), lambda h, s: (0, 0)),
        pl.BlockSpec((8, count), lambda h, s: (0, 0)),
    ]
    arguments = [spans, *arrays, col, row]
    aliases = {}
    used = len(arguments)
    if into is not None:
        aliases = {used + i: i for i in range(len(into))}
        specs = specs + [pl.BlockSpec(memory_space=pl.ANY)] * len(into)
        arguments += list(into)

    def run(*refs):
        kernel(tile, attend_lengths(count), *refs[:used], *refs[len(arguments) :])

    return pl.pallas_call(
        run,
        out_shape=[shape for shape, _ in outputs],
        grid_spec=pltpu.PrefetchScalarGridSpec(
            num_scalar_prefetch=1,
            grid=(pairs,),
            in_specs=specs,
            out_specs=[spec for _, spec in outputs],
            scratch_shapes=scratch,
        ),
        input_output_aliases=aliases,
        compiler_params=pltpu.CompilerParams(vmem_limit_bytes=48 << 20),
        cost_estimate=pl.CostEstimate(
            flops=cost * pairs * count * count * 128,
            transcendentals=0,
            bytes_accessed=8 * pairs * count * 128,
        ),
    )(*arguments)


def attend_forward(mixed, tables, tile, first, pairs, row, into=None):
    count = mixed.shape[0]
    return attend_call(
        attend_kernel,
        tile,
        count,
        pairs,
        tables,
        [mixed] * 3,
        [head_pair(count, 0, third * 6 + first) for third in range(3)],
        [
            (jax.ShapeDtypeStruct((TOKENS, D), LOW), head_pair(count, row, first)),
            (
                jax.ShapeDtypeStruct((6, 8, count), F32),
                pl.BlockSpec((1, 8, count), lambda h, s: (first + h, 0, 0)),
            ),
        ],
        into,
        [
            pltpu.VMEM((2, count, tile), F32),
            pltpu.VMEM((2, count, tile), LOW),
            pltpu.VMEM((128, count), LOW),
        ],
        40,
    )


def attend_back_kernel(
    tile, lengths, spans, q_ref, k_ref, v_ref, g_ref, total_ref, col, row,
    grad_ref, sum_ref, flipped, gkey, gvalue, probs, gprobs, low_probs, low_deltas,
):
    flipped[...] = k_ref[...].T
    gkey[...] = jnp.zeros_like(gkey)
    gvalue[...] = jnp.zeros_like(gvalue)
    sum_ref[...] = jnp.zeros_like(sum_ref)
    lane = lax.broadcasted_iota(jnp.int32, (tile, 128), 1)

    def block(index, carry):
        here = pl.ds(pl.multiple_of(index * tile, tile), tile)
        low, kind = spans[index, 0], spans[index, 1]

        def attend(length):
            there = pl.ds(pl.multiple_of(low, 128), length)
            query, grad = q_ref[here, :] * jnp.asarray(0.125, LOW), g_ref[here, :]
            zero = jnp.zeros_like(query)
            same = col[there, :] == row[0:1, here]
            own = [(lane < 64) == (head == 0) for head in range(2)]
            queries = [jnp.where(mine, query, zero) for mine in own]
            grads = [jnp.where(mine, grad, zero) for mine in own]
            dots = []
            for head in range(2):
                prob = dot(k_ref[there, :], queries[head], ACROSS)
                prob = jnp.exp(prob - total_ref[0, head : head + 1, here])
                prob = jnp.where(same, prob, 0.0)
                gprob = dot(v_ref[there, :], grads[head], ACROSS)
                total = jnp.sum((prob * gprob).reshape(-1, 8, tile), 0)
                dots.append(jnp.sum(total, 0, keepdims=True))
                probs[head, 0:length, :] = prob
                gprobs[head, 0:length, :] = gprob
                low_probs[head, 0:length, :] = prob.astype(LOW)

            def both(terms, right):
                return dot(terms[0, 0:length, :], right[0]) + dot(terms[1, 0:length, :], right[1])

            gvalue[there, :] += both(low_probs, grads)
            for head in range(2):
                delta = gprobs[head, 0:length, :] - dots[head]
                low_deltas[head, 0:length, :] = (probs[head, 0:length, :] * delta).astype(LOW)
            gkey[there, :] += both(low_deltas, queries)
            parts = []
            for head in range(2):
                keys = flipped[64 * head : 64 * head + 64, there]
                parts.append(dot(keys, low_deltas[head, 0:length, :]))
            whole = jnp.concatenate(parts, 0).T * 0.125
            grad_ref[0, here, :] = whole.astype(LOW)
            sum_ref[0:1, :] += jnp.sum(whole, 0, keepdims=True)

        for number, length in enumerate(lengths):
            pl.when(kind == number)(functools.partial(attend, length))
        return carry

    lax.fori_loop(0, q_ref.shape[0] // tile, block, 0)
    grad_ref[1] = gkey[...].astype(LOW)
    grad_ref[2] = gvalue[...].astype(LOW)
    sum_ref[1:2, :] = jnp.sum(gvalue[...], 0, keepdims=True)


def attend_backward(mixed, grad, total, tables, tile, first, pairs, row, into=None):
    count = mixed.shape[0]
    return attend_call(
        attend_back_kernel,
        tile,
        count,
        pairs,
        tables,
        [mixed] * 3 + [grad, total],
        [head_pair(count, 0, third * 6 + first) for third in range(3)]
        + [
            head_pair(count, row, first),
            pl.BlockSpec((1, 8, count), lambda h, s: (first + h, 0, 0)),
        ],
        [
            (
                jax.ShapeDtypeStruct((3, TOKENS, D), LOW),
                pl.BlockSpec((3, count, 128), lambda h, s: (0, row, first + h)),
            ),
            (
                jax.ShapeDtypeStruct((16, D), F32),
                pl.BlockSpec((16, 128), lambda h, s: (0, first + h)),
            ),
        ],
        into,
        [
            pltpu.VMEM((128, count), LOW),
            pltpu.VMEM((count, 128), F32),
            pltpu.VMEM((count, 128), F32),
            pltpu.VMEM((2, count, tile), F32),
            pltpu.VMEM((2, count, tile), F32),
            pltpu.VMEM((2, count, tile), LOW),
            pltpu.VMEM((2, count, tile), LOW),
        ],
        80,
    )


def segment_tables(segment, tile):
    count = segment.shape[0]
    lengths = jnp.asarray(attend_lengths(count), jnp.int32)
    ends = segment.reshape(count // tile, tile)
    first = jnp.sum((segment[None, :] < ends[:, :1]).astype(jnp.int32), 1) // 128 * 128
    last = jnp.sum((segment[None, :] <= ends[:, -1:]).astype(jnp.int32), 1)
    kind = jnp.sum((lengths[None, :] < (last - first)[:, None]).astype(jnp.int32), 1)
    chosen = jnp.arange(lengths.shape[0], dtype=jnp.int32)[None, :] == kind[:, None]
    keys = jnp.sum(jnp.where(chosen, lengths[None, :], 0), 1)
    return (
        jnp.stack([jnp.minimum(first, count - keys), kind], 1),
        jnp.broadcast_to(segment[:, None], (count, tile)),
        jnp.broadcast_to(segment[None, :], (8, count)),
    )


def two_terms(value):
    high = value.astype(LOW)
    return high, (value - high.astype(F32)).astype(LOW)


def sharp(cosine):
    return jnp.exp2(cosine * 14.426950408889634 - 14.426950408889634)


def score_kernel(query_ref, passage_ref, member_ref, score_ref, sums_ref):
    terms = sharp(dot(query_ref[...], passage_ref[...], ACROSS)).astype(LOW)
    sums = dot(terms, member_ref[...])
    sums_ref[...] = sums
    lane = lax.broadcasted_iota(jnp.int32, sums.shape, 1)
    soft = jnp.where(lane < PPB, 0.1 * jnp.log(jnp.where(lane < PPB, sums, 1.0)) + 1.0, 0.0)
    score_ref[...] = jnp.sum(soft.reshape(-1, QLEN, 128), 1)


def score_ratio(grad_ref, sums_ref):
    rows = sums_ref.shape[0]
    lane = lax.broadcasted_iota(jnp.int32, (rows, 128), 1)
    grads = jnp.broadcast_to(grad_ref[...][:, None, :], (rows // QLEN, QLEN, 128))
    ratio = grads.reshape(rows, 128) / jnp.where(lane % 64 < PPB, sums_ref[...], 1.0)
    high, rest = two_terms(ratio)
    return jnp.where(lane < 64, high, rest)


def score_query_kernel(query_ref, passage_ref, member_ref, grad_ref, sums_ref, out_ref):
    ratio = score_ratio(grad_ref, sums_ref)
    terms = sharp(dot(query_ref[...], passage_ref[...], ACROSS))
    terms = (terms * dot(ratio, member_ref[...], ACROSS)).astype(LOW)
    out_ref[...] = dot(terms, passage_ref[...])


def score_passage_kernel(query_ref, passage_ref, member_ref, grad_ref, sums_ref, out_ref):
    @pl.when(pl.program_id(0) == 0)
    def _():
        out_ref[...] = jnp.zeros_like(out_ref)

    ratio = score_ratio(grad_ref, sums_ref)
    terms = sharp(dot(passage_ref[...], query_ref[...], ACROSS))
    terms = (terms * dot(member_ref[...], ratio, ACROSS)).astype(LOW)
    out_ref[...] += dot(terms, query_ref[...])


SCORE_ROWS = 512


def score_call(kernel, inputs, in_specs, out_specs, out_shape, flops):
    return pl.pallas_call(
        kernel,
        grid=(inputs[0].shape[0] // SCORE_ROWS,),
        in_specs=in_specs,
        out_specs=out_specs,
        out_shape=out_shape,
        compiler_params=pltpu.CompilerParams(vmem_limit_bytes=40 << 20),
        cost_estimate=pl.CostEstimate(
            flops=flops,
            transcendentals=inputs[0].shape[0] * BIN,
            bytes_accessed=inputs[0].shape[0] * 1024,
        ),
    )(*inputs)


def score_specs():
    rows = SCORE_ROWS
    fixed = pl.BlockSpec((BIN, 128), lambda i: (0, 0))
    return (
        pl.BlockSpec((rows, 128), lambda i: (i, 0)),
        fixed,
        pl.BlockSpec((rows // QLEN, 128), lambda i: (i, 0)),
    )


def score_forward(queries, passages, member):
    rows, fixed, grads = score_specs()
    count = queries.shape[0]
    return score_call(
        score_kernel,
        (queries, passages, member),
        [rows, fixed, fixed],
        [grads, rows],
        [
            jax.ShapeDtypeStruct((count // QLEN, 128), F32),
            jax.ShapeDtypeStruct((count, 128), F32),
        ],
        6 * count * BIN * 128,
    )


def score_backward(kernel, queries, passages, member, grad_scores, sums):
    rows, fixed, grads = score_specs()
    count = queries.shape[0]
    inputs = (queries, passages, member, grad_scores, sums)
    in_specs = [rows, fixed, fixed, grads, rows]
    width, spec = (BIN, fixed) if kernel is score_passage_kernel else (count, rows)
    out = jax.ShapeDtypeStruct((width, 128), F32)
    return score_call(kernel, inputs, in_specs, spec, out, 6 * count * BIN * 128)


def cross_grad(scores, partition, passage_ids, chosen_ids, query_total):
    onehot = (passage_ids[None, :] == chosen_ids[:, None]).astype(jnp.float32)
    return (jnp.exp(scores) / partition[:, None] - onehot) / query_total


def adam_update(weight, moment_one, moment_two, gradient, factor, rate):
    clipped = gradient * factor
    new_one = beta_one * moment_one + (1.0 - beta_one) * clipped
    new_two = beta_two * moment_two + (1.0 - beta_two) * clipped * clipped
    direction = (
        new_one / (1.0 - beta_one**STEP) / (jnp.sqrt(new_two / (1.0 - beta_two**STEP)) + adam_eps)
    )
    return (weight - rate * (direction + decay_rate * weight), new_one, new_two)


def body(
    query_tokens,
    passage_tokens,
    passage_lengths,
    positives,
    qkv_weight,
    qkv_first,
    qkv_second,
    out_weight,
    out_first,
    out_second,
    up_weight,
    up_first,
    up_second,
    down_weight,
    down_first,
    down_second,
    proj_weight,
    proj_first,
    proj_second,
    vector_params,
    vector_first,
    vector_second,
):
    own_index = lax.axis_index(("pb", "pa"))
    query_total = QPD * lax.axis_size(("pb", "pa"))
    query_flat = query_tokens.reshape(QUERY_ROWS, D)
    tokens = jnp.concatenate([passage_tokens[0], query_flat], 0)
    query_tables = segment_tables(jnp.arange(QUERY_ROWS, dtype=jnp.int32) // QLEN, QUERY_ROWS)
    own_lengths = lax.dynamic_index_in_dim(passage_lengths, own_index, 0, keepdims=False)
    ends = jnp.cumsum(own_lengths)
    places = jnp.arange(BIN, dtype=jnp.int32)
    own_seg = jnp.sum((places[:, None] >= ends[None, :]).astype(jnp.int32), 1)
    passage_tables = segment_tables(own_seg, ATTEND_TILE)
    member = (own_seg[:, None] == jnp.arange(128, dtype=jnp.int32)[None, :] % 64).astype(LOW)

    vector_part = jnp.pad(vector_params.T, ((0, 0), (0, 116))).astype(LOW)
    first_part = jnp.concatenate([qkv_weight.astype(LOW), vector_part], 1)
    middle_part = jnp.concatenate([up_weight, out_weight, proj_weight], 1).astype(LOW)
    down_part = down_weight.astype(LOW)
    first_line = line_of(first_part, send_line(first_part))
    middle_moved = send_line(gate(middle_part, first_line))
    first_pair = gather_pair(first_line)
    turned = transposed(tokens)
    ready = gate((tokens, turned, query_tables, passage_tables, member), first_pair)
    first_quad = gather_quad(first_pair, ready)
    tokens, turned, query_tables, passage_tables, member = ready
    middle = gather_rest(line_of(middle_part, gate(middle_moved, first_quad)))
    qkv_matrix, vectors = gather_whole(first_quad, [(0, 2304), (2304, 2432)])
    vectors = vectors[:, :12].T.astype(F32)
    bias_qkv = jnp.concatenate([vectors[0], jnp.zeros_like(vectors[0]), vectors[1]])

    def mix(rows):
        return (dot(rows, qkv_matrix) + bias_qkv).astype(LOW)

    query_mixed = mix(query_flat)
    down_moved = send_line(gate(down_part, query_mixed))
    passage_mixed = mix(gate(passage_tokens[0], query_mixed))
    attended, query_log = attend_forward(
        gate(query_mixed, passage_mixed), query_tables, QUERY_ROWS, 0, 6, BIN // QUERY_ROWS
    )
    down_line = line_of(down_part, gate(down_moved, attended))
    passage_state = attend_forward(
        gate(passage_mixed, down_line), passage_tables, ATTEND_TILE, 0, 3, 0, (attended,)
    )
    down_pair = gather_pair(down_line, passage_state)
    attended, passage_log = attend_forward(
        gate(passage_mixed, down_pair), passage_tables, ATTEND_TILE, 3, 3, 0, passage_state
    )
    down_quad = gather_quad(down_pair, attended)
    up = columns(middle, 0, 4 * D)
    out = columns(middle, 4 * D, 5 * D)
    proj = columns(middle, 5 * D, 5 * D + 128)
    vector_rows = columns(vectors)

    def widen(rows, first, count, att, into):
        return row_call(
            widen_kernel,
            rows,
            first,
            count,
            [(tokens, first), (att, first)],
            (out, up, vector_rows),
            [(D, F32), (D, LOW), (4 * D, LOW), (4 * D, LOW)],
            into=into,
            flops=10 * D * D,
        )

    def narrow(rows, first, count, wider, into):
        return row_call(
            narrow_kernel,
            rows,
            first,
            count,
            [(wider[2], first), (wider[0], first)],
            (down, proj, vector_rows),
            [(D, F32), (D, LOW), (128, F32), (128, LOW)],
            into=into,
            flops=8 * D * D,
        )

    wider = widen(QUERY_ROWS, BIN // QUERY_ROWS, 1, gate(attended, down_quad), None)
    (down_matrix,) = gather_whole(down_quad, [(0, D)], wider)
    down = columns(down_matrix)
    narrower = narrow(QUERY_ROWS, BIN // QUERY_ROWS, 1, wider, None)
    query_part = narrower[3][BIN:]
    query_line = line_of(query_part, send_line(query_part))
    every_query = gather_rest(query_line)
    wider = widen(
        FEED_ROWS, 0, BIN // FEED_ROWS, gate(attended, query_line), gate(wider, narrower)
    )
    narrower = narrow(FEED_ROWS, 0, BIN // FEED_ROWS, wider, narrower)
    resid, normed, active, slope = wider
    two, normed_out, projected, unit = narrower
    passage_unit = unit[:BIN]

    passage_ids = own_index * PPB + jnp.arange(PPB, dtype=jnp.int32)
    scores, totals = score_forward(every_query, passage_unit, member)
    scores = scores[:, :PPB]
    partition = sum_everywhere(jnp.sum(jnp.exp(scores), 1))
    grad_scores = cross_grad(scores, partition, passage_ids, positives, query_total)
    grad_scores = jnp.tile(jnp.pad(grad_scores, ((0, 0), (0, 64 - PPB))), (1, 2))
    grad_every = score_backward(
        score_query_kernel, every_query, passage_unit, member, grad_scores, totals
    )
    whole, rounded = (True,), (False,)
    query_back = scatter_quad([grad_every], scatter_sends([grad_every], whole))
    grad_passage = score_backward(
        score_passage_kernel,
        gate(every_query, query_back),
        passage_unit,
        member,
        grad_scores,
        totals,
    )

    def go_back(rows, first, count, grad, into):
        return row_call(
            back_kernel,
            rows,
            first,
            count,
            [grad, (projected, first), (two, first), (slope, first), (resid, first)],
            (proj, down, up, out, vector_rows),
            [(128, LOW), (D, LOW), (4 * D, LOW), (D, LOW), (D, LOW)],
            (D,),
            into=into,
            flops=18 * D * D,
        )

    query_back = scatter_pair(query_back, whole)
    back = go_back(
        BACK_ROWS, 0, BIN // BACK_ROWS, (gate(grad_passage, query_back), 0), None
    )
    query_back = scatter_line(query_back, whole)
    (grad_query,) = scatter_total(gate(query_back, back), whole)
    back = go_back(QUERY_ROWS, BIN // QUERY_ROWS, 1, (grad_query, 0), back)
    gproj, gtwo, ghid, gone, gatt, sums = back

    def terms(left, right):
        return dot(left, right, (((0,), (0,)), ((), ())))

    def attend_back(first, pairs, into, *others):
        mixed = gate(passage_mixed, *others)
        return attend_backward(
            mixed, gatt, passage_log, passage_tables, ATTEND_TILE, first, pairs, 0, into
        )

    down_terms = terms(active, gtwo)
    down_sends = scatter_sends([down_terms], rounded)
    up_terms = terms(normed, gate(ghid, down_sends))
    down_back = scatter_quad([down_terms], down_sends, up_terms)
    down_pair = scatter_pair(down_back, rounded)
    rest = gate((gone, gproj), down_back)
    out_terms, proj_terms = terms(attended, rest[0]), terms(rest[1], normed_out).T
    kinds = (False, False, True)
    middle_terms = [up_terms, out_terms, proj_terms]
    middle_sends = scatter_sends(middle_terms, kinds)
    query_grads = attend_backward(
        gate(query_mixed, middle_sends),
        gatt,
        query_log,
        query_tables,
        QUERY_ROWS,
        0,
        6,
        BIN // QUERY_ROWS,
    )
    middle_back = scatter_quad(middle_terms, middle_sends, query_grads)
    middle_pair = scatter_pair(middle_back, kinds)
    down_line = scatter_line(down_pair, rounded)
    grads = attend_back(0, 2, query_grads[:1], query_grads, down_pair, middle_back)
    (down_sum,) = scatter_total(gate(down_line, grads), rounded)
    grads = attend_back(2, 2, grads, down_line)
    middle_line = scatter_line(gate(middle_pair, grads), kinds)
    grads = attend_back(4, 2, grads, middle_pair, down_sum)
    up_sum, out_sum, proj_sum = scatter_total(middle_line, kinds)
    mixed_grads = gate(grads[0], middle_line)
    first_terms = [dot(turned, mixed_grads[third]) for third in range(3)]
    mixed_sums = grads[1] + query_grads[1]
    vector_grad = jnp.concatenate([mixed_sums[:2], sums[2:12]], 0)
    vector_terms = jnp.pad(vector_grad.T, ((0, 0), (0, 116)))
    kinds = (False,) * 4
    first_terms.append(vector_terms)
    first_back = scatter_quad(first_terms, scatter_sends(first_terms, kinds))
    first_back = scatter_pair(first_back, kinds, up_sum)
    *thirds, vector_sum = scatter_total(scatter_line(first_back, kinds), kinds)
    qkv_sum = jnp.concatenate(thirds, 1)
    reduced = (qkv_sum, out_sum, up_sum, down_sum, proj_sum, vector_sum[:, :12].T)
    square = sum((jnp.sum(gradient * gradient) for gradient in reduced))
    norm_value = jnp.sqrt(sum_everywhere(jnp.full((1, 128), square))[0, 0])
    factor = jnp.minimum(1.0, clip_max / (norm_value + 1e-06))
    qkv_res = adam_update(qkv_weight, qkv_first, qkv_second, reduced[0], factor, learn_rate)
    out_res = adam_update(out_weight, out_first, out_second, reduced[1], factor, learn_rate)
    up_res = adam_update(up_weight, up_first, up_second, reduced[2], factor, learn_rate)
    down_res = adam_update(down_weight, down_first, down_second, reduced[3], factor, learn_rate)
    proj_res = adam_update(proj_weight, proj_first, proj_second, reduced[4], factor, learn_rate)
    vector_res = adam_update(
        vector_params, vector_first, vector_second, reduced[5], factor, vector_rate
    )
    return (
        norm_value,
        qkv_res[0],
        qkv_res[1],
        qkv_res[2],
        out_res[0],
        out_res[1],
        out_res[2],
        up_res[0],
        up_res[1],
        up_res[2],
        down_res[0],
        down_res[1],
        down_res[2],
        proj_res[0],
        proj_res[1],
        proj_res[2],
        vector_res[0],
        vector_res[1],
        vector_res[2],
    )


def solution(mesh):
    placed = (
        P(("pb", "pa"), None, None),
        P(("pb", "pa"), None, None),
        P(),
        P(),
        P(("pb", "pa"), None),
        P(("pb", "pa"), None),
        P(("pb", "pa"), None),
        P(("pb", "pa"), None),
        P(("pb", "pa"), None),
        P(("pb", "pa"), None),
        P(("pb", "pa"), None),
        P(("pb", "pa"), None),
        P(("pb", "pa"), None),
        P(("pb", "pa"), None),
        P(("pb", "pa"), None),
        P(("pb", "pa"), None),
        P(("pb", "pa"), None),
        P(("pb", "pa"), None),
        P(("pb", "pa"), None),
        P(None, ("pb", "pa")),
        P(None, ("pb", "pa")),
        P(None, ("pb", "pa")),
    )
    return jax.shard_map(
        body,
        mesh=mesh,
        in_specs=placed,
        out_specs=(
            P(),
            P(("pb", "pa"), None),
            P(("pb", "pa"), None),
            P(("pb", "pa"), None),
            P(("pb", "pa"), None),
            P(("pb", "pa"), None),
            P(("pb", "pa"), None),
            P(("pb", "pa"), None),
            P(("pb", "pa"), None),
            P(("pb", "pa"), None),
            P(("pb", "pa"), None),
            P(("pb", "pa"), None),
            P(("pb", "pa"), None),
            P(("pb", "pa"), None),
            P(("pb", "pa"), None),
            P(("pb", "pa"), None),
            P(None, ("pb", "pa")),
            P(None, ("pb", "pa")),
            P(None, ("pb", "pa")),
        ),
        check_vma=False,
    )
```

```python
import functools

import jax
import jax.numpy as jnp
import numpy as np
from jax import lax
from jax.experimental import pallas as pl
from jax.experimental.pallas import tpu as pltpu
from jax.sharding import PartitionSpec as P

D = 768
HEAD_DIM = 64
QLEN = 32
BIN = 1024
PPB = 8
STEP = 10
QPD = 4
QUERY_ROWS = QPD * QLEN
TOKENS = BIN + QUERY_ROWS
ATTEND_TILE = 256
FEED_ROWS = 256
BACK_ROWS = 256


F32 = jnp.float32
LOW = jnp.bfloat16
sharpness_divisor = 0.1
clip_max = 0.02
learn_rate = 0.04
vector_rate = 0.4
beta_one = 0.9
beta_two = 0.999
adam_eps = 1e-08
decay_rate = 0.01
norm_eps = 1e-12


def shift_pairs(amount):
    return [(i, (i + amount) % 4) for i in range(4)]


FIRST_STEP = [(i, i ^ 2 if i % 2 == 0 else i ^ 4) for i in range(8)]
SECOND_STEP = [(i, i ^ 4 if i % 2 == 0 else i ^ 2) for i in range(8)]
CORE_PAIR = [(i, i ^ 1) for i in range(8)]


def staged_mesh():
    return lax.axis_size("pb") == 8 and lax.axis_size("pa") == 4


def position():
    row = lax.axis_index("pb")
    core, x_bit, y_bit = row % 2, (row // 2) % 2, row // 4
    return (
        lax.axis_index("pa"),
        core,
        jnp.where(core == 0, x_bit, y_bit),
        jnp.where(core == 0, y_bit, x_bit),
    )


def gate(value, *others):
    return lax.optimization_barrier((value, others))[0]


def place_blocks(sources, copies, outputs, index):
    def run(scalars, *refs):
        given, (results, sems) = refs[: len(sources)], (refs[len(sources) : -1], refs[-1])
        moves = [
            pltpu.make_async_copy(
                given[source].at[where(scalars)], results[out].at[there(scalars)], sems.at[number]
            )
            for number, (source, where, out, there) in enumerate(copies)
        ]
        for move in moves:
            move.start()
        for move in moves:
            move.wait()

    anywhere = pl.BlockSpec(memory_space=pl.ANY)
    return pl.pallas_call(
        run,
        grid_spec=pltpu.PrefetchScalarGridSpec(
            num_scalar_prefetch=1,
            grid=(),
            in_specs=[anywhere] * len(sources),
            out_specs=[anywhere] * len(outputs),
            scratch_shapes=[pltpu.SemaphoreType.DMA((len(copies),))],
        ),
        out_shape=outputs,
        compiler_params=pltpu.CompilerParams(vmem_limit_bytes=4 << 20),
        cost_estimate=pl.CostEstimate(
            flops=0,
            transcendentals=0,
            bytes_accessed=2 * sum(o.size * o.dtype.itemsize for o in outputs),
        ),
    )(index, *sources)


def scalars_of_position():
    return jnp.stack([jnp.asarray(v, jnp.int32) for v in position()])


def send_line(part):
    if not staged_mesh():
        return [lax.all_gather(part, "pa", axis=0, tiled=True)]
    return [lax.ppermute(part, "pa", shift_pairs(k)) for k in (1, 2, 3)]


def line_of(part, moved):
    if not staged_mesh():
        return moved[0]
    depth = position()[0]
    around = [part, moved[2], moved[1], moved[0]]
    line = jnp.stack([lax.select_n((place - depth) % 4, *around) for place in range(4)])
    return line.reshape((4 * part.shape[0],) + part.shape[1:])


def gather_rest(line):
    return lax.all_gather(line, "pb", axis=0, tiled=True)


def in_order(own, other, which):
    both = jax.ShapeDtypeStruct((2,) + own.shape, own.dtype)
    copies = [
        (0, lambda s: Ellipsis, 0, lambda s: s[which]),
        (1, lambda s: Ellipsis, 0, lambda s: 1 - s[which]),
    ]
    return place_blocks([own, other], copies, [both], scalars_of_position())[0]


def gather_pair(line, *others):
    if not staged_mesh():
        return line
    return in_order(line, gate(lax.ppermute(line, "pb", FIRST_STEP), others), 2)


def gather_quad(pair, *others):
    if not staged_mesh():
        return pair
    return in_order(pair, gate(lax.ppermute(pair, "pb", SECOND_STEP), others), 3)


def gather_whole(quad, ranges, *others):
    if not staged_mesh():
        whole = gather_rest(quad)
        return [whole[:, low:high] for low, high in ranges]
    partner = gate(lax.ppermute(quad, "pb", CORE_PAIR), others)
    rows = quad.shape[2]
    copies, outputs = [], []
    for number, (low, high) in enumerate(ranges):
        outputs.append(jax.ShapeDtypeStruct((8, rows, high - low), quad.dtype))
        for source in range(2):
            for second in range(2):
                for first in range(2):

                    def where(s, second=second, first=first, low=low, high=high):
                        return second, first, slice(None), slice(low, high)

                    def there(s, source=source, second=second, first=first):
                        core = s[1] if source == 0 else 1 - s[1]
                        swapped = 4 * first + 2 * second
                        return core + jnp.where(core == 0, 4 * second + 2 * first, swapped)

                    copies.append((source, where, number, there))
    results = place_blocks([quad, partner], copies, outputs, scalars_of_position())
    return [a.reshape(8 * rows, a.shape[2]) for a in results]


def split_low(value):
    high = lax.reduce_precision(value, 8, 7)
    return high.astype(LOW), (value - high).astype(LOW)


def packed(arrays, exact):
    pieces = []
    for array, whole in zip(arrays, exact):
        pieces += split_low(array) if whole else [array.astype(LOW)]
    return pieces[0] if len(pieces) == 1 else jnp.concatenate(pieces, -1)


def joined(arrays, exact, moved):
    results, at = [], 0
    for array, whole in zip(arrays, exact):
        total = array.astype(F32)
        for _ in range(2 if whole else 1):
            total = total + moved[..., at : at + array.shape[-1]].astype(F32)
            at += array.shape[-1]
        results.append(total)
    return results


def blocks_at(arrays, place):
    return [lax.dynamic_index_in_dim(array, place, 0, False) for array in arrays]


def core_blocks(array, other):
    core = position()[1]
    parts = array.reshape((4, 2, array.shape[0] // 8) + array.shape[1:])
    return lax.dynamic_index_in_dim(parts, 1 - core if other else core, 1, False)


def scatter_sends(arrays, exact):
    if not staged_mesh():
        return arrays
    sends = [core_blocks(array, True) for array in arrays]
    return [a if whole else a.astype(LOW) for a, whole in zip(sends, exact)]


def scatter_quad(arrays, sends, *others):
    if not staged_mesh():
        return [
            lax.psum_scatter(a.astype(F32), "pb", scatter_dimension=0, tiled=True)
            for a in arrays
        ]
    moved = gate([lax.ppermute(a, "pb", CORE_PAIR) for a in sends], others)
    return [
        core_blocks(array, False).astype(F32) + m.astype(F32) for array, m in zip(arrays, moved)
    ]


def chip_pairs(arrays, bit):
    core = position()[1]
    first = jnp.where(core == 0, 2 * bit, bit)
    second = first + jnp.where(core == 0, 1, 2)
    return [
        jnp.stack([lax.dynamic_index_in_dim(a, i, 0, False) for i in (first, second)])
        for a in arrays
    ]


def pair_send(arrays, exact):
    if not staged_mesh():
        return arrays
    return packed(chip_pairs(arrays, 1 - position()[3]), exact)


def scatter_pair(arrays, send, exact, *others):
    if not staged_mesh():
        return arrays
    moved = gate(lax.ppermute(send, "pb", SECOND_STEP), others)
    return joined(chip_pairs(arrays, position()[3]), exact, moved)


def scatter_line(arrays, exact):
    if not staged_mesh():
        return arrays
    bit = position()[2]
    send = packed(blocks_at(arrays, 1 - bit), exact)
    return joined(blocks_at(arrays, bit), exact, lax.ppermute(send, "pb", FIRST_STEP))


def scatter_rest(arrays):
    return [lax.psum_scatter(a, "pa", scatter_dimension=0, tiled=True) for a in arrays]


def last_moves(arrays, exact):
    depth = position()[0]
    sends = [packed(blocks_at(arrays, (depth + k) % 4), exact) for k in (1, 2, 3)]
    return [lax.ppermute(s, "pa", shift_pairs(k + 1)) for k, s in enumerate(sends)]


def depth_blocks(arrays):
    return [a.reshape((4, a.shape[0] // 4) + a.shape[1:]) for a in arrays]


def scatter_total(arrays, exact):
    if not staged_mesh():
        return scatter_rest(arrays)
    arrays = depth_blocks(arrays)
    total = blocks_at(arrays, position()[0])
    for moved in last_moves(arrays, exact):
        total = joined(total, exact, moved)
    return total


def sum_everywhere(value):
    count = lax.axis_size(("pb", "pa"))
    copies = jnp.broadcast_to(value[None], (count,) + value.shape)
    return jnp.sum(lax.all_to_all(copies, ("pb", "pa"), 0, 0), 0)


ACROSS = (((1,), (1,)), ((), ()))
PLAIN = (((1,), (0,)), ((), ()))


def dot(left, right, dims=PLAIN):
    return lax.dot_general(left, right, dims, preferred_element_type=F32)


def standard(hidden):
    centred = hidden - jnp.mean(hidden, -1, keepdims=True)
    spread = jnp.mean(centred * centred, -1, keepdims=True)
    scale = lax.rsqrt(spread + norm_eps)
    return centred * scale, scale


def standard_backward(grad, unit, scale):
    return scale * (
        grad
        - jnp.mean(grad, -1, keepdims=True)
        - unit * jnp.mean(grad * unit, -1, keepdims=True)
    )


def gelu_with_slope(value):
    below = 0.5 + 0.5 * lax.erf(value * 0.7071067811865476)
    bell = jnp.exp2(value * (value * -0.7213475204444817))
    return value * below, below + value * (0.3989422804014327 * bell)


def columns(array, low=0, high=None):
    width = array.shape[1] - low if high is None else high - low
    spec = pl.BlockSpec(
        (array.shape[0], width), lambda i: (0, low // width), pipeline_mode=pl.Buffered(1)
    )
    return array, spec


def transposed(array):
    rows, width = array.shape
    return pl.pallas_call(
        lambda x_ref, out_ref: out_ref.__setitem__(Ellipsis, x_ref[...].T),
        grid=(width // 128,),
        in_specs=[pl.BlockSpec((rows, 128), lambda i: (0, i))],
        out_specs=pl.BlockSpec((128, rows), lambda i: (i, 0)),
        out_shape=jax.ShapeDtypeStruct((width, rows), array.dtype),
    )(array)


def row_call(kernel, rows, first, count, inputs, weights, outputs, sums=(), into=None, flops=0):
    done = 0 if into is None else len(inputs) + len(weights)

    def run(*refs):
        given, results = refs[: len(inputs) + len(weights)], refs[-len(outputs) - len(sums) :]
        if sums:

            @pl.when(pl.program_id(0) == 0)
            def _():
                for place in range(len(sums)):
                    place -= len(sums)
                    start = refs[place - len(outputs) - len(sums)] if done else None
                    here = results[place]
                    here[...] = start[...] if done else jnp.zeros_like(here)

        kernel(*given, *results)

    moved = rows * count * sum(a.shape[1] * a.dtype.itemsize for a, _ in inputs)
    moved += sum(w.size * w.dtype.itemsize for w, _ in weights)
    moved += rows * count * sum(w * jnp.dtype(t).itemsize for w, t in outputs)

    def rows_at(width, begin):
        return pl.BlockSpec((rows, width), lambda i: (begin + i, 0))

    sum_specs = [pl.BlockSpec((16, w), lambda i: (0, 0)) for w in sums]
    in_specs = [rows_at(a.shape[1], begin) for a, begin in inputs]
    in_specs += [spec for _, spec in weights]
    arguments = [a for a, _ in inputs] + [w for w, _ in weights]
    if into is not None:
        in_specs += [pl.BlockSpec(memory_space=pl.ANY)] * len(outputs) + sum_specs
        arguments += list(into)
    return pl.pallas_call(
        run,
        grid=(count,),
        in_specs=in_specs,
        out_specs=[rows_at(w, first) for w, _ in outputs] + sum_specs,
        out_shape=[jax.ShapeDtypeStruct((TOKENS, w), t) for w, t in outputs]
        + [jax.ShapeDtypeStruct((16, w), F32) for w in sums],
        input_output_aliases={done + i: i for i in range(len(outputs) + len(sums))} if done else {},
        compiler_params=pltpu.CompilerParams(vmem_limit_bytes=56 << 20),
        cost_estimate=pl.CostEstimate(
            flops=flops * rows * count, transcendentals=0, bytes_accessed=moved
        ),
    )(*arguments)


def widen_kernel(x_ref, att_ref, out_w, up_w, vec, resid_ref, low_ref, act_ref, slope_ref):
    resid = x_ref[...].astype(F32) + dot(att_ref[...], out_w[...]) + vec[2:3]
    resid_ref[...] = resid
    low = (standard(resid)[0] * vec[3:4] + vec[4:5]).astype(LOW)
    low_ref[...] = low
    for row in range(4):
        part = slice(row * D, row * D + D)
        value, slope = gelu_with_slope(dot(low, up_w[:, part]) + vec[5 + row : 6 + row])
        act_ref[:, part] = value.astype(LOW)
        slope_ref[:, part] = slope.astype(LOW)


def narrow_kernel(act_ref, resid_ref, down_w, proj_w, vec, two_ref, low_ref, proj_ref, unit_ref):
    normed = standard(resid_ref[...])[0] * vec[3:4] + vec[4:5]
    two = normed + dot(act_ref[...], down_w[...]) + vec[9:10]
    two_ref[...] = two
    low = (standard(two)[0] * vec[10:11] + vec[11:12]).astype(LOW)
    low_ref[...] = low
    projected = dot(low, proj_w[...])
    proj_ref[...] = projected
    square = jnp.sum(projected * projected, -1, keepdims=True) + 1e-06
    unit_ref[...] = (projected * lax.rsqrt(square)).astype(LOW)


def back_kernel(
    grad_ref, proj_ref, two_ref, slope_ref, resid_ref,
    proj_w, down_w, up_w, out_w, vec,
    gproj_ref, gtwo_ref, ghid_ref, gone_ref, gatt_ref, sum_ref,
):
    def add(row, value):
        sum_ref[row : row + 1, :] += jnp.sum(value, 0, keepdims=True)

    grad, projected = grad_ref[...], proj_ref[...]
    scale = lax.rsqrt(jnp.sum(projected * projected, -1, keepdims=True) + 1e-06)
    along = jnp.sum(projected * grad, -1, keepdims=True)
    gproj = (scale * grad - projected * (scale * scale * scale * along)).astype(LOW)
    gproj_ref[...] = gproj
    gnormed = dot(gproj, proj_w[...], ACROSS)
    unit, scale = standard(two_ref[...])
    add(10, gnormed * unit)
    add(11, gnormed)
    gtwo = standard_backward(gnormed * vec[10:11], unit, scale)
    add(9, gtwo)
    gtwo_low = gtwo.astype(LOW)
    gtwo_ref[...] = gtwo_low
    gnormed = gtwo
    for row in range(4):
        part = slice(row * D, row * D + D)
        ghid = dot(gtwo_low, down_w[part, :], ACROSS) * slope_ref[:, part].astype(F32)
        add(5 + row, ghid)
        ghid_low = ghid.astype(LOW)
        ghid_ref[:, part] = ghid_low
        gnormed = gnormed + dot(ghid_low, up_w[:, part], ACROSS)
    unit, scale = standard(resid_ref[...])
    add(3, gnormed * unit)
    add(4, gnormed)
    gone = standard_backward(gnormed * vec[3:4], unit, scale)
    add(2, gone)
    gone_low = gone.astype(LOW)
    gone_ref[...] = gone_low
    gatt_ref[...] = dot(gone_low, out_w[...], ACROSS).astype(LOW)


def attend_kernel(
    tile, lengths, spans, q_ref, k_ref, v_ref, col, row, out_ref, total_ref, logits, probs, flipped
):
    flipped[...] = v_ref[...].T
    lane = lax.broadcasted_iota(jnp.int32, (tile, 128), 1)

    def block(index, carry):
        here = pl.ds(pl.multiple_of(index * tile, tile), tile)
        low, kind = spans[index, 0], spans[index, 1]

        def attend(length):
            there = pl.ds(pl.multiple_of(low, 128), length)
            query = q_ref[here, :] * jnp.asarray(0.125, LOW)
            same = col[there, :] == row[0:1, here]
            tops = []
            for head in range(2):
                own = jnp.where((lane < 64) == (head == 0), query, jnp.zeros_like(query))
                value = jnp.where(same, dot(k_ref[there, :], own, ACROSS), -1e30)
                logits[head, 0:length, :] = value
                top = jnp.max(value.reshape(-1, 8, tile), 0)
                tops.append(jnp.max(top, 0, keepdims=True))
            sums = []
            for head in range(2):
                term = jnp.exp(logits[head, 0:length, :] - tops[head])
                sums.append(jnp.sum(term.reshape(-1, 8, tile), 0))
                probs[head, 0:length, :] = term.astype(LOW)
            parts = []
            for head in range(2):
                total = jnp.sum(sums[head], 0, keepdims=True)
                values = flipped[64 * head : 64 * head + 64, there]
                parts.append(dot(values, probs[head, 0:length, :]) / total)
                total_ref[0, head : head + 1, here] = tops[head] + jnp.log(total)
            out_ref[here, :] = jnp.concatenate(parts, 0).T.astype(LOW)

        for number, length in enumerate(lengths):
            pl.when(kind == number)(functools.partial(attend, length))
        return carry

    lax.fori_loop(0, q_ref.shape[0] // tile, block, 0)


def head_pair(count, row, first):
    return pl.BlockSpec((count, 128), lambda h, s: (row, first + h))


def attend_lengths(count):
    return [length for length in (128, 256, 384, 512, 640, 768, 1024) if count < 256 or length > 128][
        : 1 if count < 256 else None
    ]


def attend_call(kernel, tile, count, pairs, tables, arrays, specs, outputs, into, scratch, cost):
    spans, col, row = tables
    specs = specs + [
        pl.BlockSpec((count, tile), lambda h, s: (0, 0)),
        pl.BlockSpec((8, count), lambda h, s: (0, 0)),
    ]
    arguments = [spans, *arrays, col, row]
    aliases = {}
    used = len(arguments)
    if into is not None:
        aliases = {used + i: i for i in range(len(into))}
        specs = specs + [pl.BlockSpec(memory_space=pl.ANY)] * len(into)
        arguments += list(into)

    def run(*refs):
        kernel(tile, attend_lengths(count), *refs[:used], *refs[len(arguments) :])

    return pl.pallas_call(
        run,
        out_shape=[shape for shape, _ in outputs],
        grid_spec=pltpu.PrefetchScalarGridSpec(
            num_scalar_prefetch=1,
            grid=(pairs,),
            in_specs=specs,
            out_specs=[spec for _, spec in outputs],
            scratch_shapes=scratch,
        ),
        input_output_aliases=aliases,
        compiler_params=pltpu.CompilerParams(vmem_limit_bytes=48 << 20),
        cost_estimate=pl.CostEstimate(
            flops=cost * pairs * count * count * 128,
            transcendentals=0,
            bytes_accessed=8 * pairs * count * 128,
        ),
    )(*arguments)


def attend_forward(mixed, tables, tile, first, pairs, row, into=None):
    count = mixed.shape[0]
    return attend_call(
        attend_kernel,
        tile,
        count,
        pairs,
        tables,
        [mixed] * 3,
        [head_pair(count, 0, third * 6 + first) for third in range(3)],
        [
            (jax.ShapeDtypeStruct((TOKENS, D), LOW), head_pair(count, row, first)),
            (
                jax.ShapeDtypeStruct((6, 8, count), F32),
                pl.BlockSpec((1, 8, count), lambda h, s: (first + h, 0, 0)),
            ),
        ],
        into,
        [
            pltpu.VMEM((2, count, tile), F32),
            pltpu.VMEM((2, count, tile), LOW),
            pltpu.VMEM((128, count), LOW),
        ],
        40,
    )


def attend_back_kernel(
    tile, lengths, spans, q_ref, k_ref, v_ref, g_ref, total_ref, col, row,
    grad_ref, sum_ref, flipped, gkey, gvalue, probs, gprobs, low_probs, low_deltas,
):
    flipped[...] = k_ref[...].T
    gkey[...] = jnp.zeros_like(gkey)
    gvalue[...] = jnp.zeros_like(gvalue)
    sum_ref[...] = jnp.zeros_like(sum_ref)
    lane = lax.broadcasted_iota(jnp.int32, (tile, 128), 1)

    def block(index, carry):
        here = pl.ds(pl.multiple_of(index * tile, tile), tile)
        low, kind = spans[index, 0], spans[index, 1]

        def attend(length):
            there = pl.ds(pl.multiple_of(low, 128), length)
            query, grad = q_ref[here, :] * jnp.asarray(0.125, LOW), g_ref[here, :]
            zero = jnp.zeros_like(query)
            same = col[there, :] == row[0:1, here]
            own = [(lane < 64) == (head == 0) for head in range(2)]
            queries = [jnp.where(mine, query, zero) for mine in own]
            grads = [jnp.where(mine, grad, zero) for mine in own]
            dots = []
            for head in range(2):
                prob = dot(k_ref[there, :], queries[head], ACROSS)
                prob = jnp.exp(prob - total_ref[0, head : head + 1, here])
                prob = jnp.where(same, prob, 0.0)
                gprob = dot(v_ref[there, :], grads[head], ACROSS)
                total = jnp.sum((prob * gprob).reshape(-1, 8, tile), 0)
                dots.append(jnp.sum(total, 0, keepdims=True))
                probs[head, 0:length, :] = prob
                gprobs[head, 0:length, :] = gprob
                low_probs[head, 0:length, :] = prob.astype(LOW)

            def both(terms, right):
                return dot(terms[0, 0:length, :], right[0]) + dot(terms[1, 0:length, :], right[1])

            gvalue[there, :] += both(low_probs, grads)
            for head in range(2):
                delta = gprobs[head, 0:length, :] - dots[head]
                low_deltas[head, 0:length, :] = (probs[head, 0:length, :] * delta).astype(LOW)
            gkey[there, :] += both(low_deltas, queries)
            parts = []
            for head in range(2):
                keys = flipped[64 * head : 64 * head + 64, there]
                parts.append(dot(keys, low_deltas[head, 0:length, :]))
            whole = jnp.concatenate(parts, 0).T * 0.125
            grad_ref[0, here, :] = whole.astype(LOW)
            sum_ref[0:1, :] += jnp.sum(whole, 0, keepdims=True)

        for number, length in enumerate(lengths):
            pl.when(kind == number)(functools.partial(attend, length))
        return carry

    lax.fori_loop(0, q_ref.shape[0] // tile, block, 0)
    grad_ref[1] = gkey[...].astype(LOW)
    grad_ref[2] = gvalue[...].astype(LOW)
    sum_ref[1:2, :] = jnp.sum(gvalue[...], 0, keepdims=True)


def attend_backward(mixed, grad, total, tables, tile, first, pairs, row, into=None):
    count = mixed.shape[0]
    return attend_call(
        attend_back_kernel,
        tile,
        count,
        pairs,
        tables,
        [mixed] * 3 + [grad, total],
        [head_pair(count, 0, third * 6 + first) for third in range(3)]
        + [
            head_pair(count, row, first),
            pl.BlockSpec((1, 8, count), lambda h, s: (first + h, 0, 0)),
        ],
        [
            (
                jax.ShapeDtypeStruct((3, TOKENS, D), LOW),
                pl.BlockSpec((3, count, 128), lambda h, s: (0, row, first + h)),
            ),
            (
                jax.ShapeDtypeStruct((16, D), F32),
                pl.BlockSpec((16, 128), lambda h, s: (0, first + h)),
            ),
        ],
        into,
        [
            pltpu.VMEM((128, count), LOW),
            pltpu.VMEM((count, 128), F32),
            pltpu.VMEM((count, 128), F32),
            pltpu.VMEM((2, count, tile), F32),
            pltpu.VMEM((2, count, tile), F32),
            pltpu.VMEM((2, count, tile), LOW),
            pltpu.VMEM((2, count, tile), LOW),
        ],
        80,
    )


def segment_tables(segment, tile):
    count = segment.shape[0]
    lengths = jnp.asarray(attend_lengths(count), jnp.int32)
    ends = segment.reshape(count // tile, tile)
    first = jnp.sum((segment[None, :] < ends[:, :1]).astype(jnp.int32), 1) // 128 * 128
    last = jnp.sum((segment[None, :] <= ends[:, -1:]).astype(jnp.int32), 1)
    kind = jnp.sum((lengths[None, :] < (last - first)[:, None]).astype(jnp.int32), 1)
    chosen = jnp.arange(lengths.shape[0], dtype=jnp.int32)[None, :] == kind[:, None]
    keys = jnp.sum(jnp.where(chosen, lengths[None, :], 0), 1)
    return (
        jnp.stack([jnp.minimum(first, count - keys), kind], 1),
        jnp.broadcast_to(segment[:, None], (count, tile)),
        jnp.broadcast_to(segment[None, :], (8, count)),
    )


def two_terms(value):
    high = value.astype(LOW)
    return high, (value - high.astype(F32)).astype(LOW)


def sharp(cosine):
    return jnp.exp2(cosine * 14.426950408889634 - 14.426950408889634)


def score_kernel(query_ref, passage_ref, member_ref, score_ref, sums_ref, terms_ref):
    terms = sharp(dot(query_ref[...], passage_ref[...], ACROSS)).astype(LOW)
    terms_ref[...] = terms
    sums = dot(terms, member_ref[...])
    sums_ref[...] = sums
    lane = lax.broadcasted_iota(jnp.int32, sums.shape, 1)
    soft = jnp.where(lane < PPB, 0.1 * jnp.log(jnp.where(lane < PPB, sums, 1.0)) + 1.0, 0.0)
    score_ref[...] = jnp.sum(soft.reshape(-1, QLEN, 128), 1)


def score_ratio(grad_ref, sums_ref):
    rows = sums_ref.shape[0]
    lane = lax.broadcasted_iota(jnp.int32, (rows, 128), 1)
    grads = jnp.broadcast_to(grad_ref[...][:, None, :], (rows // QLEN, QLEN, 128))
    ratio = grads.reshape(rows, 128) / jnp.where(lane % 64 < PPB, sums_ref[...], 1.0)
    high, rest = two_terms(ratio)
    return jnp.where(lane < 64, high, rest)


def score_query_kernel(terms_ref, passage_ref, member_ref, grad_ref, sums_ref, out_ref):
    spread = dot(score_ratio(grad_ref, sums_ref), member_ref[...], ACROSS)
    terms = (terms_ref[...].astype(F32) * spread).astype(LOW)
    out_ref[...] = dot(terms, passage_ref[...])


def score_passage_kernel(query_ref, passage_ref, member_ref, grad_ref, sums_ref, out_ref):
    @pl.when(pl.program_id(0) == 0)
    def _():
        out_ref[...] = jnp.zeros_like(out_ref)

    ratio = score_ratio(grad_ref, sums_ref)
    terms = sharp(dot(passage_ref[...], query_ref[...], ACROSS))
    terms = (terms * dot(member_ref[...], ratio, ACROSS)).astype(LOW)
    out_ref[...] += dot(terms, query_ref[...])


SCORE_ROWS = 1024


def score_call(kernel, inputs, in_specs, out_specs, out_shape, flops):
    return pl.pallas_call(
        kernel,
        grid=(inputs[0].shape[0] // SCORE_ROWS,),
        in_specs=in_specs,
        out_specs=out_specs,
        out_shape=out_shape,
        compiler_params=pltpu.CompilerParams(vmem_limit_bytes=40 << 20),
        cost_estimate=pl.CostEstimate(
            flops=flops,
            transcendentals=inputs[0].shape[0] * BIN,
            bytes_accessed=inputs[0].shape[0] * 1024,
        ),
    )(*inputs)


def score_specs():
    rows = SCORE_ROWS
    fixed = pl.BlockSpec((BIN, 128), lambda i: (0, 0))
    return (
        pl.BlockSpec((rows, 128), lambda i: (i, 0)),
        fixed,
        pl.BlockSpec((rows // QLEN, 128), lambda i: (i, 0)),
    )


def score_forward(queries, passages, member):
    rows, fixed, grads = score_specs()
    count = queries.shape[0]
    return score_call(
        score_kernel,
        (queries, passages, member),
        [rows, fixed, fixed],
        [grads, rows, pl.BlockSpec((SCORE_ROWS, BIN), lambda i: (i, 0))],
        [
            jax.ShapeDtypeStruct((count // QLEN, 128), F32),
            jax.ShapeDtypeStruct((count, 128), F32),
            jax.ShapeDtypeStruct((count, BIN), LOW),
        ],
        6 * count * BIN * 128,
    )


def score_backward(kernel, queries, passages, member, grad_scores, sums):
    rows, fixed, grads = score_specs()
    count = queries.shape[0]
    inputs = (queries, passages, member, grad_scores, sums)
    left = pl.BlockSpec((SCORE_ROWS, queries.shape[1]), lambda i: (i, 0))
    in_specs = [left, fixed, fixed, grads, rows]
    width, spec = (BIN, fixed) if kernel is score_passage_kernel else (count, rows)
    out = jax.ShapeDtypeStruct((width, 128), F32)
    return score_call(kernel, inputs, in_specs, spec, out, 6 * count * BIN * 128)


def finish_kernel(scalars, *refs):
    own, moved, sums, (first_ref, vector_ref, square_ref) = refs[:4], refs[4:7], refs[7:-3], refs[-3:]
    rows = first_ref.shape[0]
    here = pl.ds(pl.multiple_of(scalars[0] * rows, rows), rows)
    square = jnp.zeros((1, 1), F32)
    at = 0
    for ref in own:
        part = slice(at, at + ref.shape[1])
        total = ref[here, :]
        for more in moved:
            total = total + more[:, part].astype(F32)
        if at < 3 * D:
            first_ref[:, part] = total
        else:
            vector_ref[...] = total
        square = square + jnp.sum(total * total, keepdims=True)
        at += ref.shape[1]
    for ref in sums:
        square = square + jnp.sum(ref[...] * ref[...], keepdims=True)
    square_ref[...] = jnp.broadcast_to(square, square_ref.shape)


def finish(arrays, sums):
    kinds = (False,) * 4
    if not staged_mesh():
        *thirds, vector = scatter_rest(arrays)
        square = sum(jnp.sum(a * a) for a in (*thirds, vector, *sums))
        return jnp.concatenate(thirds, 1), vector, jnp.full((1, 128), square)
    rows = arrays[0].shape[0] // 4
    inputs = [*arrays, *last_moves(depth_blocks(arrays), kinds), *sums]
    shapes = [(rows, 3 * D), (rows, 128), (1, 128)]
    return pl.pallas_call(
        finish_kernel,
        grid_spec=pltpu.PrefetchScalarGridSpec(
            num_scalar_prefetch=1,
            grid=(1,),
            in_specs=[pl.BlockSpec(a.shape, lambda i, s: (0, 0)) for a in inputs],
            out_specs=[pl.BlockSpec(shape, lambda i, s: (0, 0)) for shape in shapes],
        ),
        out_shape=[jax.ShapeDtypeStruct(shape, F32) for shape in shapes],
        compiler_params=pltpu.CompilerParams(vmem_limit_bytes=32 << 20),
    )(scalars_of_position(), *inputs)


def cross_grad(scores, partition, passage_ids, chosen_ids, query_total):
    onehot = (passage_ids[None, :] == chosen_ids[:, None]).astype(jnp.float32)
    return (jnp.exp(scores) / partition[:, None] - onehot) / query_total


def adam_update(weight, moment_one, moment_two, gradient, factor, rate):
    clipped = gradient * factor
    new_one = beta_one * moment_one + (1.0 - beta_one) * clipped
    new_two = beta_two * moment_two + (1.0 - beta_two) * clipped * clipped
    direction = (
        new_one / (1.0 - beta_one**STEP) / (jnp.sqrt(new_two / (1.0 - beta_two**STEP)) + adam_eps)
    )
    return (weight - rate * (direction + decay_rate * weight), new_one, new_two)


def body(
    query_tokens,
    passage_tokens,
    passage_lengths,
    positives,
    qkv_weight,
    qkv_first,
    qkv_second,
    out_weight,
    out_first,
    out_second,
    up_weight,
    up_first,
    up_second,
    down_weight,
    down_first,
    down_second,
    proj_weight,
    proj_first,
    proj_second,
    vector_params,
    vector_first,
    vector_second,
):
    vector_part = jnp.pad(vector_params.T, ((0, 0), (0, 116))).astype(LOW)
    first_part = jnp.concatenate([qkv_weight.astype(LOW), vector_part], 1)
    middle_part = jnp.concatenate([up_weight, out_weight, proj_weight], 1).astype(LOW)
    down_part = down_weight.astype(LOW)
    first_line = line_of(first_part, send_line(first_part))
    middle_moved = send_line(gate(middle_part, first_line))
    first_pair = gather_pair(first_line)
    own_index = lax.axis_index(("pb", "pa"))
    query_total = QPD * lax.axis_size(("pb", "pa"))
    query_flat = query_tokens.reshape(QUERY_ROWS, D)
    lengths, passages = gate((passage_lengths, passage_tokens[0]), first_pair)
    tokens = jnp.concatenate([passages, query_flat], 0)
    query_seg = np.arange(QUERY_ROWS, dtype=np.int32) // QLEN
    query_tables = (
        jnp.zeros((1, 2), jnp.int32),
        jnp.asarray(np.broadcast_to(query_seg[:, None], (QUERY_ROWS, QUERY_ROWS))),
        jnp.asarray(np.broadcast_to(query_seg[None, :], (8, QUERY_ROWS))),
    )
    own_lengths = lax.dynamic_index_in_dim(lengths, own_index, 0, keepdims=False)
    upto = np.tril(np.ones((PPB, PPB), np.int32))
    ends = jnp.sum(jnp.where(upto > 0, own_lengths[None, :], 0), 1)
    places = jnp.arange(BIN, dtype=jnp.int32)
    own_seg = jnp.sum((places[:, None] >= ends[None, :]).astype(jnp.int32), 1)
    passage_tables = segment_tables(own_seg, ATTEND_TILE)
    member = (own_seg[:, None] == jnp.arange(128, dtype=jnp.int32)[None, :] % 64).astype(LOW)
    ready = tokens, passage_tables, member
    first_quad = gather_quad(first_pair, ready)
    middle = gather_rest(line_of(middle_part, gate(middle_moved, first_quad)))
    qkv_matrix, vectors = gather_whole(first_quad, [(0, 2304), (2304, 2432)])
    vectors = vectors[:, :12].T.astype(F32)
    bias_qkv = jnp.concatenate([vectors[0], jnp.zeros_like(vectors[0]), vectors[1]])

    def mix(rows):
        return (dot(rows, qkv_matrix) + bias_qkv).astype(LOW)

    query_mixed = mix(query_flat)
    down_moved = send_line(gate(down_part, query_mixed))
    passage_mixed = mix(gate(passage_tokens[0], query_mixed))
    down_line = line_of(down_part, gate(down_moved, passage_mixed))
    attended, query_log = attend_forward(
        gate(query_mixed, down_line), query_tables, QUERY_ROWS, 0, 6, BIN // QUERY_ROWS
    )
    passage_state = attend_forward(
        gate(passage_mixed, down_line), passage_tables, ATTEND_TILE, 0, 3, 0, (attended,)
    )
    down_pair = gather_pair(down_line, passage_state)
    attended, passage_log = attend_forward(
        gate(passage_mixed, down_pair), passage_tables, ATTEND_TILE, 3, 3, 0, passage_state
    )
    down_quad = gather_quad(down_pair, attended)
    up = columns(middle, 0, 4 * D)
    out = columns(middle, 4 * D, 5 * D)
    proj = columns(middle, 5 * D, 5 * D + 128)
    vector_rows = columns(vectors)

    def widen(rows, first, count, att, into):
        return row_call(
            widen_kernel,
            rows,
            first,
            count,
            [(tokens, first), (att, first)],
            (out, up, vector_rows),
            [(D, F32), (D, LOW), (4 * D, LOW), (4 * D, LOW)],
            into=into,
            flops=10 * D * D,
        )

    def narrow(rows, first, count, wider, into):
        return row_call(
            narrow_kernel,
            rows,
            first,
            count,
            [(wider[2], first), (wider[0], first)],
            (down, proj, vector_rows),
            [(D, F32), (D, LOW), (128, F32), (128, LOW)],
            into=into,
            flops=8 * D * D,
        )

    wider = widen(QUERY_ROWS, BIN // QUERY_ROWS, 1, gate(attended, down_quad), None)
    (down_matrix,) = gather_whole(down_quad, [(0, D)], wider)
    down = columns(down_matrix)
    narrower = narrow(QUERY_ROWS, BIN // QUERY_ROWS, 1, wider, None)
    query_part = narrower[3][BIN:]
    query_line = line_of(query_part, send_line(query_part))
    every_query = gather_rest(query_line)
    wider = widen(
        FEED_ROWS, 0, BIN // FEED_ROWS, gate(attended, query_line), gate(wider, narrower)
    )
    narrower = narrow(FEED_ROWS, 0, BIN // FEED_ROWS, wider, narrower)
    resid, normed, active, slope = wider
    two, normed_out, projected, unit = narrower
    passage_unit = unit[:BIN]

    passage_ids = own_index * PPB + jnp.arange(PPB, dtype=jnp.int32)
    scores, totals, score_terms = score_forward(every_query, passage_unit, member)
    scores = scores[:, :PPB]
    turned = transposed(gate(tokens, scores))
    partition = gate(sum_everywhere(jnp.sum(jnp.exp(scores), 1)), turned)
    grad_scores = cross_grad(scores, partition, passage_ids, positives, query_total)
    grad_scores = jnp.tile(jnp.pad(grad_scores, ((0, 0), (0, 64 - PPB))), (1, 2))
    grad_every = score_backward(
        score_query_kernel, score_terms, passage_unit, member, grad_scores, totals
    )
    whole, rounded = (True,), (False,)
    query_back = scatter_quad([grad_every], scatter_sends([grad_every], whole))
    grad_passage = score_backward(
        score_passage_kernel,
        gate(every_query, query_back),
        passage_unit,
        member,
        grad_scores,
        totals,
    )

    def go_back(rows, first, count, grad, into):
        return row_call(
            back_kernel,
            rows,
            first,
            count,
            [grad, (projected, first), (two, first), (slope, first), (resid, first)],
            (proj, down, up, out, vector_rows),
            [(128, LOW), (D, LOW), (4 * D, LOW), (D, LOW), (D, LOW)],
            (D,),
            into=into,
            flops=18 * D * D,
        )

    query_back = scatter_pair(query_back, pair_send(query_back, whole), whole)
    back = go_back(
        BACK_ROWS, 0, BIN // BACK_ROWS, (gate(grad_passage, query_back), 0), None
    )
    query_back = scatter_line(query_back, whole)
    (grad_query,) = scatter_total(gate(query_back, back), whole)
    back = go_back(QUERY_ROWS, BIN // QUERY_ROWS, 1, (grad_query, 0), back)
    gproj, gtwo, ghid, gone, gatt, sums = back

    def terms(left, right):
        return dot(left, right, (((0,), (0,)), ((), ()))).astype(LOW)

    def attend_back(first, pairs, into, *others):
        mixed = gate(passage_mixed, *others)
        return attend_backward(
            mixed, gatt, passage_log, passage_tables, ATTEND_TILE, first, pairs, 0, into
        )

    down_terms = terms(active, gtwo)
    down_sends = scatter_sends([down_terms], rounded)
    up_terms = terms(normed, gate(ghid, down_sends))
    down_back = scatter_quad([down_terms], down_sends, up_terms)
    down_send = pair_send(down_back, rounded)
    down_pair = scatter_pair(down_back, down_send, rounded)
    rest = gate((gone, gproj), down_send)
    out_terms, proj_terms = terms(attended, rest[0]), dot(rest[1], normed_out, (((0,), (0,)), ((), ()))).T
    kinds = (False, False, True)
    middle_terms = [up_terms, out_terms, proj_terms]
    middle_sends = scatter_sends(middle_terms, kinds)
    query_grads = attend_backward(
        gate(query_mixed, middle_sends),
        gatt,
        query_log,
        query_tables,
        QUERY_ROWS,
        0,
        6,
        BIN // QUERY_ROWS,
    )
    middle_back = scatter_quad(middle_terms, middle_sends, query_grads)
    middle_send = pair_send(middle_back, kinds)
    middle_pair = scatter_pair(middle_back, middle_send, kinds)
    down_line = scatter_line(down_pair, rounded)
    grads = attend_back(0, 2, query_grads[:1], query_grads, down_pair, middle_send)
    (down_sum,) = scatter_total(gate(down_line, grads), rounded)
    grads = attend_back(2, 2, grads, down_line)
    middle_line = scatter_line(gate(middle_pair, grads), kinds)
    grads = attend_back(4, 2, grads, middle_pair, down_sum)
    up_sum, out_sum, proj_sum = scatter_total(middle_line, kinds)
    mixed_grads = gate(grads[0], middle_line)
    first_terms = [dot(turned, mixed_grads[third]).astype(LOW) for third in range(3)]
    mixed_sums = grads[1] + query_grads[1]
    vector_grad = jnp.concatenate([mixed_sums[:2], sums[2:12]], 0)
    vector_terms = jnp.pad(vector_grad.T, ((0, 0), (0, 116)))
    kinds = (False,) * 4
    first_terms.append(vector_terms)
    first_back = scatter_quad(first_terms, scatter_sends(first_terms, kinds))
    first_back = scatter_pair(first_back, pair_send(first_back, kinds), kinds, up_sum, down_sum)
    qkv_sum, vector_sum, square = finish(
        scatter_line(first_back, kinds), (out_sum, up_sum, down_sum, proj_sum)
    )
    reduced = (qkv_sum, out_sum, up_sum, down_sum, proj_sum, vector_sum[:, :12].T)
    norm_value = jnp.sqrt(sum_everywhere(square)[0, 0])
    factor = jnp.minimum(1.0, clip_max / (norm_value + 1e-06))
    qkv_res = adam_update(qkv_weight, qkv_first, qkv_second, reduced[0], factor, learn_rate)
    out_res = adam_update(out_weight, out_first, out_second, reduced[1], factor, learn_rate)
    up_res = adam_update(up_weight, up_first, up_second, reduced[2], factor, learn_rate)
    down_res = adam_update(down_weight, down_first, down_second, reduced[3], factor, learn_rate)
    proj_res = adam_update(proj_weight, proj_first, proj_second, reduced[4], factor, learn_rate)
    vector_res = adam_update(
        vector_params, vector_first, vector_second, reduced[5], factor, vector_rate
    )
    return (
        norm_value,
        qkv_res[0],
        qkv_res[1],
        qkv_res[2],
        out_res[0],
        out_res[1],
        out_res[2],
        up_res[0],
        up_res[1],
        up_res[2],
        down_res[0],
        down_res[1],
        down_res[2],
        proj_res[0],
        proj_res[1],
        proj_res[2],
        vector_res[0],
        vector_res[1],
        vector_res[2],
    )


def solution(mesh):
    placed = (
        P(("pb", "pa"), None, None),
        P(("pb", "pa"), None, None),
        P(),
        P(),
        P(("pb", "pa"), None),
        P(("pb", "pa"), None),
        P(("pb", "pa"), None),
        P(("pb", "pa"), None),
        P(("pb", "pa"), None),
        P(("pb", "pa"), None),
        P(("pb", "pa"), None),
        P(("pb", "pa"), None),
        P(("pb", "pa"), None),
        P(("pb", "pa"), None),
        P(("pb", "pa"), None),
        P(("pb", "pa"), None),
        P(("pb", "pa"), None),
        P(("pb", "pa"), None),
        P(("pb", "pa"), None),
        P(None, ("pb", "pa")),
        P(None, ("pb", "pa")),
        P(None, ("pb", "pa")),
    )
    return jax.shard_map(
        body,
        mesh=mesh,
        in_specs=placed,
        out_specs=(
            P(),
            P(("pb", "pa"), None),
            P(("pb", "pa"), None),
            P(("pb", "pa"), None),
            P(("pb", "pa"), None),
            P(("pb", "pa"), None),
            P(("pb", "pa"), None),
            P(("pb", "pa"), None),
            P(("pb", "pa"), None),
            P(("pb", "pa"), None),
            P(("pb", "pa"), None),
            P(("pb", "pa"), None),
            P(("pb", "pa"), None),
            P(("pb", "pa"), None),
            P(("pb", "pa"), None),
            P(("pb", "pa"), None),
            P(None, ("pb", "pa")),
            P(None, ("pb", "pa")),
            P(None, ("pb", "pa")),
        ),
        check_vma=False,
    )
```

```python
import functools

import jax
import jax.numpy as jnp
import numpy as np
from jax import lax
from jax.experimental import pallas as pl
from jax.experimental.pallas import tpu as pltpu
from jax.sharding import PartitionSpec as P

D = 768
HEAD_DIM = 64
QLEN = 32
BIN = 1024
PPB = 8
STEP = 10
QPD = 4
QUERY_ROWS = QPD * QLEN
TOKENS = BIN + QUERY_ROWS
ATTEND_TILE = 256
FEED_ROWS = 256
BACK_ROWS = 256


F32 = jnp.float32
LOW = jnp.bfloat16
sharpness_divisor = 0.1
clip_max = 0.02
learn_rate = 0.04
vector_rate = 0.4
beta_one = 0.9
beta_two = 0.999
adam_eps = 1e-08
decay_rate = 0.01
norm_eps = 1e-12


def shift_pairs(amount):
    return [(i, (i + amount) % 4) for i in range(4)]


FIRST_STEP = [(i, i ^ 2 if i % 2 == 0 else i ^ 4) for i in range(8)]
SECOND_STEP = [(i, i ^ 4 if i % 2 == 0 else i ^ 2) for i in range(8)]
CORE_PAIR = [(i, i ^ 1) for i in range(8)]


def staged_mesh():
    return lax.axis_size("pb") == 8 and lax.axis_size("pa") == 4


def position():
    row = lax.axis_index("pb")
    core, x_bit, y_bit = row % 2, (row // 2) % 2, row // 4
    return (
        lax.axis_index("pa"),
        core,
        jnp.where(core == 0, x_bit, y_bit),
        jnp.where(core == 0, y_bit, x_bit),
    )


def gate(value, *others):
    return lax.optimization_barrier((value, others))[0]


def place_blocks(sources, copies, outputs, index):
    def run(scalars, *refs):
        given, (results, sems) = refs[: len(sources)], (refs[len(sources) : -1], refs[-1])
        moves = [
            pltpu.make_async_copy(
                given[source].at[where(scalars)], results[out].at[there(scalars)], sems.at[number]
            )
            for number, (source, where, out, there) in enumerate(copies)
        ]
        for move in moves:
            move.start()
        for move in moves:
            move.wait()

    anywhere = pl.BlockSpec(memory_space=pl.ANY)
    return pl.pallas_call(
        run,
        grid_spec=pltpu.PrefetchScalarGridSpec(
            num_scalar_prefetch=1,
            grid=(),
            in_specs=[anywhere] * len(sources),
            out_specs=[anywhere] * len(outputs),
            scratch_shapes=[pltpu.SemaphoreType.DMA((len(copies),))],
        ),
        out_shape=outputs,
        compiler_params=pltpu.CompilerParams(vmem_limit_bytes=4 << 20),
        cost_estimate=pl.CostEstimate(
            flops=0,
            transcendentals=0,
            bytes_accessed=2 * sum(o.size * o.dtype.itemsize for o in outputs),
        ),
    )(index, *sources)


def scalars_of_position():
    return jnp.stack([jnp.asarray(v, jnp.int32) for v in position()])


def send_line(part):
    if not staged_mesh():
        return [lax.all_gather(part, "pa", axis=0, tiled=True)]
    return [lax.ppermute(part, "pa", shift_pairs(k)) for k in (1, 2, 3)]


def line_of(part, moved):
    if not staged_mesh():
        return moved[0]
    depth = position()[0]
    around = [part, moved[2], moved[1], moved[0]]
    line = jnp.stack([lax.select_n((place - depth) % 4, *around) for place in range(4)])
    return line.reshape((4 * part.shape[0],) + part.shape[1:])


def gather_rest(line):
    return lax.all_gather(line, "pb", axis=0, tiled=True)


def in_order(own, other, which):
    both = jax.ShapeDtypeStruct((2,) + own.shape, own.dtype)
    copies = [
        (0, lambda s: Ellipsis, 0, lambda s: s[which]),
        (1, lambda s: Ellipsis, 0, lambda s: 1 - s[which]),
    ]
    return place_blocks([own, other], copies, [both], scalars_of_position())[0]


def gather_pair(line, *others):
    if not staged_mesh():
        return line
    return in_order(line, gate(lax.ppermute(line, "pb", FIRST_STEP), others), 2)


def gather_quad(pair, *others):
    if not staged_mesh():
        return pair
    return in_order(pair, gate(lax.ppermute(pair, "pb", SECOND_STEP), others), 3)


def gather_whole(quad, ranges, *others):
    if not staged_mesh():
        whole = gather_rest(quad)
        return [whole[:, low:high] for low, high in ranges]
    partner = gate(lax.ppermute(quad, "pb", CORE_PAIR), others)
    rows = quad.shape[2]
    copies, outputs = [], []
    for number, (low, high) in enumerate(ranges):
        outputs.append(jax.ShapeDtypeStruct((8, rows, high - low), quad.dtype))
        for source in range(2):
            for second in range(2):
                for first in range(2):

                    def where(s, second=second, first=first, low=low, high=high):
                        return second, first, slice(None), slice(low, high)

                    def there(s, source=source, second=second, first=first):
                        core = s[1] if source == 0 else 1 - s[1]
                        swapped = 4 * first + 2 * second
                        return core + jnp.where(core == 0, 4 * second + 2 * first, swapped)

                    copies.append((source, where, number, there))
    results = place_blocks([quad, partner], copies, outputs, scalars_of_position())
    return [a.reshape(8 * rows, a.shape[2]) for a in results]


def split_low(value):
    high = lax.reduce_precision(value, 8, 7)
    return high.astype(LOW), (value - high).astype(LOW)


def packed(arrays, exact):
    if exact == (None,):
        return arrays[0]
    pieces = []
    for array, whole in zip(arrays, exact):
        pieces += split_low(array) if whole else [array.astype(LOW)]
    return pieces[0] if len(pieces) == 1 else jnp.concatenate(pieces, -1)


def joined(arrays, exact, moved):
    results, at = [], 0
    for array, whole in zip(arrays, exact):
        total = array.astype(F32)
        for _ in range(2 if whole else 1):
            total = total + moved[..., at : at + array.shape[-1]].astype(F32)
            at += array.shape[-1]
        results.append(total)
    return results


def blocks_at(arrays, place):
    return [lax.dynamic_index_in_dim(array, place, 0, False) for array in arrays]


def core_blocks(array, other):
    core = position()[1]
    parts = array.reshape((4, 2, array.shape[0] // 8) + array.shape[1:])
    return lax.dynamic_index_in_dim(parts, 1 - core if other else core, 1, False)


def scatter_sends(arrays, exact):
    if not staged_mesh():
        return arrays
    sends = [core_blocks(array, True) for array in arrays]
    return [a.astype(LOW) if whole is False else a for a, whole in zip(sends, exact)]


def scatter_quad(arrays, sends, *others):
    if not staged_mesh():
        return [
            lax.psum_scatter(a.astype(F32), "pb", scatter_dimension=0, tiled=True)
            for a in arrays
        ]
    moved = gate([lax.ppermute(a, "pb", CORE_PAIR) for a in sends], others)
    return [
        core_blocks(array, False).astype(F32) + m.astype(F32) for array, m in zip(arrays, moved)
    ]


def chip_pairs(arrays, bit):
    core = position()[1]
    first = jnp.where(core == 0, 2 * bit, bit)
    second = first + jnp.where(core == 0, 1, 2)
    return [
        jnp.stack([lax.dynamic_index_in_dim(a, i, 0, False) for i in (first, second)])
        for a in arrays
    ]


def pair_send(arrays, exact):
    if not staged_mesh():
        return arrays
    return packed(chip_pairs(arrays, 1 - position()[3]), exact)


def scatter_pair(arrays, send, exact, *others):
    if not staged_mesh():
        return arrays
    moved = gate(lax.ppermute(send, "pb", SECOND_STEP), others)
    return joined(chip_pairs(arrays, position()[3]), exact, moved)


def scatter_line(arrays, exact):
    if not staged_mesh():
        return arrays
    bit = position()[2]
    send = packed(blocks_at(arrays, 1 - bit), exact)
    return joined(blocks_at(arrays, bit), exact, lax.ppermute(send, "pb", FIRST_STEP))


def scatter_rest(arrays):
    return [lax.psum_scatter(a, "pa", scatter_dimension=0, tiled=True) for a in arrays]


def last_moves(arrays, exact):
    depth = position()[0]
    sends = [packed(blocks_at(arrays, (depth + k) % 4), exact) for k in (1, 2, 3)]
    return [lax.ppermute(s, "pa", shift_pairs(k + 1)) for k, s in enumerate(sends)]


def depth_blocks(arrays):
    return [a.reshape((4, a.shape[0] // 4) + a.shape[1:]) for a in arrays]


def scatter_total(arrays, exact):
    if not staged_mesh():
        return scatter_rest(arrays)
    arrays = depth_blocks(arrays)
    total = blocks_at(arrays, position()[0])
    for moved in last_moves(arrays, exact):
        total = joined(total, exact, moved)
    return total


def everywhere(value):
    count = lax.axis_size(("pb", "pa"))
    copies = jnp.broadcast_to(value[None], (count,) + value.shape)
    return lax.all_to_all(copies, ("pb", "pa"), 0, 0)


ACROSS = (((1,), (1,)), ((), ()))
PLAIN = (((1,), (0,)), ((), ()))


def dot(left, right, dims=PLAIN):
    return lax.dot_general(left, right, dims, preferred_element_type=F32)


def standard(hidden):
    centred = hidden - jnp.mean(hidden, -1, keepdims=True)
    spread = jnp.mean(centred * centred, -1, keepdims=True)
    scale = lax.rsqrt(spread + norm_eps)
    return centred * scale, scale


def standard_backward(grad, unit, scale):
    return scale * (
        grad
        - jnp.mean(grad, -1, keepdims=True)
        - unit * jnp.mean(grad * unit, -1, keepdims=True)
    )


def gelu_with_slope(value):
    below = 0.5 + 0.5 * lax.erf(value * 0.7071067811865476)
    bell = jnp.exp2(value * (value * -0.7213475204444817))
    return value * below, below + value * (0.3989422804014327 * bell)


def columns(array, low=0, high=None):
    width = array.shape[1] - low if high is None else high - low
    spec = pl.BlockSpec(
        (array.shape[0], width), lambda i: (0, low // width), pipeline_mode=pl.Buffered(1)
    )
    return array, spec


def transposed(array):
    rows, width = array.shape
    return pl.pallas_call(
        lambda x_ref, out_ref: out_ref.__setitem__(Ellipsis, x_ref[...].T),
        grid=(width // 128,),
        in_specs=[pl.BlockSpec((rows, 128), lambda i: (0, i))],
        out_specs=pl.BlockSpec((128, rows), lambda i: (i, 0)),
        out_shape=jax.ShapeDtypeStruct((width, rows), array.dtype),
    )(array)


def row_call(kernel, rows, first, count, inputs, weights, outputs, sums=(), into=None, flops=0):
    done = 0 if into is None else len(inputs) + len(weights)

    def run(*refs):
        given, results = refs[: len(inputs) + len(weights)], refs[-len(outputs) - len(sums) :]
        if sums:

            @pl.when(pl.program_id(0) == 0)
            def _():
                for place in range(len(sums)):
                    place -= len(sums)
                    start = refs[place - len(outputs) - len(sums)] if done else None
                    here = results[place]
                    here[...] = start[...] if done else jnp.zeros_like(here)

        kernel(*given, *results)

    moved = rows * count * sum(a.shape[1] * a.dtype.itemsize for a, _ in inputs)
    moved += sum(w.size * w.dtype.itemsize for w, _ in weights)
    moved += rows * count * sum(w * jnp.dtype(t).itemsize for w, t in outputs)

    def rows_at(width, begin):
        return pl.BlockSpec((rows, width), lambda i: (begin + i, 0))

    sum_specs = [pl.BlockSpec((16, w), lambda i: (0, 0)) for w in sums]
    in_specs = [rows_at(a.shape[1], begin) for a, begin in inputs]
    in_specs += [spec for _, spec in weights]
    arguments = [a for a, _ in inputs] + [w for w, _ in weights]
    if into is not None:
        in_specs += [pl.BlockSpec(memory_space=pl.ANY)] * len(outputs) + sum_specs
        arguments += list(into)
    return pl.pallas_call(
        run,
        grid=(count,),
        in_specs=in_specs,
        out_specs=[rows_at(w, first) for w, _ in outputs] + sum_specs,
        out_shape=[jax.ShapeDtypeStruct((TOKENS, w), t) for w, t in outputs]
        + [jax.ShapeDtypeStruct((16, w), F32) for w in sums],
        input_output_aliases={done + i: i for i in range(len(outputs) + len(sums))} if done else {},
        compiler_params=pltpu.CompilerParams(vmem_limit_bytes=56 << 20),
        cost_estimate=pl.CostEstimate(
            flops=flops * rows * count, transcendentals=0, bytes_accessed=moved
        ),
    )(*arguments)


def row_parts(ref):
    return [slice(at, at + 128) for at in range(0, ref.shape[0], 128)]


def widen_kernel(x_ref, att_ref, out_w, up_w, vec, resid_ref, low_ref, act_ref, slope_ref):
    lows = []
    for part in row_parts(x_ref):
        resid = x_ref[part, :].astype(F32) + dot(att_ref[part, :], out_w[...]) + vec[2:3]
        resid_ref[part, :] = resid
        lows.append((standard(resid)[0] * vec[3:4] + vec[4:5]).astype(LOW))
        low_ref[part, :] = lows[-1]
    for row in range(4):
        cols = slice(row * D, row * D + D)
        for part, low in zip(row_parts(x_ref), lows):
            value, slope = gelu_with_slope(dot(low, up_w[:, cols]) + vec[5 + row : 6 + row])
            act_ref[part, cols] = value.astype(LOW)
            slope_ref[part, cols] = slope.astype(LOW)


def narrow_kernel(act_ref, resid_ref, down_w, proj_w, vec, two_ref, low_ref, proj_ref, unit_ref):
    branches = [dot(act_ref[part, :], down_w[...]) for part in row_parts(act_ref)]
    for part, branch in zip(row_parts(act_ref), branches):
        normed = standard(resid_ref[part, :])[0] * vec[3:4] + vec[4:5]
        two = normed + branch + vec[9:10]
        two_ref[part, :] = two
        low = (standard(two)[0] * vec[10:11] + vec[11:12]).astype(LOW)
        low_ref[part, :] = low
        projected = dot(low, proj_w[...])
        proj_ref[part, :] = projected
        square = jnp.sum(projected * projected, -1, keepdims=True) + 1e-06
        unit_ref[part, :] = (projected * lax.rsqrt(square)).astype(LOW)


def back_kernel(
    grad_ref, proj_ref, two_ref, slope_ref, resid_ref,
    proj_w, down_w, up_w, out_w, vec,
    gproj_ref, gtwo_ref, ghid_ref, gone_ref, gatt_ref, sum_ref,
):
    def add(row, value):
        sum_ref[row : row + 1, :] += jnp.sum(value, 0, keepdims=True)

    grad, projected = grad_ref[...], proj_ref[...]
    scale = lax.rsqrt(jnp.sum(projected * projected, -1, keepdims=True) + 1e-06)
    along = jnp.sum(projected * grad, -1, keepdims=True)
    gproj = (scale * grad - projected * (scale * scale * scale * along)).astype(LOW)
    gproj_ref[...] = gproj
    gnormed = dot(gproj, proj_w[...], ACROSS)
    unit, scale = standard(two_ref[...])
    add(10, gnormed * unit)
    add(11, gnormed)
    gtwo = standard_backward(gnormed * vec[10:11], unit, scale)
    add(9, gtwo)
    gtwo_low = gtwo.astype(LOW)
    gtwo_ref[...] = gtwo_low
    gnormed = gtwo
    for row in range(4):
        part = slice(row * D, row * D + D)
        ghid = dot(gtwo_low, down_w[part, :], ACROSS) * slope_ref[:, part].astype(F32)
        add(5 + row, ghid)
        ghid_low = ghid.astype(LOW)
        ghid_ref[:, part] = ghid_low
        gnormed = gnormed + dot(ghid_low, up_w[:, part], ACROSS)
    unit, scale = standard(resid_ref[...])
    add(3, gnormed * unit)
    add(4, gnormed)
    gone = standard_backward(gnormed * vec[3:4], unit, scale)
    add(2, gone)
    gone_low = gone.astype(LOW)
    gone_ref[...] = gone_low
    gatt_ref[...] = dot(gone_low, out_w[...], ACROSS).astype(LOW)


def attend_kernel(
    tile, lengths, spans, q_ref, k_ref, v_ref, col, row, out_ref, total_ref, logits, probs, flipped
):
    flipped[...] = v_ref[...].T
    lane = lax.broadcasted_iota(jnp.int32, (tile, 128), 1)

    def block(index, carry):
        here = pl.ds(pl.multiple_of(index * tile, tile), tile)
        low, kind = spans[index, 0], spans[index, 1]

        def attend(length):
            there = pl.ds(pl.multiple_of(low, 128), length)
            query = q_ref[here, :] * jnp.asarray(0.125, LOW)
            same = col[there, :] == row[0:1, here]
            tops = []
            for head in range(2):
                own = jnp.where((lane < 64) == (head == 0), query, jnp.zeros_like(query))
                value = jnp.where(same, dot(k_ref[there, :], own, ACROSS), -1e30)
                logits[head, 0:length, :] = value
                top = jnp.max(value.reshape(-1, 8, tile), 0)
                tops.append(jnp.max(top, 0, keepdims=True))
            sums = []
            for head in range(2):
                term = jnp.exp(logits[head, 0:length, :] - tops[head])
                sums.append(jnp.sum(term.reshape(-1, 8, tile), 0))
                probs[head, 0:length, :] = term.astype(LOW)
            parts = []
            for head in range(2):
                total = jnp.sum(sums[head], 0, keepdims=True)
                values = flipped[64 * head : 64 * head + 64, there]
                parts.append(dot(values, probs[head, 0:length, :]) / total)
                total_ref[0, head : head + 1, here] = tops[head] + jnp.log(total)
            out_ref[here, :] = jnp.concatenate(parts, 0).T.astype(LOW)

        for number, length in enumerate(lengths):
            pl.when(kind == number)(functools.partial(attend, length))
        return carry

    lax.fori_loop(0, q_ref.shape[0] // tile, block, 0)


def head_pair(count, row, first):
    return pl.BlockSpec((count, 128), lambda h, s: (row, first + h))


def attend_lengths(count):
    return [length for length in (128, 256, 384, 512, 640, 768, 1024) if count < 256 or length > 128][
        : 1 if count < 256 else None
    ]


def attend_call(kernel, tile, count, pairs, tables, arrays, specs, outputs, into, scratch, cost):
    spans, col, row = tables
    specs = specs + [
        pl.BlockSpec((count, tile), lambda h, s: (0, 0)),
        pl.BlockSpec((8, count), lambda h, s: (0, 0)),
    ]
    arguments = [spans, *arrays, col, row]
    aliases = {}
    used = len(arguments)
    if into is not None:
        aliases = {used + i: i for i in range(len(into))}
        specs = specs + [pl.BlockSpec(memory_space=pl.ANY)] * len(into)
        arguments += list(into)

    def run(*refs):
        kernel(tile, attend_lengths(count), *refs[:used], *refs[len(arguments) :])

    return pl.pallas_call(
        run,
        out_shape=[shape for shape, _ in outputs],
        grid_spec=pltpu.PrefetchScalarGridSpec(
            num_scalar_prefetch=1,
            grid=(pairs,),
            in_specs=specs,
            out_specs=[spec for _, spec in outputs],
            scratch_shapes=scratch,
        ),
        input_output_aliases=aliases,
        compiler_params=pltpu.CompilerParams(vmem_limit_bytes=48 << 20),
        cost_estimate=pl.CostEstimate(
            flops=cost * pairs * count * count * 128,
            transcendentals=0,
            bytes_accessed=8 * pairs * count * 128,
        ),
    )(*arguments)


def attend_forward(mixed, tables, tile, first, pairs, row, into=None):
    count = mixed.shape[0]
    return attend_call(
        attend_kernel,
        tile,
        count,
        pairs,
        tables,
        [mixed] * 3,
        [head_pair(count, 0, third * 6 + first) for third in range(3)],
        [
            (jax.ShapeDtypeStruct((TOKENS, D), LOW), head_pair(count, row, first)),
            (
                jax.ShapeDtypeStruct((6, 8, count), F32),
                pl.BlockSpec((1, 8, count), lambda h, s: (first + h, 0, 0)),
            ),
        ],
        into,
        [
            pltpu.VMEM((2, count, tile), F32),
            pltpu.VMEM((2, count, tile), LOW),
            pltpu.VMEM((128, count), LOW),
        ],
        40,
    )


def attend_back_kernel(
    tile, lengths, spans, q_ref, k_ref, v_ref, g_ref, total_ref, col, row,
    grad_ref, sum_ref, flipped, gkey, gvalue, probs, gprobs, low_probs, low_deltas,
):
    flipped[...] = k_ref[...].T
    gkey[...] = jnp.zeros_like(gkey)
    gvalue[...] = jnp.zeros_like(gvalue)
    sum_ref[...] = jnp.zeros_like(sum_ref)
    lane = lax.broadcasted_iota(jnp.int32, (tile, 128), 1)

    def block(index, carry):
        here = pl.ds(pl.multiple_of(index * tile, tile), tile)
        low, kind = spans[index, 0], spans[index, 1]

        def attend(length):
            there = pl.ds(pl.multiple_of(low, 128), length)
            query, grad = q_ref[here, :] * jnp.asarray(0.125, LOW), g_ref[here, :]
            zero = jnp.zeros_like(query)
            same = col[there, :] == row[0:1, here]
            own = [(lane < 64) == (head == 0) for head in range(2)]
            queries = [jnp.where(mine, query, zero) for mine in own]
            grads = [jnp.where(mine, grad, zero) for mine in own]
            dots = []
            for head in range(2):
                prob = dot(k_ref[there, :], queries[head], ACROSS)
                prob = jnp.exp(prob - total_ref[0, head : head + 1, here])
                prob = jnp.where(same, prob, 0.0)
                gprob = dot(v_ref[there, :], grads[head], ACROSS)
                total = jnp.sum((prob * gprob).reshape(-1, 8, tile), 0)
                dots.append(jnp.sum(total, 0, keepdims=True))
                probs[head, 0:length, :] = prob
                gprobs[head, 0:length, :] = gprob
                low_probs[head, 0:length, :] = prob.astype(LOW)

            def both(terms, right):
                return dot(terms[0, 0:length, :], right[0]) + dot(terms[1, 0:length, :], right[1])

            gvalue[there, :] += both(low_probs, grads)
            for head in range(2):
                delta = gprobs[head, 0:length, :] - dots[head]
                low_deltas[head, 0:length, :] = (probs[head, 0:length, :] * delta).astype(LOW)
            gkey[there, :] += both(low_deltas, queries)
            parts = []
            for head in range(2):
                keys = flipped[64 * head : 64 * head + 64, there]
                parts.append(dot(keys, low_deltas[head, 0:length, :]))
            whole = jnp.concatenate(parts, 0).T * 0.125
            grad_ref[0, here, :] = whole.astype(LOW)
            sum_ref[0:1, :] += jnp.sum(whole, 0, keepdims=True)

        for number, length in enumerate(lengths):
            pl.when(kind == number)(functools.partial(attend, length))
        return carry

    lax.fori_loop(0, q_ref.shape[0] // tile, block, 0)
    grad_ref[1] = gkey[...].astype(LOW)
    grad_ref[2] = gvalue[...].astype(LOW)
    sum_ref[1:2, :] = jnp.sum(gvalue[...], 0, keepdims=True)


def attend_backward(mixed, grad, total, tables, tile, first, pairs, row, into=None):
    count = mixed.shape[0]
    return attend_call(
        attend_back_kernel,
        tile,
        count,
        pairs,
        tables,
        [mixed] * 3 + [grad, total],
        [head_pair(count, 0, third * 6 + first) for third in range(3)]
        + [
            head_pair(count, row, first),
            pl.BlockSpec((1, 8, count), lambda h, s: (first + h, 0, 0)),
        ],
        [
            (
                jax.ShapeDtypeStruct((3, TOKENS, D), LOW),
                pl.BlockSpec((3, count, 128), lambda h, s: (0, row, first + h)),
            ),
            (
                jax.ShapeDtypeStruct((16, D), F32),
                pl.BlockSpec((16, 128), lambda h, s: (0, first + h)),
            ),
        ],
        into,
        [
            pltpu.VMEM((128, count), LOW),
            pltpu.VMEM((count, 128), F32),
            pltpu.VMEM((count, 128), F32),
            pltpu.VMEM((2, count, tile), F32),
            pltpu.VMEM((2, count, tile), F32),
            pltpu.VMEM((2, count, tile), LOW),
            pltpu.VMEM((2, count, tile), LOW),
        ],
        80,
    )


def segment_tables(segment, tile):
    count = segment.shape[0]
    lengths = jnp.asarray(attend_lengths(count), jnp.int32)
    ends = segment.reshape(count // tile, tile)
    first = jnp.sum((segment[None, :] < ends[:, :1]).astype(jnp.int32), 1) // 128 * 128
    last = jnp.sum((segment[None, :] <= ends[:, -1:]).astype(jnp.int32), 1)
    kind = jnp.sum((lengths[None, :] < (last - first)[:, None]).astype(jnp.int32), 1)
    chosen = jnp.arange(lengths.shape[0], dtype=jnp.int32)[None, :] == kind[:, None]
    keys = jnp.sum(jnp.where(chosen, lengths[None, :], 0), 1)
    return (
        jnp.stack([jnp.minimum(first, count - keys), kind], 1),
        jnp.broadcast_to(segment[:, None], (count, tile)),
        jnp.broadcast_to(segment[None, :], (8, count)),
    )


def two_terms(value):
    high = value.astype(LOW)
    return high, (value - high.astype(F32)).astype(LOW)


def sharp(cosine):
    return jnp.exp2(cosine * 14.426950408889634 - 14.426950408889634)


def score_kernel(query_ref, passage_ref, member_ref, score_ref, sums_ref, terms_ref):
    terms = sharp(dot(query_ref[...], passage_ref[...], ACROSS)).astype(LOW)
    terms_ref[...] = terms
    sums = dot(terms, member_ref[...])
    sums_ref[...] = sums
    lane = lax.broadcasted_iota(jnp.int32, sums.shape, 1)
    soft = jnp.where(lane < PPB, 0.1 * jnp.log(jnp.where(lane < PPB, sums, 1.0)) + 1.0, 0.0)
    score_ref[...] = jnp.sum(soft.reshape(-1, QLEN, 128), 1)


def score_ratio(grad_ref, sums_ref):
    rows = sums_ref.shape[0]
    lane = lax.broadcasted_iota(jnp.int32, (rows, 128), 1)
    grads = jnp.broadcast_to(grad_ref[...][:, None, :], (rows // QLEN, QLEN, 128))
    ratio = grads.reshape(rows, 128) / jnp.where(lane % 64 < PPB, sums_ref[...], 1.0)
    high, rest = two_terms(ratio)
    return jnp.where(lane < 64, high, rest)


def score_query_kernel(terms_ref, passage_ref, member_ref, grad_ref, sums_ref, out_ref):
    spread = dot(score_ratio(grad_ref, sums_ref), member_ref[...], ACROSS)
    terms = (terms_ref[...].astype(F32) * spread).astype(LOW)
    out_ref[...] = dot(terms, passage_ref[...])


def score_passage_kernel(query_ref, passage_ref, member_ref, grad_ref, sums_ref, out_ref):
    @pl.when(pl.program_id(0) == 0)
    def _():
        out_ref[...] = jnp.zeros_like(out_ref)

    ratio = score_ratio(grad_ref, sums_ref)
    terms = sharp(dot(passage_ref[...], query_ref[...], ACROSS))
    terms = (terms * dot(member_ref[...], ratio, ACROSS)).astype(LOW)
    out_ref[...] += dot(terms, query_ref[...])


SCORE_ROWS = 1024


def score_call(kernel, inputs, in_specs, out_specs, out_shape, flops):
    return pl.pallas_call(
        kernel,
        grid=(inputs[0].shape[0] // SCORE_ROWS,),
        in_specs=in_specs,
        out_specs=out_specs,
        out_shape=out_shape,
        compiler_params=pltpu.CompilerParams(vmem_limit_bytes=40 << 20),
        cost_estimate=pl.CostEstimate(
            flops=flops,
            transcendentals=inputs[0].shape[0] * BIN,
            bytes_accessed=inputs[0].shape[0] * 1024,
        ),
    )(*inputs)


def score_specs():
    rows = SCORE_ROWS
    fixed = pl.BlockSpec((BIN, 128), lambda i: (0, 0))
    return (
        pl.BlockSpec((rows, 128), lambda i: (i, 0)),
        fixed,
        pl.BlockSpec((rows // QLEN, 128), lambda i: (i, 0)),
    )


def score_forward(queries, passages, member):
    rows, fixed, grads = score_specs()
    count = queries.shape[0]
    return score_call(
        score_kernel,
        (queries, passages, member),
        [rows, fixed, fixed],
        [grads, rows, pl.BlockSpec((SCORE_ROWS, BIN), lambda i: (i, 0))],
        [
            jax.ShapeDtypeStruct((count // QLEN, 128), F32),
            jax.ShapeDtypeStruct((count, 128), F32),
            jax.ShapeDtypeStruct((count, BIN), LOW),
        ],
        6 * count * BIN * 128,
    )


def score_backward(kernel, queries, passages, member, grad_scores, sums):
    rows, fixed, grads = score_specs()
    count = queries.shape[0]
    inputs = (queries, passages, member, grad_scores, sums)
    left = pl.BlockSpec((SCORE_ROWS, queries.shape[1]), lambda i: (i, 0))
    in_specs = [left, fixed, fixed, grads, rows]
    width, spec = (BIN, fixed) if kernel is score_passage_kernel else (count, rows)
    out = jax.ShapeDtypeStruct((width, 128), F32)
    return score_call(kernel, inputs, in_specs, spec, out, 6 * count * BIN * 128)


def finish_kernel(scalars, *refs):
    own, moved, sums, (first_ref, vector_ref, square_ref) = refs[:4], refs[4:7], refs[7:-3], refs[-3:]
    rows = first_ref.shape[0]
    here = pl.ds(pl.multiple_of(scalars[0] * rows, rows), rows)
    square = jnp.zeros((1, 1), F32)
    at = 0
    for ref in own:
        part = slice(at, at + ref.shape[1])
        total = ref[here, :]
        for more in moved:
            total = total + more[:, part].astype(F32)
        if at < 3 * D:
            first_ref[:, part] = total
        else:
            vector_ref[...] = total
        square = square + jnp.sum(total * total, keepdims=True)
        at += ref.shape[1]
    for ref in sums:
        square = square + jnp.sum(ref[...] * ref[...], keepdims=True)
    square_ref[...] = jnp.broadcast_to(square, square_ref.shape)


def finish(arrays, sums):
    kinds = (False,) * 4
    if not staged_mesh():
        *thirds, vector = scatter_rest(arrays)
        square = sum(jnp.sum(a * a) for a in (*thirds, vector, *sums))
        return jnp.concatenate(thirds, 1), vector, jnp.full((1, 128), square)
    rows = arrays[0].shape[0] // 4
    inputs = [*arrays, *last_moves(depth_blocks(arrays), kinds), *sums]
    shapes = [(rows, 3 * D), (rows, 128), (1, 128)]
    return pl.pallas_call(
        finish_kernel,
        grid_spec=pltpu.PrefetchScalarGridSpec(
            num_scalar_prefetch=1,
            grid=(1,),
            in_specs=[pl.BlockSpec(a.shape, lambda i, s: (0, 0)) for a in inputs],
            out_specs=[pl.BlockSpec(shape, lambda i, s: (0, 0)) for shape in shapes],
        ),
        out_shape=[jax.ShapeDtypeStruct(shape, F32) for shape in shapes],
        compiler_params=pltpu.CompilerParams(vmem_limit_bytes=32 << 20),
    )(scalars_of_position(), *inputs)


def cross_grad(scores, partition, passage_ids, chosen_ids, query_total):
    onehot = (passage_ids[None, :] == chosen_ids[:, None]).astype(jnp.float32)
    return (jnp.exp(scores) / partition[:, None] - onehot) / query_total


def adam_kernel(square_ref, *refs):
    count = 6
    given, (norm_ref, *results) = refs[: 4 * count], refs[4 * count :]
    norm = jnp.sqrt(jnp.sum(square_ref[...], 0, keepdims=True)[:, 0:1])
    norm_ref[...] = jnp.broadcast_to(norm, norm_ref.shape)
    factor = jnp.minimum(1.0, clip_max / (norm + 1e-06))
    for number in range(count):
        weight, first, second, gradient = (r[...] for r in given[4 * number : 4 * number + 4])
        rate = vector_rate if number == count - 1 else learn_rate
        clipped = gradient * factor
        new_first = beta_one * first + (1.0 - beta_one) * clipped
        new_second = beta_two * second + (1.0 - beta_two) * clipped * clipped
        spread = jnp.sqrt(new_second / (1.0 - beta_two**STEP)) + adam_eps
        direction = new_first / (1.0 - beta_one**STEP) / spread
        results[3 * number][...] = weight - rate * (direction + decay_rate * weight)
        results[3 * number + 1][...] = new_first
        results[3 * number + 2][...] = new_second


def adam_updates(squares, groups):
    inputs = [squares] + [array for group in groups for array in group]
    shapes = [(1, 128)] + [group[0].shape for group in groups for _ in range(3)]
    return pl.pallas_call(
        adam_kernel,
        grid=(1,),
        in_specs=[pl.BlockSpec(a.shape, lambda i: (0, 0)) for a in inputs],
        out_specs=[pl.BlockSpec(shape, lambda i: (0, 0)) for shape in shapes],
        out_shape=[jax.ShapeDtypeStruct(shape, F32) for shape in shapes],
        compiler_params=pltpu.CompilerParams(vmem_limit_bytes=58 << 20),
    )(*inputs)


def body(
    query_tokens,
    passage_tokens,
    passage_lengths,
    positives,
    qkv_weight,
    qkv_first,
    qkv_second,
    out_weight,
    out_first,
    out_second,
    up_weight,
    up_first,
    up_second,
    down_weight,
    down_first,
    down_second,
    proj_weight,
    proj_first,
    proj_second,
    vector_params,
    vector_first,
    vector_second,
):
    vector_part = jnp.pad(vector_params.T, ((0, 0), (0, 116))).astype(LOW)
    first_part = jnp.concatenate([qkv_weight.astype(LOW), vector_part], 1)
    middle_part = jnp.concatenate([up_weight, out_weight, proj_weight], 1).astype(LOW)
    down_part = down_weight.astype(LOW)
    first_line = line_of(first_part, send_line(first_part))
    middle_moved = send_line(gate(middle_part, first_line))
    first_pair = gather_pair(first_line)
    own_index = lax.axis_index(("pb", "pa"))
    query_total = QPD * lax.axis_size(("pb", "pa"))
    query_flat = query_tokens.reshape(QUERY_ROWS, D)
    lengths, passages = gate((passage_lengths, passage_tokens[0]), first_pair)
    tokens = jnp.concatenate([passages, query_flat], 0)
    query_seg = np.arange(QUERY_ROWS, dtype=np.int32) // QLEN
    query_tables = (
        jnp.zeros((1, 2), jnp.int32),
        jnp.asarray(np.broadcast_to(query_seg[:, None], (QUERY_ROWS, QUERY_ROWS))),
        jnp.asarray(np.broadcast_to(query_seg[None, :], (8, QUERY_ROWS))),
    )
    own_lengths = lax.dynamic_index_in_dim(lengths, own_index, 0, keepdims=False)
    upto = np.tril(np.ones((PPB, PPB), np.int32))
    ends = jnp.sum(jnp.where(upto > 0, own_lengths[None, :], 0), 1)
    places = jnp.arange(BIN, dtype=jnp.int32)
    own_seg = jnp.sum((places[:, None] >= ends[None, :]).astype(jnp.int32), 1)
    passage_tables = segment_tables(own_seg, ATTEND_TILE)
    member = (own_seg[:, None] == jnp.arange(128, dtype=jnp.int32)[None, :] % 64).astype(LOW)
    ready = tokens, passage_tables, member
    first_quad = gather_quad(first_pair, ready)
    middle = gather_rest(line_of(middle_part, gate(middle_moved, first_quad)))
    qkv_matrix, vectors = gather_whole(first_quad, [(0, 2304), (2304, 2432)])
    vectors = vectors[:, :12].T.astype(F32)
    bias_qkv = jnp.concatenate([vectors[0], jnp.zeros_like(vectors[0]), vectors[1]])

    def mix(rows):
        return (dot(rows, qkv_matrix) + bias_qkv).astype(LOW)

    query_mixed = mix(query_flat)
    down_moved = send_line(gate(down_part, query_mixed))
    passage_mixed = mix(gate(passage_tokens[0], query_mixed))
    down_line = line_of(down_part, gate(down_moved, passage_mixed))
    attended, query_log = attend_forward(
        gate(query_mixed, down_line), query_tables, QUERY_ROWS, 0, 6, BIN // QUERY_ROWS
    )
    passage_state = attend_forward(
        gate(passage_mixed, down_line), passage_tables, ATTEND_TILE, 0, 3, 0, (attended,)
    )
    down_pair = gather_pair(down_line, passage_state)
    attended, passage_log = attend_forward(
        gate(passage_mixed, down_pair), passage_tables, ATTEND_TILE, 3, 3, 0, passage_state
    )
    down_quad = gather_quad(down_pair, attended)
    up = columns(middle, 0, 4 * D)
    out = columns(middle, 4 * D, 5 * D)
    proj = columns(middle, 5 * D, 5 * D + 128)
    vector_rows = columns(vectors)

    def widen(rows, first, count, att, into):
        return row_call(
            widen_kernel,
            rows,
            first,
            count,
            [(tokens, first), (att, first)],
            (out, up, vector_rows),
            [(D, F32), (D, LOW), (4 * D, LOW), (4 * D, LOW)],
            into=into,
            flops=10 * D * D,
        )

    def narrow(rows, first, count, wider, into):
        return row_call(
            narrow_kernel,
            rows,
            first,
            count,
            [(wider[2], first), (wider[0], first)],
            (down, proj, vector_rows),
            [(D, F32), (D, LOW), (128, F32), (128, LOW)],
            into=into,
            flops=8 * D * D,
        )

    wider = widen(QUERY_ROWS, BIN // QUERY_ROWS, 1, gate(attended, down_quad), None)
    (down_matrix,) = gather_whole(down_quad, [(0, D)], wider)
    down = columns(down_matrix)
    narrower = narrow(QUERY_ROWS, BIN // QUERY_ROWS, 1, wider, None)
    query_part = narrower[3][BIN:]
    query_line = line_of(query_part, send_line(query_part))
    every_query = gather_rest(query_line)
    wider = widen(
        FEED_ROWS, 0, BIN // FEED_ROWS, gate(attended, query_line), gate(wider, narrower)
    )
    narrower = narrow(FEED_ROWS, 0, BIN // FEED_ROWS, wider, narrower)
    resid, normed, active, slope = wider
    two, normed_out, projected, unit = narrower
    passage_unit = unit

    passage_ids = own_index * PPB + jnp.arange(PPB, dtype=jnp.int32)
    scores, totals, score_terms = score_forward(every_query, passage_unit, member)
    scores = scores[:, :PPB]
    turned = transposed(gate(tokens, scores))
    partition = gate(jnp.sum(everywhere(jnp.sum(jnp.exp(scores), 1)), 0), turned)
    grad_scores = cross_grad(scores, partition, passage_ids, positives, query_total)
    grad_scores = jnp.tile(jnp.pad(grad_scores, ((0, 0), (0, 64 - PPB))), (1, 2))
    grad_every = score_backward(
        score_query_kernel, score_terms, passage_unit, member, grad_scores, totals
    )
    whole, rounded = (None,), (False,)
    query_back = scatter_quad([grad_every], scatter_sends([grad_every], whole))
    grad_passage = score_backward(
        score_passage_kernel,
        gate(every_query, query_back),
        passage_unit,
        member,
        grad_scores,
        totals,
    )

    def go_back(rows, first, count, grad, into):
        return row_call(
            back_kernel,
            rows,
            first,
            count,
            [grad, (projected, first), (two, first), (slope, first), (resid, first)],
            (proj, down, up, out, vector_rows),
            [(128, LOW), (D, LOW), (4 * D, LOW), (D, LOW), (D, LOW)],
            (D,),
            into=into,
            flops=18 * D * D,
        )

    query_back = scatter_pair(query_back, pair_send(query_back, whole), whole)
    back = go_back(
        BACK_ROWS, 0, BIN // BACK_ROWS, (gate(grad_passage, query_back), 0), None
    )
    query_back = scatter_line(query_back, whole)
    (grad_query,) = scatter_total(gate(query_back, back), whole)
    back = go_back(QUERY_ROWS, BIN // QUERY_ROWS, 1, (grad_query, 0), back)
    gproj, gtwo, ghid, gone, gatt, sums = back

    def terms(left, right):
        return dot(left, right, (((0,), (0,)), ((), ()))).astype(LOW)

    def attend_back(first, pairs, into, *others):
        mixed = gate(passage_mixed, *others)
        return attend_backward(
            mixed, gatt, passage_log, passage_tables, ATTEND_TILE, first, pairs, 0, into
        )

    down_terms = terms(active, gtwo)
    down_sends = scatter_sends([down_terms], rounded)
    up_terms = terms(normed, gate(ghid, down_sends))
    down_back = scatter_quad([down_terms], down_sends, up_terms)
    down_send = pair_send(down_back, rounded)
    down_pair = scatter_pair(down_back, down_send, rounded)
    rest = gate((gone, gproj), down_send)
    out_terms, proj_terms = terms(attended, rest[0]), dot(rest[1], normed_out, (((0,), (0,)), ((), ()))).T
    kinds = (False, False, True)
    middle_terms = [up_terms, out_terms, proj_terms]
    middle_sends = scatter_sends(middle_terms, kinds)
    query_grads = attend_backward(
        gate(query_mixed, middle_sends),
        gatt,
        query_log,
        query_tables,
        QUERY_ROWS,
        0,
        6,
        BIN // QUERY_ROWS,
    )
    middle_back = scatter_quad(middle_terms, middle_sends, query_grads)
    middle_send = pair_send(middle_back, kinds)
    middle_pair = scatter_pair(middle_back, middle_send, kinds)
    down_line = scatter_line(down_pair, rounded)
    grads = attend_back(0, 2, query_grads[:1], query_grads, down_pair, middle_send)
    (down_sum,) = scatter_total(gate(down_line, grads), rounded)
    grads = attend_back(2, 2, grads, down_line)
    middle_line = scatter_line(gate(middle_pair, grads), kinds)
    grads = attend_back(4, 2, grads, middle_pair, down_sum)
    up_sum, out_sum, proj_sum = scatter_total(middle_line, kinds)
    mixed_grads = gate(grads[0], middle_line)
    first_terms = [dot(turned, mixed_grads[third]).astype(LOW) for third in range(3)]
    mixed_sums = grads[1] + query_grads[1]
    vector_grad = jnp.concatenate([mixed_sums[:2], sums[2:12]], 0)
    vector_terms = jnp.pad(vector_grad.T, ((0, 0), (0, 116)))
    kinds = (False,) * 4
    first_terms.append(vector_terms)
    first_back = scatter_quad(first_terms, scatter_sends(first_terms, kinds))
    first_back = scatter_pair(first_back, pair_send(first_back, kinds), kinds, up_sum, down_sum)
    qkv_sum, vector_sum, square = finish(
        scatter_line(first_back, kinds), (out_sum, up_sum, down_sum, proj_sum)
    )
    groups = (
        (qkv_weight, qkv_first, qkv_second, qkv_sum),
        (out_weight, out_first, out_second, out_sum),
        (up_weight, up_first, up_second, up_sum),
        (down_weight, down_first, down_second, down_sum),
        (proj_weight, proj_first, proj_second, proj_sum),
        (vector_params, vector_first, vector_second, vector_sum[:, :12].T),
    )
    norm, *results = adam_updates(everywhere(square)[:, 0], groups)
    return (norm[0, 0], *results)


def solution(mesh):
    placed = (
        P(("pb", "pa"), None, None),
        P(("pb", "pa"), None, None),
        P(),
        P(),
        P(("pb", "pa"), None),
        P(("pb", "pa"), None),
        P(("pb", "pa"), None),
        P(("pb", "pa"), None),
        P(("pb", "pa"), None),
        P(("pb", "pa"), None),
        P(("pb", "pa"), None),
        P(("pb", "pa"), None),
        P(("pb", "pa"), None),
        P(("pb", "pa"), None),
        P(("pb", "pa"), None),
        P(("pb", "pa"), None),
        P(("pb", "pa"), None),
        P(("pb", "pa"), None),
        P(("pb", "pa"), None),
        P(None, ("pb", "pa")),
        P(None, ("pb", "pa")),
        P(None, ("pb", "pa")),
    )
    return jax.shard_map(
        body,
        mesh=mesh,
        in_specs=placed,
        out_specs=(
            P(),
            P(("pb", "pa"), None),
            P(("pb", "pa"), None),
            P(("pb", "pa"), None),
            P(("pb", "pa"), None),
            P(("pb", "pa"), None),
            P(("pb", "pa"), None),
            P(("pb", "pa"), None),
            P(("pb", "pa"), None),
            P(("pb", "pa"), None),
            P(("pb", "pa"), None),
            P(("pb", "pa"), None),
            P(("pb", "pa"), None),
            P(("pb", "pa"), None),
            P(("pb", "pa"), None),
            P(("pb", "pa"), None),
            P(None, ("pb", "pa")),
            P(None, ("pb", "pa")),
            P(None, ("pb", "pa")),
        ),
        check_vma=False,
    )
```

```python
import functools

import jax
import jax.numpy as jnp
import numpy as np
from jax import lax
from jax.experimental import pallas as pl
from jax.experimental.pallas import tpu as pltpu
from jax.sharding import PartitionSpec as P

D = 768
HEAD_DIM = 64
QLEN = 32
BIN = 1024
PPB = 8
STEP = 10
QPD = 4
QUERY_ROWS = QPD * QLEN
TOKENS = BIN + QUERY_ROWS
ATTEND_TILE = 256
FEED_ROWS = 256
BACK_ROWS = 256


F32 = jnp.float32
LOW = jnp.bfloat16
sharpness_divisor = 0.1
clip_max = 0.02
learn_rate = 0.04
vector_rate = 0.4
beta_one = 0.9
beta_two = 0.999
adam_eps = 1e-08
decay_rate = 0.01
norm_eps = 1e-12


def shift_pairs(amount):
    return [(i, (i + amount) % 4) for i in range(4)]


FIRST_STEP = [(i, i ^ 2 if i % 2 == 0 else i ^ 4) for i in range(8)]
SECOND_STEP = [(i, i ^ 4 if i % 2 == 0 else i ^ 2) for i in range(8)]
CORE_PAIR = [(i, i ^ 1) for i in range(8)]


def staged_mesh():
    return lax.axis_size("pb") == 8 and lax.axis_size("pa") == 4


def position():
    row = lax.axis_index("pb")
    core, x_bit, y_bit = row % 2, (row // 2) % 2, row // 4
    return (
        lax.axis_index("pa"),
        core,
        jnp.where(core == 0, x_bit, y_bit),
        jnp.where(core == 0, y_bit, x_bit),
    )


def gate(value, *others):
    return lax.optimization_barrier((value, others))[0]


def place_blocks(sources, copies, outputs, index):
    def run(scalars, *refs):
        given, (results, sems) = refs[: len(sources)], (refs[len(sources) : -1], refs[-1])
        moves = [
            pltpu.make_async_copy(
                given[source].at[where(scalars)], results[out].at[there(scalars)], sems.at[number]
            )
            for number, (source, where, out, there) in enumerate(copies)
        ]
        for move in moves:
            move.start()
        for move in moves:
            move.wait()

    anywhere = pl.BlockSpec(memory_space=pl.ANY)
    return pl.pallas_call(
        run,
        grid_spec=pltpu.PrefetchScalarGridSpec(
            num_scalar_prefetch=1,
            grid=(),
            in_specs=[anywhere] * len(sources),
            out_specs=[anywhere] * len(outputs),
            scratch_shapes=[pltpu.SemaphoreType.DMA((len(copies),))],
        ),
        out_shape=outputs,
        compiler_params=pltpu.CompilerParams(vmem_limit_bytes=4 << 20),
        cost_estimate=pl.CostEstimate(
            flops=0,
            transcendentals=0,
            bytes_accessed=2 * sum(o.size * o.dtype.itemsize for o in outputs),
        ),
    )(index, *sources)


def scalars_of_position():
    return jnp.stack([jnp.asarray(v, jnp.int32) for v in position()])


def send_line(part):
    if not staged_mesh():
        return [lax.all_gather(part, "pa", axis=0, tiled=True)]
    return [lax.ppermute(part, "pa", shift_pairs(k)) for k in (1, 2, 3)]


def line_of(part, moved):
    if not staged_mesh():
        return moved[0]
    depth = position()[0]
    around = [part, moved[2], moved[1], moved[0]]
    line = jnp.stack([lax.select_n((place - depth) % 4, *around) for place in range(4)])
    return line.reshape((4 * part.shape[0],) + part.shape[1:])


def gather_rest(line):
    return lax.all_gather(line, "pb", axis=0, tiled=True)


def in_order(own, other, which):
    both = jax.ShapeDtypeStruct((2,) + own.shape, own.dtype)
    copies = [
        (0, lambda s: Ellipsis, 0, lambda s: s[which]),
        (1, lambda s: Ellipsis, 0, lambda s: 1 - s[which]),
    ]
    return place_blocks([own, other], copies, [both], scalars_of_position())[0]


def gather_pair(line, *others):
    if not staged_mesh():
        return line
    return in_order(line, gate(lax.ppermute(line, "pb", FIRST_STEP), others), 2)


def gather_quad(pair, *others):
    if not staged_mesh():
        return pair
    return in_order(pair, gate(lax.ppermute(pair, "pb", SECOND_STEP), others), 3)


def gather_whole(quad, ranges, *others):
    if not staged_mesh():
        whole = gather_rest(quad)
        return [whole[:, low:high] for low, high in ranges]
    partner = gate(lax.ppermute(quad, "pb", CORE_PAIR), others)
    rows = quad.shape[2]
    copies, outputs = [], []
    for number, (low, high) in enumerate(ranges):
        outputs.append(jax.ShapeDtypeStruct((8, rows, high - low), quad.dtype))
        for source in range(2):
            for second in range(2):
                for first in range(2):

                    def where(s, second=second, first=first, low=low, high=high):
                        return second, first, slice(None), slice(low, high)

                    def there(s, source=source, second=second, first=first):
                        core = s[1] if source == 0 else 1 - s[1]
                        swapped = 4 * first + 2 * second
                        return core + jnp.where(core == 0, 4 * second + 2 * first, swapped)

                    copies.append((source, where, number, there))
    results = place_blocks([quad, partner], copies, outputs, scalars_of_position())
    return [a.reshape(8 * rows, a.shape[2]) for a in results]


def split_low(value):
    high = lax.reduce_precision(value, 8, 7)
    return high.astype(LOW), (value - high).astype(LOW)


def packed(arrays, exact):
    if exact == (None,):
        return arrays[0]
    pieces = []
    for array, whole in zip(arrays, exact):
        pieces += split_low(array) if whole else [array.astype(LOW)]
    return pieces[0] if len(pieces) == 1 else jnp.concatenate(pieces, -1)


def joined(arrays, exact, moved):
    results, at = [], 0
    for array, whole in zip(arrays, exact):
        total = array.astype(F32)
        for _ in range(2 if whole else 1):
            total = total + moved[..., at : at + array.shape[-1]].astype(F32)
            at += array.shape[-1]
        results.append(total)
    return results


def blocks_at(arrays, place):
    return [lax.dynamic_index_in_dim(array, place, 0, False) for array in arrays]


def core_blocks(array, other):
    core = position()[1]
    parts = array.reshape((4, 2, array.shape[0] // 8) + array.shape[1:])
    return lax.dynamic_index_in_dim(parts, 1 - core if other else core, 1, False)


def scatter_sends(arrays, exact):
    if not staged_mesh():
        return arrays
    sends = [core_blocks(array, True) for array in arrays]
    return [a.astype(LOW) if whole is False else a for a, whole in zip(sends, exact)]


def scatter_quad(arrays, sends, *others):
    if not staged_mesh():
        return [
            lax.psum_scatter(a.astype(F32), "pb", scatter_dimension=0, tiled=True)
            for a in arrays
        ]
    moved = gate([lax.ppermute(a, "pb", CORE_PAIR) for a in sends], others)
    return [
        core_blocks(array, False).astype(F32) + m.astype(F32) for array, m in zip(arrays, moved)
    ]


def chip_pairs(arrays, bit):
    core = position()[1]
    first = jnp.where(core == 0, 2 * bit, bit)
    second = first + jnp.where(core == 0, 1, 2)
    return [
        jnp.stack([lax.dynamic_index_in_dim(a, i, 0, False) for i in (first, second)])
        for a in arrays
    ]


def pair_send(arrays, exact):
    if not staged_mesh():
        return arrays
    return packed(chip_pairs(arrays, 1 - position()[3]), exact)


def scatter_pair(arrays, send, exact, *others):
    if not staged_mesh():
        return arrays
    moved = gate(lax.ppermute(send, "pb", SECOND_STEP), others)
    return joined(chip_pairs(arrays, position()[3]), exact, moved)


def scatter_line(arrays, exact):
    if not staged_mesh():
        return arrays
    bit = position()[2]
    send = packed(blocks_at(arrays, 1 - bit), exact)
    return joined(blocks_at(arrays, bit), exact, lax.ppermute(send, "pb", FIRST_STEP))


def scatter_rest(arrays):
    return [lax.psum_scatter(a, "pa", scatter_dimension=0, tiled=True) for a in arrays]


def last_moves(arrays, exact):
    depth = position()[0]
    sends = [packed(blocks_at(arrays, (depth + k) % 4), exact) for k in (1, 2, 3)]
    return [lax.ppermute(s, "pa", shift_pairs(k + 1)) for k, s in enumerate(sends)]


def depth_blocks(arrays):
    return [a.reshape((4, a.shape[0] // 4) + a.shape[1:]) for a in arrays]


def scatter_total(arrays, exact):
    if not staged_mesh():
        return scatter_rest(arrays)
    arrays = depth_blocks(arrays)
    total = blocks_at(arrays, position()[0])
    for moved in last_moves(arrays, exact):
        total = joined(total, exact, moved)
    return total


def everywhere(value):
    count = lax.axis_size(("pb", "pa"))
    copies = jnp.broadcast_to(value[None], (count,) + value.shape)
    return lax.all_to_all(copies, ("pb", "pa"), 0, 0)


ACROSS = (((1,), (1,)), ((), ()))
PLAIN = (((1,), (0,)), ((), ()))


def dot(left, right, dims=PLAIN):
    return lax.dot_general(left, right, dims, preferred_element_type=F32)


def standard(hidden):
    centred = hidden - jnp.mean(hidden, -1, keepdims=True)
    spread = jnp.mean(centred * centred, -1, keepdims=True)
    scale = lax.rsqrt(spread + norm_eps)
    return centred * scale, scale


def standard_backward(grad, unit, scale):
    return scale * (
        grad
        - jnp.mean(grad, -1, keepdims=True)
        - unit * jnp.mean(grad * unit, -1, keepdims=True)
    )


def gelu_with_slope(value):
    below = 0.5 + 0.5 * lax.erf(value * 0.7071067811865476)
    bell = jnp.exp2(value * (value * -0.7213475204444817))
    return value * below, below + value * (0.3989422804014327 * bell)


def columns(array, low=0, high=None):
    width = array.shape[1] - low if high is None else high - low
    spec = pl.BlockSpec(
        (array.shape[0], width), lambda i: (0, low // width), pipeline_mode=pl.Buffered(1)
    )
    return array, spec


def transposed(array):
    rows, width = array.shape
    return pl.pallas_call(
        lambda x_ref, out_ref: out_ref.__setitem__(Ellipsis, x_ref[...].T),
        grid=(width // 128,),
        in_specs=[pl.BlockSpec((rows, 128), lambda i: (0, i))],
        out_specs=pl.BlockSpec((128, rows), lambda i: (i, 0)),
        out_shape=jax.ShapeDtypeStruct((width, rows), array.dtype),
    )(array)


def row_call(kernel, rows, first, count, inputs, weights, outputs, sums=(), into=None, flops=0):
    done = 0 if into is None else len(inputs) + len(weights)

    def run(*refs):
        given, results = refs[: len(inputs) + len(weights)], refs[-len(outputs) - len(sums) :]
        if sums:

            @pl.when(pl.program_id(0) == 0)
            def _():
                for place in range(len(sums)):
                    place -= len(sums)
                    start = refs[place - len(outputs) - len(sums)] if done else None
                    here = results[place]
                    here[...] = start[...] if done else jnp.zeros_like(here)

        kernel(*given, *results)

    moved = rows * count * sum(a.shape[1] * a.dtype.itemsize for a, _ in inputs)
    moved += sum(w.size * w.dtype.itemsize for w, _ in weights)
    moved += rows * count * sum(w * jnp.dtype(t).itemsize for w, t in outputs)

    def rows_at(width, begin):
        return pl.BlockSpec((rows, width), lambda i: (begin + i, 0))

    sum_specs = [pl.BlockSpec((16, w), lambda i: (0, 0)) for w in sums]
    in_specs = [rows_at(a.shape[1], begin) for a, begin in inputs]
    in_specs += [spec for _, spec in weights]
    arguments = [a for a, _ in inputs] + [w for w, _ in weights]
    if into is not None:
        in_specs += [pl.BlockSpec(memory_space=pl.ANY)] * len(outputs) + sum_specs
        arguments += list(into)
    return pl.pallas_call(
        run,
        grid=(count,),
        in_specs=in_specs,
        out_specs=[rows_at(w, first) for w, _ in outputs] + sum_specs,
        out_shape=[jax.ShapeDtypeStruct((TOKENS, w), t) for w, t in outputs]
        + [jax.ShapeDtypeStruct((16, w), F32) for w in sums],
        input_output_aliases={done + i: i for i in range(len(outputs) + len(sums))} if done else {},
        compiler_params=pltpu.CompilerParams(vmem_limit_bytes=56 << 20),
        cost_estimate=pl.CostEstimate(
            flops=flops * rows * count, transcendentals=0, bytes_accessed=moved
        ),
    )(*arguments)


def row_parts(ref):
    return [slice(at, at + 128) for at in range(0, ref.shape[0], 128)]


def widen_kernel(x_ref, att_ref, out_w, up_w, vec, resid_ref, low_ref, act_ref, slope_ref):
    lows = []
    for part in row_parts(x_ref):
        resid = x_ref[part, :].astype(F32) + dot(att_ref[part, :], out_w[...]) + vec[2:3]
        resid_ref[part, :] = resid
        lows.append((standard(resid)[0] * vec[3:4] + vec[4:5]).astype(LOW))
        low_ref[part, :] = lows[-1]
    for row in range(4):
        cols = slice(row * D, row * D + D)
        for part, low in zip(row_parts(x_ref), lows):
            value, slope = gelu_with_slope(dot(low, up_w[:, cols]) + vec[5 + row : 6 + row])
            act_ref[part, cols] = value.astype(LOW)
            slope_ref[part, cols] = slope.astype(LOW)


def narrow_kernel(act_ref, resid_ref, down_w, proj_w, vec, two_ref, low_ref, proj_ref, unit_ref):
    branches = [dot(act_ref[part, :], down_w[...]) for part in row_parts(act_ref)]
    for part, branch in zip(row_parts(act_ref), branches):
        normed = standard(resid_ref[part, :])[0] * vec[3:4] + vec[4:5]
        two = normed + branch + vec[9:10]
        two_ref[part, :] = two
        low = (standard(two)[0] * vec[10:11] + vec[11:12]).astype(LOW)
        low_ref[part, :] = low
        projected = dot(low, proj_w[...])
        proj_ref[part, :] = projected
        square = jnp.sum(projected * projected, -1, keepdims=True) + 1e-06
        unit_ref[part, :] = (projected * lax.rsqrt(square)).astype(LOW)


def back_kernel(
    grad_ref, proj_ref, two_ref, slope_ref, resid_ref,
    proj_w, down_w, up_w, out_w, vec,
    gproj_ref, gtwo_ref, ghid_ref, gone_ref, gatt_ref, sum_ref,
):
    def add(row, value):
        sum_ref[row : row + 1, :] += jnp.sum(value, 0, keepdims=True)

    grad, projected = grad_ref[...], proj_ref[...]
    scale = lax.rsqrt(jnp.sum(projected * projected, -1, keepdims=True) + 1e-06)
    along = jnp.sum(projected * grad, -1, keepdims=True)
    gproj = (scale * grad - projected * (scale * scale * scale * along)).astype(LOW)
    gproj_ref[...] = gproj
    gnormed = dot(gproj, proj_w[...], ACROSS)
    unit, scale = standard(two_ref[...])
    add(10, gnormed * unit)
    add(11, gnormed)
    gtwo = standard_backward(gnormed * vec[10:11], unit, scale)
    add(9, gtwo)
    gtwo_low = gtwo.astype(LOW)
    gtwo_ref[...] = gtwo_low
    gnormed = gtwo
    for row in range(4):
        part = slice(row * D, row * D + D)
        ghid = dot(gtwo_low, down_w[part, :], ACROSS) * slope_ref[:, part].astype(F32)
        add(5 + row, ghid)
        ghid_low = ghid.astype(LOW)
        ghid_ref[:, part] = ghid_low
        gnormed = gnormed + dot(ghid_low, up_w[:, part], ACROSS)
    unit, scale = standard(resid_ref[...])
    add(3, gnormed * unit)
    add(4, gnormed)
    gone = standard_backward(gnormed * vec[3:4], unit, scale)
    add(2, gone)
    gone_low = gone.astype(LOW)
    gone_ref[...] = gone_low
    gatt_ref[...] = dot(gone_low, out_w[...], ACROSS).astype(LOW)


def attend_kernel(
    tile, lengths, spans, q_ref, k_ref, v_ref, col, row, out_ref, total_ref, logits, probs, flipped
):
    flipped[...] = v_ref[...].T
    lane = lax.broadcasted_iota(jnp.int32, (tile, 128), 1)

    def block(index, carry):
        here = pl.ds(pl.multiple_of(index * tile, tile), tile)
        low, kind = spans[index, 0], spans[index, 1]

        def attend(length):
            there = pl.ds(pl.multiple_of(low, 128), length)
            query = q_ref[here, :] * jnp.asarray(0.125, LOW)
            same = col[there, :] == row[0:1, here]
            tops = []
            for head in range(2):
                own = jnp.where((lane < 64) == (head == 0), query, jnp.zeros_like(query))
                value = jnp.where(same, dot(k_ref[there, :], own, ACROSS), -1e30)
                logits[head, 0:length, :] = value
                top = jnp.max(value.reshape(-1, 8, tile), 0)
                tops.append(jnp.max(top, 0, keepdims=True))
            sums = []
            for head in range(2):
                term = jnp.exp(logits[head, 0:length, :] - tops[head])
                sums.append(jnp.sum(term.reshape(-1, 8, tile), 0))
                probs[head, 0:length, :] = term.astype(LOW)
            parts = []
            for head in range(2):
                total = jnp.sum(sums[head], 0, keepdims=True)
                values = flipped[64 * head : 64 * head + 64, there]
                parts.append(dot(values, probs[head, 0:length, :]) / total)
                total_ref[0, head : head + 1, here] = tops[head] + jnp.log(total)
            out_ref[here, :] = jnp.concatenate(parts, 0).T.astype(LOW)

        for number, length in enumerate(lengths):
            pl.when(kind == number)(functools.partial(attend, length))
        return carry

    lax.fori_loop(0, q_ref.shape[0] // tile, block, 0)


def head_pair(count, row, first):
    return pl.BlockSpec((count, 128), lambda h, s: (row, first + h))


def attend_lengths(count):
    return [length for length in (128, 256, 384, 512, 640, 768, 1024) if count < 256 or length > 128][
        : 1 if count < 256 else None
    ]


def attend_call(kernel, tile, count, pairs, tables, arrays, specs, outputs, into, scratch, cost):
    spans, col, row = tables
    specs = specs + [
        pl.BlockSpec((count, tile), lambda h, s: (0, 0)),
        pl.BlockSpec((8, count), lambda h, s: (0, 0)),
    ]
    arguments = [spans, *arrays, col, row]
    aliases = {}
    used = len(arguments)
    if into is not None:
        aliases = {used + i: i for i in range(len(into))}
        specs = specs + [pl.BlockSpec(memory_space=pl.ANY)] * len(into)
        arguments += list(into)

    def run(*refs):
        kernel(tile, attend_lengths(count), *refs[:used], *refs[len(arguments) :])

    return pl.pallas_call(
        run,
        out_shape=[shape for shape, _ in outputs],
        grid_spec=pltpu.PrefetchScalarGridSpec(
            num_scalar_prefetch=1,
            grid=(pairs,),
            in_specs=specs,
            out_specs=[spec for _, spec in outputs],
            scratch_shapes=scratch,
        ),
        input_output_aliases=aliases,
        compiler_params=pltpu.CompilerParams(vmem_limit_bytes=48 << 20),
        cost_estimate=pl.CostEstimate(
            flops=cost * pairs * count * count * 128,
            transcendentals=0,
            bytes_accessed=8 * pairs * count * 128,
        ),
    )(*arguments)


def attend_forward(mixed, tables, tile, first, pairs, row, into=None):
    count = mixed.shape[0]
    return attend_call(
        attend_kernel,
        tile,
        count,
        pairs,
        tables,
        [mixed] * 3,
        [head_pair(count, 0, third * 6 + first) for third in range(3)],
        [
            (jax.ShapeDtypeStruct((TOKENS, D), LOW), head_pair(count, row, first)),
            (
                jax.ShapeDtypeStruct((6, 8, count), F32),
                pl.BlockSpec((1, 8, count), lambda h, s: (first + h, 0, 0)),
            ),
        ],
        into,
        [
            pltpu.VMEM((2, count, tile), F32),
            pltpu.VMEM((2, count, tile), LOW),
            pltpu.VMEM((128, count), LOW),
        ],
        40,
    )


def attend_back_kernel(
    tile, lengths, spans, q_ref, k_ref, v_ref, g_ref, total_ref, col, row,
    grad_ref, sum_ref, flipped, gkey, gvalue, probs, gprobs, low_probs, low_deltas,
):
    flipped[...] = k_ref[...].T
    gkey[...] = jnp.zeros_like(gkey)
    gvalue[...] = jnp.zeros_like(gvalue)
    sum_ref[...] = jnp.zeros_like(sum_ref)
    lane = lax.broadcasted_iota(jnp.int32, (tile, 128), 1)

    def block(index, carry):
        here = pl.ds(pl.multiple_of(index * tile, tile), tile)
        low, kind = spans[index, 0], spans[index, 1]

        def attend(length):
            there = pl.ds(pl.multiple_of(low, 128), length)
            query, grad = q_ref[here, :] * jnp.asarray(0.125, LOW), g_ref[here, :]
            zero = jnp.zeros_like(query)
            same = col[there, :] == row[0:1, here]
            own = [(lane < 64) == (head == 0) for head in range(2)]
            queries = [jnp.where(mine, query, zero) for mine in own]
            grads = [jnp.where(mine, grad, zero) for mine in own]
            dots = []
            for head in range(2):
                prob = dot(k_ref[there, :], queries[head], ACROSS)
                prob = jnp.exp(prob - total_ref[0, head : head + 1, here])
                prob = jnp.where(same, prob, 0.0)
                gprob = dot(v_ref[there, :], grads[head], ACROSS)
                total = jnp.sum((prob * gprob).reshape(-1, 8, tile), 0)
                dots.append(jnp.sum(total, 0, keepdims=True))
                probs[head, 0:length, :] = prob
                gprobs[head, 0:length, :] = gprob
                low_probs[head, 0:length, :] = prob.astype(LOW)

            def both(terms, right):
                return dot(terms[0, 0:length, :], right[0]) + dot(terms[1, 0:length, :], right[1])

            gvalue[there, :] += both(low_probs, grads)
            for head in range(2):
                delta = gprobs[head, 0:length, :] - dots[head]
                low_deltas[head, 0:length, :] = (probs[head, 0:length, :] * delta).astype(LOW)
            gkey[there, :] += both(low_deltas, queries)
            parts = []
            for head in range(2):
                keys = flipped[64 * head : 64 * head + 64, there]
                parts.append(dot(keys, low_deltas[head, 0:length, :]))
            whole = jnp.concatenate(parts, 0).T * 0.125
            grad_ref[0, here, :] = whole.astype(LOW)
            sum_ref[0:1, :] += jnp.sum(whole, 0, keepdims=True)

        for number, length in enumerate(lengths):
            pl.when(kind == number)(functools.partial(attend, length))
        return carry

    lax.fori_loop(0, q_ref.shape[0] // tile, block, 0)
    grad_ref[1] = gkey[...].astype(LOW)
    grad_ref[2] = gvalue[...].astype(LOW)
    sum_ref[1:2, :] = jnp.sum(gvalue[...], 0, keepdims=True)


def attend_backward(mixed, grad, total, tables, tile, first, pairs, row, into=None):
    count = mixed.shape[0]
    return attend_call(
        attend_back_kernel,
        tile,
        count,
        pairs,
        tables,
        [mixed] * 3 + [grad, total],
        [head_pair(count, 0, third * 6 + first) for third in range(3)]
        + [
            head_pair(count, row, first),
            pl.BlockSpec((1, 8, count), lambda h, s: (first + h, 0, 0)),
        ],
        [
            (
                jax.ShapeDtypeStruct((3, TOKENS, D), LOW),
                pl.BlockSpec((3, count, 128), lambda h, s: (0, row, first + h)),
            ),
            (
                jax.ShapeDtypeStruct((16, D), F32),
                pl.BlockSpec((16, 128), lambda h, s: (0, first + h)),
            ),
        ],
        into,
        [
            pltpu.VMEM((128, count), LOW),
            pltpu.VMEM((count, 128), F32),
            pltpu.VMEM((count, 128), F32),
            pltpu.VMEM((2, count, tile), F32),
            pltpu.VMEM((2, count, tile), F32),
            pltpu.VMEM((2, count, tile), LOW),
            pltpu.VMEM((2, count, tile), LOW),
        ],
        80,
    )


def segment_tables(segment, tile):
    count = segment.shape[0]
    lengths = jnp.asarray(attend_lengths(count), jnp.int32)
    ends = segment.reshape(count // tile, tile)
    first = jnp.sum((segment[None, :] < ends[:, :1]).astype(jnp.int32), 1) // 128 * 128
    last = jnp.sum((segment[None, :] <= ends[:, -1:]).astype(jnp.int32), 1)
    kind = jnp.sum((lengths[None, :] < (last - first)[:, None]).astype(jnp.int32), 1)
    chosen = jnp.arange(lengths.shape[0], dtype=jnp.int32)[None, :] == kind[:, None]
    keys = jnp.sum(jnp.where(chosen, lengths[None, :], 0), 1)
    return (
        jnp.stack([jnp.minimum(first, count - keys), kind], 1),
        jnp.broadcast_to(segment[:, None], (count, tile)),
        jnp.broadcast_to(segment[None, :], (8, count)),
    )


def two_terms(value):
    high = value.astype(LOW)
    return high, (value - high.astype(F32)).astype(LOW)


def sharp(cosine):
    return jnp.exp2(cosine * 14.426950408889634 - 14.426950408889634)


def score_kernel(query_ref, passage_ref, member_ref, score_ref, sums_ref, terms_ref):
    terms = sharp(dot(query_ref[...], passage_ref[...], ACROSS)).astype(LOW)
    terms_ref[...] = terms
    sums = dot(terms, member_ref[...])
    sums_ref[...] = sums
    lane = lax.broadcasted_iota(jnp.int32, sums.shape, 1)
    soft = jnp.where(lane < PPB, 0.1 * jnp.log(jnp.where(lane < PPB, sums, 1.0)) + 1.0, 0.0)
    score_ref[...] = jnp.sum(soft.reshape(-1, QLEN, 128), 1)


def score_ratio(grad_ref, sums_ref):
    rows = sums_ref.shape[0]
    lane = lax.broadcasted_iota(jnp.int32, (rows, 128), 1)
    grads = jnp.broadcast_to(grad_ref[...][:, None, :], (rows // QLEN, QLEN, 128))
    ratio = grads.reshape(rows, 128) / jnp.where(lane % 64 < PPB, sums_ref[...], 1.0)
    high, rest = two_terms(ratio)
    return jnp.where(lane < 64, high, rest)


def score_query_kernel(terms_ref, passage_ref, member_ref, grad_ref, sums_ref, out_ref):
    spread = dot(score_ratio(grad_ref, sums_ref), member_ref[...], ACROSS)
    terms = (terms_ref[...].astype(F32) * spread).astype(LOW)
    out_ref[...] = dot(terms, passage_ref[...])


def score_passage_kernel(query_ref, passage_ref, member_ref, grad_ref, sums_ref, out_ref):
    @pl.when(pl.program_id(0) == 0)
    def _():
        out_ref[...] = jnp.zeros_like(out_ref)

    ratio = score_ratio(grad_ref, sums_ref)
    terms = sharp(dot(passage_ref[...], query_ref[...], ACROSS))
    terms = (terms * dot(member_ref[...], ratio, ACROSS)).astype(LOW)
    out_ref[...] += dot(terms, query_ref[...])


SCORE_ROWS = 1024


def score_call(kernel, inputs, in_specs, out_specs, out_shape, flops):
    return pl.pallas_call(
        kernel,
        grid=(inputs[0].shape[0] // SCORE_ROWS,),
        in_specs=in_specs,
        out_specs=out_specs,
        out_shape=out_shape,
        compiler_params=pltpu.CompilerParams(vmem_limit_bytes=40 << 20),
        cost_estimate=pl.CostEstimate(
            flops=flops,
            transcendentals=inputs[0].shape[0] * BIN,
            bytes_accessed=inputs[0].shape[0] * 1024,
        ),
    )(*inputs)


def score_specs():
    rows = SCORE_ROWS
    fixed = pl.BlockSpec((BIN, 128), lambda i: (0, 0))
    return (
        pl.BlockSpec((rows, 128), lambda i: (i, 0)),
        fixed,
        pl.BlockSpec((rows // QLEN, 128), lambda i: (i, 0)),
    )


def score_forward(queries, passages, member):
    rows, fixed, grads = score_specs()
    count = queries.shape[0]
    return score_call(
        score_kernel,
        (queries, passages, member),
        [rows, fixed, fixed],
        [grads, rows, pl.BlockSpec((SCORE_ROWS, BIN), lambda i: (i, 0))],
        [
            jax.ShapeDtypeStruct((count // QLEN, 128), F32),
            jax.ShapeDtypeStruct((count, 128), F32),
            jax.ShapeDtypeStruct((count, BIN), LOW),
        ],
        6 * count * BIN * 128,
    )


def score_backward(kernel, queries, passages, member, grad_scores, sums):
    rows, fixed, grads = score_specs()
    count = queries.shape[0]
    inputs = (queries, passages, member, grad_scores, sums)
    left = pl.BlockSpec((SCORE_ROWS, queries.shape[1]), lambda i: (i, 0))
    in_specs = [left, fixed, fixed, grads, rows]
    width, spec = (BIN, fixed) if kernel is score_passage_kernel else (count, rows)
    out = jax.ShapeDtypeStruct((width, 128), F32)
    return score_call(kernel, inputs, in_specs, spec, out, 6 * count * BIN * 128)


def finish_kernel(scalars, *refs):
    own, moved, sums, (first_ref, vector_ref, square_ref) = refs[:4], refs[4:7], refs[7:-3], refs[-3:]
    rows = first_ref.shape[0]
    here = pl.ds(pl.multiple_of(scalars[0] * rows, rows), rows)
    square = jnp.zeros((1, 1), F32)
    at = 0
    for ref in own:
        part = slice(at, at + ref.shape[1])
        total = ref[here, :]
        for more in moved:
            total = total + more[:, part].astype(F32)
        if at < 3 * D:
            first_ref[:, part] = total
        else:
            vector_ref[...] = total
        square = square + jnp.sum(total * total, keepdims=True)
        at += ref.shape[1]
    for ref in sums:
        square = square + jnp.sum(ref[...] * ref[...], keepdims=True)
    square_ref[...] = jnp.broadcast_to(square, square_ref.shape)


def finish(arrays, sums):
    kinds = (False,) * 4
    if not staged_mesh():
        *thirds, vector = scatter_rest(arrays)
        square = sum(jnp.sum(a * a) for a in (*thirds, vector, *sums))
        return jnp.concatenate(thirds, 1), vector, jnp.full((1, 128), square)
    rows = arrays[0].shape[0] // 4
    inputs = [*arrays, *last_moves(depth_blocks(arrays), kinds), *sums]
    shapes = [(rows, 3 * D), (rows, 128), (1, 128)]
    return pl.pallas_call(
        finish_kernel,
        grid_spec=pltpu.PrefetchScalarGridSpec(
            num_scalar_prefetch=1,
            grid=(1,),
            in_specs=[pl.BlockSpec(a.shape, lambda i, s: (0, 0)) for a in inputs],
            out_specs=[pl.BlockSpec(shape, lambda i, s: (0, 0)) for shape in shapes],
        ),
        out_shape=[jax.ShapeDtypeStruct(shape, F32) for shape in shapes],
        compiler_params=pltpu.CompilerParams(vmem_limit_bytes=32 << 20),
    )(scalars_of_position(), *inputs)


def cross_grad(scores, partition, passage_ids, chosen_ids, query_total):
    onehot = (passage_ids[None, :] == chosen_ids[:, None]).astype(jnp.float32)
    return (jnp.exp(scores) / partition[:, None] - onehot) / query_total


def adam_kernel(square_ref, *refs):
    count = 6
    given, (norm_ref, *results) = refs[: 4 * count], refs[4 * count :]
    norm = jnp.sqrt(jnp.sum(square_ref[...], 0, keepdims=True)[:, 0:1])
    norm_ref[...] = jnp.broadcast_to(norm, norm_ref.shape)
    factor = jnp.minimum(1.0, clip_max / (norm + 1e-06))
    for number in range(count):
        weight, first, second, gradient = (r[...] for r in given[4 * number : 4 * number + 4])
        rate = vector_rate if number == count - 1 else learn_rate
        clipped = gradient * factor
        new_first = beta_one * first + (1.0 - beta_one) * clipped
        new_second = beta_two * second + (1.0 - beta_two) * clipped * clipped
        spread = jnp.sqrt(new_second / (1.0 - beta_two**STEP)) + adam_eps
        direction = new_first / (1.0 - beta_one**STEP) / spread
        results[3 * number][...] = weight - rate * (direction + decay_rate * weight)
        results[3 * number + 1][...] = new_first
        results[3 * number + 2][...] = new_second


def adam_updates(squares, groups):
    inputs = [squares] + [array for group in groups for array in group]
    shapes = [(1, 128)] + [group[0].shape for group in groups for _ in range(3)]
    return pl.pallas_call(
        adam_kernel,
        grid=(1,),
        in_specs=[pl.BlockSpec(a.shape, lambda i: (0, 0)) for a in inputs],
        out_specs=[pl.BlockSpec(shape, lambda i: (0, 0)) for shape in shapes],
        out_shape=[jax.ShapeDtypeStruct(shape, F32) for shape in shapes],
        compiler_params=pltpu.CompilerParams(vmem_limit_bytes=58 << 20),
    )(*inputs)


def body(
    query_tokens,
    passage_tokens,
    passage_lengths,
    positives,
    qkv_weight,
    qkv_first,
    qkv_second,
    out_weight,
    out_first,
    out_second,
    up_weight,
    up_first,
    up_second,
    down_weight,
    down_first,
    down_second,
    proj_weight,
    proj_first,
    proj_second,
    vector_params,
    vector_first,
    vector_second,
):
    vector_part = jnp.pad(vector_params.T, ((0, 0), (0, 116))).astype(LOW)
    first_part = jnp.concatenate([qkv_weight.astype(LOW), vector_part], 1)
    middle_part = jnp.concatenate([up_weight, out_weight, proj_weight], 1).astype(LOW)
    down_part = down_weight.astype(LOW)
    first_line = line_of(first_part, send_line(first_part))
    middle_moved = send_line(gate(middle_part, first_line))
    first_pair = gather_pair(first_line)
    own_index = lax.axis_index(("pb", "pa"))
    query_total = QPD * lax.axis_size(("pb", "pa"))
    query_flat = query_tokens.reshape(QUERY_ROWS, D)
    lengths, passages = gate((passage_lengths, passage_tokens[0]), first_pair)
    tokens = jnp.concatenate([passages, query_flat], 0)
    query_seg = np.arange(QUERY_ROWS, dtype=np.int32) // QLEN
    query_tables = (
        jnp.zeros((1, 2), jnp.int32),
        jnp.asarray(np.broadcast_to(query_seg[:, None], (QUERY_ROWS, QUERY_ROWS))),
        jnp.asarray(np.broadcast_to(query_seg[None, :], (8, QUERY_ROWS))),
    )
    own_lengths = lax.dynamic_index_in_dim(lengths, own_index, 0, keepdims=False)
    upto = np.tril(np.ones((PPB, PPB), np.int32))
    ends = jnp.sum(jnp.where(upto > 0, own_lengths[None, :], 0), 1)
    places = jnp.arange(BIN, dtype=jnp.int32)
    own_seg = jnp.sum((places[:, None] >= ends[None, :]).astype(jnp.int32), 1)
    passage_tables = segment_tables(own_seg, ATTEND_TILE)
    member = (own_seg[:, None] == jnp.arange(128, dtype=jnp.int32)[None, :] % 64).astype(LOW)
    ready = tokens, passage_tables, member
    first_quad = gather_quad(first_pair, ready)
    middle_line = line_of(middle_part, gate(middle_moved, first_quad))
    middle = gather_rest(middle_line)
    down_moved = send_line(gate(down_part, middle_line))
    qkv_matrix, vectors = gather_whole(first_quad, [(0, 2304), (2304, 2432)])
    vectors = vectors[:, :12].T.astype(F32)
    bias_qkv = jnp.concatenate([vectors[0], jnp.zeros_like(vectors[0]), vectors[1]])

    def mix(rows):
        return (dot(rows, qkv_matrix) + bias_qkv).astype(LOW)

    query_mixed = mix(query_flat)
    passage_mixed = mix(gate(passage_tokens[0], query_mixed))
    down_line = line_of(down_part, gate(down_moved, passage_mixed))
    attended, query_log = attend_forward(
        gate(query_mixed, down_line), query_tables, QUERY_ROWS, 0, 6, BIN // QUERY_ROWS
    )
    passage_state = attend_forward(
        gate(passage_mixed, down_line), passage_tables, ATTEND_TILE, 0, 3, 0, (attended,)
    )
    down_pair = gather_pair(down_line, passage_state)
    attended, passage_log = attend_forward(
        gate(passage_mixed, down_pair), passage_tables, ATTEND_TILE, 3, 3, 0, passage_state
    )
    down_quad = gather_quad(down_pair, attended)
    up = columns(middle, 0, 4 * D)
    out = columns(middle, 4 * D, 5 * D)
    proj = columns(middle, 5 * D, 5 * D + 128)
    vector_rows = columns(vectors)

    def widen(rows, first, count, att, into):
        return row_call(
            widen_kernel,
            rows,
            first,
            count,
            [(tokens, first), (att, first)],
            (out, up, vector_rows),
            [(D, F32), (D, LOW), (4 * D, LOW), (4 * D, LOW)],
            into=into,
            flops=10 * D * D,
        )

    def narrow(rows, first, count, wider, into):
        return row_call(
            narrow_kernel,
            rows,
            first,
            count,
            [(wider[2], first), (wider[0], first)],
            (down, proj, vector_rows),
            [(D, F32), (D, LOW), (128, F32), (128, LOW)],
            into=into,
            flops=8 * D * D,
        )

    wider = widen(QUERY_ROWS, BIN // QUERY_ROWS, 1, gate(attended, down_quad), None)
    (down_matrix,) = gather_whole(down_quad, [(0, D)], wider)
    down = columns(down_matrix)
    narrower = narrow(QUERY_ROWS, BIN // QUERY_ROWS, 1, wider, None)
    query_part = narrower[3][BIN:]
    query_line = line_of(query_part, send_line(query_part))
    every_query = gather_rest(query_line)
    wider = widen(
        FEED_ROWS, 0, BIN // FEED_ROWS, gate(attended, query_line), gate(wider, narrower)
    )
    narrower = narrow(FEED_ROWS, 0, BIN // FEED_ROWS, wider, narrower)
    resid, normed, active, slope = wider
    two, normed_out, projected, unit = narrower
    passage_unit = unit

    passage_ids = own_index * PPB + jnp.arange(PPB, dtype=jnp.int32)
    scores, totals, score_terms = score_forward(every_query, passage_unit, member)
    scores = scores[:, :PPB]
    turned = transposed(gate(tokens, scores))
    partition = gate(jnp.sum(everywhere(jnp.sum(jnp.exp(scores), 1)), 0), turned)
    grad_scores = cross_grad(scores, partition, passage_ids, positives, query_total)
    grad_scores = jnp.tile(jnp.pad(grad_scores, ((0, 0), (0, 64 - PPB))), (1, 2))
    grad_every = score_backward(
        score_query_kernel, score_terms, passage_unit, member, grad_scores, totals
    )
    whole, rounded = (None,), (False,)
    query_back = scatter_quad([grad_every], scatter_sends([grad_every], whole))
    grad_passage = score_backward(
        score_passage_kernel,
        gate(every_query, query_back),
        passage_unit,
        member,
        grad_scores,
        totals,
    )

    def go_back(rows, first, count, grad, into):
        return row_call(
            back_kernel,
            rows,
            first,
            count,
            [grad, (projected, first), (two, first), (slope, first), (resid, first)],
            (proj, down, up, out, vector_rows),
            [(128, LOW), (D, LOW), (4 * D, LOW), (D, LOW), (D, LOW)],
            (D,),
            into=into,
            flops=18 * D * D,
        )

    query_back = scatter_pair(query_back, pair_send(query_back, whole), whole)
    back = go_back(
        BACK_ROWS, 0, BIN // BACK_ROWS, (gate(grad_passage, query_back), 0), None
    )
    query_back = scatter_line(query_back, whole)
    (grad_query,) = scatter_total(gate(query_back, back), whole)
    back = go_back(QUERY_ROWS, BIN // QUERY_ROWS, 1, (grad_query, 0), back)
    gproj, gtwo, ghid, gone, gatt, sums = back

    def terms(left, right):
        return dot(left, right, (((0,), (0,)), ((), ()))).astype(LOW)

    def attend_back(first, pairs, into, *others):
        mixed = gate(passage_mixed, *others)
        return attend_backward(
            mixed, gatt, passage_log, passage_tables, ATTEND_TILE, first, pairs, 0, into
        )

    down_terms = terms(active, gtwo)
    down_sends = scatter_sends([down_terms], rounded)
    up_terms = terms(normed, gate(ghid, down_sends))
    down_back = scatter_quad([down_terms], down_sends, up_terms)
    down_send = pair_send(down_back, rounded)
    down_pair = scatter_pair(down_back, down_send, rounded)
    rest = gate((gone, gproj), down_send)
    out_terms, proj_terms = terms(attended, rest[0]), dot(rest[1], normed_out, (((0,), (0,)), ((), ()))).T
    kinds = (False, False, True)
    middle_terms = [up_terms, out_terms, proj_terms]
    middle_sends = scatter_sends(middle_terms, kinds)
    query_grads = attend_backward(
        gate(query_mixed, middle_sends),
        gatt,
        query_log,
        query_tables,
        QUERY_ROWS,
        0,
        6,
        BIN // QUERY_ROWS,
    )
    middle_back = scatter_quad(middle_terms, middle_sends, query_grads)
    middle_send = pair_send(middle_back, kinds)
    middle_pair = scatter_pair(middle_back, middle_send, kinds)
    down_line = scatter_line(down_pair, rounded)
    grads = attend_back(0, 2, query_grads[:1], query_grads, down_pair, middle_send)
    (down_sum,) = scatter_total(gate(down_line, grads), rounded)
    grads = attend_back(2, 2, grads, down_line)
    middle_line = scatter_line(gate(middle_pair, grads), kinds)
    grads = attend_back(4, 2, grads, middle_pair, down_sum)
    up_sum, out_sum, proj_sum = scatter_total(middle_line, kinds)
    mixed_grads = gate(grads[0], middle_line)
    first_terms = [dot(turned, mixed_grads[third]).astype(LOW) for third in range(3)]
    mixed_sums = grads[1] + query_grads[1]
    vector_grad = jnp.concatenate([mixed_sums[:2], sums[2:12]], 0)
    vector_terms = jnp.pad(vector_grad.T, ((0, 0), (0, 116)))
    kinds = (False,) * 4
    first_terms.append(vector_terms)
    first_back = scatter_quad(first_terms, scatter_sends(first_terms, kinds))
    first_back = scatter_pair(first_back, pair_send(first_back, kinds), kinds, up_sum, down_sum)
    qkv_sum, vector_sum, square = finish(
        scatter_line(first_back, kinds), (out_sum, up_sum, down_sum, proj_sum)
    )
    groups = (
        (qkv_weight, qkv_first, qkv_second, qkv_sum),
        (out_weight, out_first, out_second, out_sum),
        (up_weight, up_first, up_second, up_sum),
        (down_weight, down_first, down_second, down_sum),
        (proj_weight, proj_first, proj_second, proj_sum),
        (vector_params, vector_first, vector_second, vector_sum[:, :12].T),
    )
    norm, *results = adam_updates(everywhere(square)[:, 0], groups)
    return (norm[0, 0], *results)


def solution(mesh):
    placed = (
        P(("pb", "pa"), None, None),
        P(("pb", "pa"), None, None),
        P(),
        P(),
        P(("pb", "pa"), None),
        P(("pb", "pa"), None),
        P(("pb", "pa"), None),
        P(("pb", "pa"), None),
        P(("pb", "pa"), None),
        P(("pb", "pa"), None),
        P(("pb", "pa"), None),
        P(("pb", "pa"), None),
        P(("pb", "pa"), None),
        P(("pb", "pa"), None),
        P(("pb", "pa"), None),
        P(("pb", "pa"), None),
        P(("pb", "pa"), None),
        P(("pb", "pa"), None),
        P(("pb", "pa"), None),
        P(None, ("pb", "pa")),
        P(None, ("pb", "pa")),
        P(None, ("pb", "pa")),
    )
    return jax.shard_map(
        body,
        mesh=mesh,
        in_specs=placed,
        out_specs=(
            P(),
            P(("pb", "pa"), None),
            P(("pb", "pa"), None),
            P(("pb", "pa"), None),
            P(("pb", "pa"), None),
            P(("pb", "pa"), None),
            P(("pb", "pa"), None),
            P(("pb", "pa"), None),
            P(("pb", "pa"), None),
            P(("pb", "pa"), None),
            P(("pb", "pa"), None),
            P(("pb", "pa"), None),
            P(("pb", "pa"), None),
            P(("pb", "pa"), None),
            P(("pb", "pa"), None),
            P(("pb", "pa"), None),
            P(None, ("pb", "pa")),
            P(None, ("pb", "pa")),
            P(None, ("pb", "pa")),
        ),
        check_vma=False,
    )
```
